32 devices in a mesh: depth: 8 (over y, x, core), mode: 4 (over z).
Axes of the slice: x: 2, y: 2, z: 4, core: 2. Of those that a mesh axis runs over, the one named last changes fastest.
Arguments:
- blocks: float32 [128, 2, 128, 128], P(('depth', 'mode')), may hold values from -6 to 6
- live_slots: int32 [128], P(('depth', 'mode')), may hold values from 0 to 1, as said below
- parent_index: int32 [128], P(('depth', 'mode')), may hold values from 0 to 15, as said below
- bath_mode: int32 [128], P(('depth', 'mode')), may hold values from 0 to 7, as said below
- hamiltonian: float32 [128, 128], replicated, may hold values from -0.5 to 0.5
- coupling: float32 [8, 128, 128], P('mode'), may hold values from -0.5 to 0.5
- correlation: float32 [8, 2], P('mode'), may hold values from -1 to 1
- damping: float32 [128], P(('depth', 'mode')), may hold values from 0.01 to 0.1
- link_weight: float32 [128], P(('depth', 'mode')), may hold values from 0.5 to 2
Outputs:
- evolved: float32 [128, 2, 128, 128], P(('depth', 'mode'))
The draws below stay inside these ranges and needn't reach their ends.
Inputs may be any that keep to these rules, and one draw needn't show every extreme that they name: `live_slots`: on each device the live slots come first and slot 0 is live; every slot of the deepest depth is live in every draw. `parent_index`: for a block of depth d >= 1, m * 4 + s names a live block of depth d - 1, held on index m of mode in slot s; 0 at depth 0. `bath_mode`: A block held on index m of mode links through a bath mode from m * 2 to m * 2 + 1.
All inputs are finite; a program needn't handle non-finite values.
Results may differ from the reference program's by a relative error of at most 0.0001.
Values sent between devices are 32-bit elements; how exact they have to be, the bound alone decides.
No kernel may reach another device: no remote copies, remote signals or barrier semaphores. Data moves between devices by JAX's collectives and lax.ppermute only.
A program may use at most 64 MiB of HBM per device.

```python
import math
import jax
import jax.numpy as jnp
from jax import lax

STATES = 128
BLOCKS_DEV = 4
MODES_DEV = 2
SUBSTEPS = 2
HALF_STEPS = 4
LEVELS = 8
MODE_GROUP = 4
BATH_MODES = 8
LEVEL_BLOCKS = 16
ALL_BLOCKS = 128


def slot_counts(key):
    level_ids = jnp.arange(LEVELS, dtype=jnp.int32)[:, None]
    random_part = jax.random.randint(jax.random.fold_in(key, 11), (LEVELS, MODE_GROUP), 0, LEVELS)
    counts = 1 + (BLOCKS_DEV - 1) * (level_ids + random_part) // (LEVELS - 1)
    counts = jnp.minimum(counts, BLOCKS_DEV)
    return jnp.where(level_ids == LEVELS - 1, BLOCKS_DEV, counts).astype(jnp.int32)


def draw_live_slots(key, part):
    counts = slot_counts(key)
    slot_ids = jnp.arange(BLOCKS_DEV, dtype=jnp.int32)
    alive_mask = slot_ids[None, None, :] < counts[:, :, None]
    return alive_mask.astype(jnp.int32).reshape(ALL_BLOCKS)


def draw_parent_index(key, part):
    counts = slot_counts(key)
    owners = jax.random.randint(jax.random.fold_in(key, 23), (LEVELS, MODE_GROUP, BLOCKS_DEV), 0, MODE_GROUP)
    raw_bits = jax.random.randint(jax.random.fold_in(key, 29), (LEVELS, MODE_GROUP, BLOCKS_DEV), 0, 1048576)
    previous = jnp.concatenate([counts[:1], counts[:-1]], axis=0)
    matches = owners[..., None] == jnp.arange(MODE_GROUP, dtype=jnp.int32)[None, None, None, :]
    available = jnp.sum(jnp.where(matches, previous[:, None, None, :], 0), axis=-1)
    slot_pick = raw_bits % available
    parents = owners * BLOCKS_DEV + slot_pick
    level_ids = jnp.arange(LEVELS, dtype=jnp.int32)[:, None, None]
    parents = jnp.where(level_ids == 0, 0, parents)
    return parents.astype(jnp.int32).reshape(ALL_BLOCKS)


def draw_bath_mode(key, part):
    group_ids = jnp.arange(MODE_GROUP, dtype=jnp.int32)[None, :, None] * MODES_DEV
    offsets = jax.random.randint(key, (LEVELS, MODE_GROUP, BLOCKS_DEV), 0, MODES_DEV)
    return (group_ids + offsets).astype(jnp.int32).reshape(ALL_BLOCKS)


def block_levels(rng, dims, pieces, smallest, largest):
    level, own = 1.0, jax.random.fold_in(rng, 6)
    for axis_at, parts in pieces:
        draws = jnp.exp(jax.random.uniform(jax.random.fold_in(own, axis_at), (parts,), jnp.float32, smallest / len(pieces), largest / len(pieces)))
        level = level * jnp.repeat(draws, dims[axis_at] // parts).reshape([-1 if axis == axis_at else 1 for axis in range(len(dims))])
    return level


def scatter_about(own_key, dims, deviation, limit, shards=(), kind=jnp.bfloat16):
    loudness = block_levels(own_key, dims, shards, -0.22, 0.18) if shards else 1.0
    result = jax.random.normal(own_key, dims, jnp.float32) * deviation * loudness
    return jnp.minimum(jnp.maximum(result, -limit), limit).astype(kind)


def setup_inputs(seed: int = 0) -> dict:
    splits = jax.random.split(jax.random.key(seed), 10)
    blocks = scatter_about(splits[0], (ALL_BLOCKS, 2, STATES, STATES), 1.0, 6.0, ((0, 32),), jnp.float32)
    live_slots = draw_live_slots(jax.random.fold_in(splits[9], 71), 0)
    parent_index = draw_parent_index(jax.random.fold_in(splits[9], 71), 0)
    bath_mode = draw_bath_mode(jax.random.fold_in(splits[9], 71), 0)
    hamiltonian = scatter_about(splits[4], (STATES, STATES), STATES ** -0.5, 0.5, (), jnp.float32)
    coupling = scatter_about(splits[5], (BATH_MODES, STATES, STATES), STATES ** -0.5, 0.5, ((0, 4),), jnp.float32)
    correlation = jnp.clip(jax.random.uniform(splits[6], (BATH_MODES, 2), jnp.float32, -1.0, 1.0) * block_levels(splits[6], (BATH_MODES, 2), ((0, 4),), -0.4, 0.0), -1.0, 1.0)
    damping = jnp.clip(jnp.exp(math.log(0.1) - 2.3025851 * jax.random.uniform(splits[7], (ALL_BLOCKS,), jnp.float32) ** block_levels(splits[7], (ALL_BLOCKS,), ((0, 32),), -0.2, 0.2)), 0.01, 0.1)
    link_weight = jnp.clip(jnp.exp(math.log(2.0) - 1.3862944 * jax.random.uniform(splits[8], (ALL_BLOCKS,), jnp.float32) ** block_levels(splits[8], (ALL_BLOCKS,), ((0, 32),), -0.2, 0.2)), 0.5, 2.0)
    return {"blocks": blocks, "live_slots": live_slots, "parent_index": parent_index, "bath_mode": bath_mode, "hamiltonian": hamiltonian, "coupling": coupling, "correlation": correlation, "damping": damping, "link_weight": link_weight}


top_level_index = lax.Precision.HIGHEST
substep = 0.7
couple_step = 0.2


def product(first_factor, second_factor):
    return jnp.matmul(first_factor, second_factor, precision=top_level_index)


def liouville(states, sym_energy):
    bracket = product(sym_energy, states) - product(states, sym_energy)
    return jnp.stack([bracket[:, 1], -bracket[:, 0]], axis=1)


def evolve(states, sym_energy, decay_factor):
    def one_step(turn_index, current):
        series = current
        for power in (4.0, 3.0, 2.0, 1.0):
            series = current + (substep / power) * liouville(series, sym_energy)
        return series

    states = lax.fori_loop(0, SUBSTEPS, one_step, states)
    return states * decay_factor[:, None, None, None]


def child_terms(states, sym_coupling, weights):
    bracket = product(sym_coupling[:, None], states) - product(states, sym_coupling[:, None])
    return weights[:, None, None, None] * jnp.stack([bracket[:, 1], -bracket[:, 0]], axis=1)


def parent_terms(parents, sym_coupling, bath_coeff, weights):
    left_product = product(sym_coupling[:, None], parents)
    right_product = product(parents, sym_coupling[:, None])
    differ = left_product - right_product
    summed = left_product + right_product
    bath_real = bath_coeff[:, 0][:, None, None]
    bath_imag = bath_coeff[:, 1][:, None, None]
    real_part = bath_real * differ[:, 1] + bath_imag * summed[:, 0]
    imaginary = -bath_real * differ[:, 0] + bath_imag * summed[:, 1]
    return weights[:, None, None, None] * jnp.stack([real_part, imaginary], axis=1)


def reference(blocks, live_slots, parent_index, bath_mode, hamiltonian, coupling, correlation, damping, link_weight):
    sym_energy = (hamiltonian + hamiltonian.T) * 0.5
    sym_all = (coupling + jnp.swapaxes(coupling, 1, 2)) * 0.5
    sym_coupling = sym_all[bath_mode]
    bath_coeff = correlation[bath_mode]
    alive_mask = live_slots.astype(jnp.float32)[:, None, None, None]
    decay_factor = jnp.exp(-damping * (SUBSTEPS * substep))
    depth_ids = jnp.arange(ALL_BLOCKS, dtype=jnp.int32) // LEVEL_BLOCKS
    slot_ids = jnp.arange(LEVEL_BLOCKS, dtype=jnp.int32)
    select_entries = (parent_index.reshape(LEVELS, LEVEL_BLOCKS)[:, :, None] == slot_ids[None, None, :]).astype(jnp.float32)
    states = blocks * alive_mask
    zero_level = jnp.zeros((1, LEVEL_BLOCKS, 2, STATES, STATES), jnp.float32)
    for half_step in range(HALF_STEPS):
        active = (depth_ids % 2 == half_step % 2).astype(jnp.float32)[:, None, None, None]
        child_portion_term = (child_terms(states, sym_coupling, link_weight) * alive_mask).reshape(LEVELS, LEVEL_BLOCKS, 2, STATES, STATES)
        collected_rows = jnp.einsum('pnc,pnatf->pcatf', select_entries[1:], child_portion_term[1:], precision=top_level_index)
        child_sum = jnp.concatenate([collected_rows, zero_level], axis=0).reshape(blocks.shape)
        grouped_by_level = states.reshape(LEVELS, LEVEL_BLOCKS, 2, STATES, STATES)
        selected_rows = jnp.einsum('cqg,cgfew->cqfew', select_entries[1:], grouped_by_level[:-1], precision=top_level_index)
        parents = jnp.concatenate([zero_level, selected_rows], axis=0).reshape(blocks.shape)
        couple = child_sum + parent_terms(parents, sym_coupling, bath_coeff, link_weight)
        states = alive_mask * (evolve(states, sym_energy, decay_factor) + couple_step * active * couple)
    return states
```

```python
import math
import jax
import jax.numpy as jnp
from jax import lax
from jax.experimental import pallas as pl
from jax.experimental.pallas import tpu as pltpu
from jax.sharding import PartitionSpec as P

SUBSTEPS = 2
HALF_STEPS = 4
ORDER = 4
substep = 0.7
couple_step = 0.2

AXES = ("depth", "mode")
VMEM = pltpu.VMEM
SMEM = pltpu.SMEM
bf16 = jnp.bfloat16
f32 = jnp.float32


def split(value):
    high = value.astype(bf16)
    return high, (value - high.astype(f32)).astype(bf16)


def stack_rows(value):
    high, low = split(value)
    return jnp.concatenate([high, high, low], axis=0)


def stack_cols(value):
    high, low = split(value)
    return jnp.concatenate([high, low, high], axis=1)


def dot(first, second):
    return jnp.dot(first, second, preferred_element_type=f32)


def exact(first, second):
    return jnp.dot(first, second, preferred_element_type=f32, precision=lax.Precision.HIGHEST)


def powers_kernel(ham_ref, right_ref, left_ref):
    n = ham_ref.shape[0]
    ham = (ham_ref[...] + ham_ref[...].T) * 0.5
    power = ham
    for k in range(1, ORDER + 1):
        if k > 1:
            power = exact(power, ham)
        scaled = power * (substep**k / math.factorial(k))
        right_ref[:, (k - 1) * n : k * n] = stack_rows(scaled)
        left_ref[:, (k - 1) * 3 * n : k * 3 * n] = stack_cols(scaled)


def coupling_kernel(coupling_ref, right_ref, left_ref):
    for k in range(coupling_ref.shape[0]):
        sym = (coupling_ref[k] + coupling_ref[k].T) * 0.5
        right_ref[k] = stack_rows(sym)
        left_ref[k] = stack_cols(sym)


def taylor(real, imag, right, left):
    n = real.shape[0]
    out = dot(stack_cols(jnp.concatenate([real, imag], axis=0)), right)
    rp = [out[:n, k * n : (k + 1) * n] for k in range(ORDER)]
    ip = [out[n:, k * n : (k + 1) * n] for k in range(ORDER)]
    u_real, u_imag = real, imag
    stacked = [None] * ORDER
    for k in range(ORDER + 1):
        if k:
            turn = k % 4
            if turn == 1:
                u_real, u_imag = u_real - ip[k - 1], u_imag + rp[k - 1]
            elif turn == 2:
                u_real, u_imag = u_real - rp[k - 1], u_imag - ip[k - 1]
            elif turn == 3:
                u_real, u_imag = u_real + ip[k - 1], u_imag - rp[k - 1]
            else:
                u_real, u_imag = u_real + rp[k - 1], u_imag + ip[k - 1]
        j = ORDER - k
        if j:
            turn = j % 4
            if turn == 1:
                pair = (u_imag, -u_real)
            elif turn == 2:
                pair = (-u_real, -u_imag)
            elif turn == 3:
                pair = (-u_imag, u_real)
            else:
                pair = (u_real, u_imag)
            stacked[j - 1] = stack_rows(jnp.concatenate(pair, axis=1))
    done = dot(left, jnp.concatenate(stacked, axis=0))
    return u_real + done[:, :n], u_imag + done[:, n:]


def free_kernel(factor_ref, states_ref, right_ref, left_ref, out_ref):
    right, left = right_ref[...], left_ref[...]

    @pl.loop(0, states_ref.shape[0])
    def _(b):
        real, imag = states_ref[b, 0], states_ref[b, 1]
        for _ in range(SUBSTEPS):
            real, imag = taylor(real, imag, right, left)
        factor = factor_ref[b]
        out_ref[b, 0] = real * factor
        out_ref[b, 1] = imag * factor


def sided(real, imag, right, left):
    n = real.shape[0]
    after = dot(stack_cols(jnp.concatenate([real, imag], axis=0)), right)
    before = dot(left, stack_rows(jnp.concatenate([real, imag], axis=1)))
    return after[:n], after[n:], before[:, :n], before[:, n:]


def send_kernel(sends, target_ref, mode_ref, weight_ref, parent_ref, flag_ref, right_ref, left_ref, *refs):
    groups, (sum_ref, pick_ref) = refs[:-2], refs[-2:]
    slots = groups[0].shape[0]

    @pl.when(flag_ref[0] > 0)
    def _():
        sum_ref[...] = jnp.zeros_like(sum_ref)
        for k, group in enumerate(groups):

            @pl.loop(0, slots)
            def _(s):
                c = k * slots + s
                target = target_ref[c]

                @pl.when(target >= 0)
                def _():
                    mode = mode_ref[c]
                    weight = weight_ref[c]
                    ra, ia, rb, ib = sided(group[s, 0], group[s, 1], right_ref[mode], left_ref[mode])
                    sum_ref[target, 0] = sum_ref[target, 0] + weight * (ib - ia)
                    sum_ref[target, 1] = sum_ref[target, 1] + weight * (ra - rb)

                parent = parent_ref[s] - k * slots

                @pl.when(jnp.logical_and(parent >= 0, parent < slots))
                def _():
                    pick_ref[s] = group[parent]


def join_kernel(flag_ref, live_ref, mode_ref, weight_ref, coeff_a_ref, coeff_c_ref, free_ref, sum_ref, pick_ref, right_ref, left_ref, out_ref):
    slots = free_ref.shape[0]

    @pl.when(flag_ref[0] > 0)
    def _():
        @pl.loop(0, slots)
        def _(s):
            mode = mode_ref[s]
            ra, ia, rb, ib = sided(pick_ref[s, 0], pick_ref[s, 1], right_ref[mode], left_ref[mode])
            wa = weight_ref[s] * coeff_a_ref[s]
            wc = weight_ref[s] * coeff_c_ref[s]
            live = live_ref[s]
            real = sum_ref[s, 0] + (wa * (ib - ia) + wc * (rb + ra))
            imag = sum_ref[s, 1] + (wa * (ra - rb) + wc * (ib + ia))
            out_ref[s, 0] = live * (free_ref[s, 0] + couple_step * real)
            out_ref[s, 1] = live * (free_ref[s, 1] + couple_step * imag)

    @pl.when(flag_ref[0] == 0)
    def _():
        @pl.loop(0, slots)
        def _(s):
            out_ref[s] = live_ref[s] * free_ref[s]


def call(kernel, out_shapes, smem_count, args, flops=0):
    specs = [pl.BlockSpec(memory_space=SMEM)] * smem_count
    specs += [pl.BlockSpec(memory_space=VMEM)] * (len(args) - smem_count)
    return pl.pallas_call(
        kernel,
        out_shape=out_shapes,
        in_specs=specs,
        out_specs=jax.tree.map(lambda _: pl.BlockSpec(memory_space=VMEM), out_shapes),
        cost_estimate=pl.CostEstimate(flops=flops, bytes_accessed=1 << 20, transcendentals=0),
    )(*args)


def shards(sizes, blocks, live_slots, parent_index, bath_mode, hamiltonian, coupling, correlation, damping, link_weight):
    depths, group = sizes
    slots, _, n, _ = blocks.shape
    modes = coupling.shape[0]
    depth = lax.axis_index("depth")
    here = lax.axis_index("mode")

    def place(d, m):
        return d * group + m

    def turn(value, k, parity=None):
        pairs = [
            (place(d, m), place(d, (m + k) % group))
            for d in range(depths)
            for m in range(group)
            if parity is None or d % 2 == parity
        ]
        return lax.ppermute(value, AXES, pairs)

    def shift(value, step, parity=None):
        pairs = [
            (place(d, m), place(d + step, m))
            for d in range(depths)
            for m in range(group)
            if 0 <= d + step < depths and (parity is None or d % 2 == parity)
        ]
        return lax.ppermute(value, AXES, pairs)

    first = [blocks] + [turn(blocks, k, 1) for k in range(1, group)]

    live = live_slots.astype(f32)
    local_mode = bath_mode - here * modes
    packed = jnp.stack([parent_index.astype(f32), local_mode.astype(f32), link_weight * live])
    level = [packed] + [turn(packed, k) for k in range(1, group)]
    below = shift(packed, -1)

    sds = jax.ShapeDtypeStruct
    ham_right, ham_left = call(
        powers_kernel, (sds((3 * n, ORDER * n), bf16), sds((n, 3 * ORDER * n), bf16)), 0, (hamiltonian,)
    )
    operators = [coupling] + [turn(coupling, k) for k in range(1, group)]
    all_right, all_left = call(
        lambda *refs: [
            coupling_kernel(refs[k], refs[-2].at[pl.ds(k * modes, modes)], refs[-1].at[pl.ds(k * modes, modes)])
            for k in range(group)
        ]
        and None,
        (sds((group * modes, 3 * n, n), bf16), sds((group * modes, n, 3 * n), bf16)),
        0,
        operators,
    )
    own_right, own_left = call(
        coupling_kernel, (sds((modes, 3 * n, n), bf16), sds((modes, n, 3 * n), bf16)), 0, (coupling,)
    )

    table = jnp.concatenate(level, axis=1)
    child_parent = table[0].astype(jnp.int32)
    target = jnp.where(child_parent // slots == here, child_parent % slots, -1)
    back = jnp.repeat(jnp.arange(group, dtype=jnp.int32), slots)
    child_mode = table[1].astype(jnp.int32) + back * modes
    child_weight = table[2]
    next_parent = below[0].astype(jnp.int32)
    picked = ((here - next_parent // slots) % group) * slots + next_parent % slots

    own_select = (local_mode[:, None] == jnp.arange(modes, dtype=jnp.int32)[None, :]).astype(f32)
    coeff = jnp.sum(own_select[:, :, None] * correlation[None], axis=1)
    factor = jnp.exp(-damping * (SUBSTEPS * substep))

    state_shape = sds(blocks.shape, f32)
    states = blocks
    for half_step in range(HALF_STEPS):
        receiving = (depth % 2 == half_step % 2).astype(jnp.int32).reshape(1)
        sender = 1 - half_step % 2
        gathered = first if half_step == 0 else [states] + [turn(states, k, sender) for k in range(1, group)]
        free = call(free_kernel, state_shape, 1, (factor, states, ham_right, ham_left), flops=1 << 30)
        sums, picks = call(
            lambda *refs: send_kernel(None, *refs),
            (state_shape, state_shape),
            5,
            (target, child_mode, child_weight, picked, 1 - receiving, all_right, all_left, *gathered),
            flops=1 << 28,
        )
        sums = shift(sums, -1, sender)
        picks = shift(picks, 1, sender)
        states = call(
            join_kernel,
            state_shape,
            6,
            (receiving, live, local_mode, link_weight, coeff[:, 0], coeff[:, 1], free, sums, picks, own_right, own_left),
            flops=1 << 27,
        )
    return states


def solution(mesh):
    sizes = (mesh.shape["depth"], mesh.shape["mode"])
    return jax.shard_map(
        lambda *args: shards(sizes, *args),
        mesh=mesh,
        in_specs=(
            P(("depth", "mode"), None, None, None),
            P(("depth", "mode")),
            P(("depth", "mode")),
            P(("depth", "mode")),
            P(),
            P("mode", None, None),
            P("mode", None),
            P(("depth", "mode")),
            P(("depth", "mode")),
        ),
        out_specs=P(("depth", "mode"), None, None, None),
        check_vma=False,
    )
```

```python
import functools
import math
import jax
import jax.numpy as jnp
from jax import lax
from jax.experimental import pallas as pl
from jax.experimental.pallas import tpu as pltpu
from jax.sharding import PartitionSpec as P

SUBSTEPS = 2
HALF_STEPS = 4
ORDER = 4
substep = 0.7
couple_step = 0.2

AXES = ("depth", "mode")
VMEM = pltpu.VMEM
SMEM = pltpu.SMEM
bf16 = jnp.bfloat16
f32 = jnp.float32


def split(value):
    high = value.astype(bf16)
    return high, (value - high.astype(f32)).astype(bf16)


def stack_rows(value):
    high, low = split(value)
    return jnp.concatenate([high, high, low], axis=0)


def stack_cols(value):
    high, low = split(value)
    return jnp.concatenate([high, low, high], axis=1)


def dot(first, second):
    return jnp.dot(first, second, preferred_element_type=f32)


def exact(first, second):
    return jnp.dot(first, second, preferred_element_type=f32, precision=lax.Precision.HIGHEST)


def powers_kernel(ham_ref, right_ref, left_ref):
    n = ham_ref.shape[0]
    ham = (ham_ref[...] + ham_ref[...].T) * 0.5
    power = ham
    for k in range(1, ORDER + 1):
        if k > 1:
            power = exact(power, ham)
        scaled = power * (substep**k / math.factorial(k))
        right_ref[:, (k - 1) * n : k * n] = stack_rows(scaled)
        left_ref[:, (k - 1) * 3 * n : k * 3 * n] = stack_cols(scaled)


def coupling_kernel(group, modes, ints_ref, *refs):
    right_ref, left_ref = refs[-2:]
    own, turned, passed = refs[0], refs[1:group], refs[group : 2 * group - 1]
    odd = ints_ref[0] > 0
    for k in range(group):
        for i in range(modes):
            value = own[i] if k == 0 else jnp.where(odd, turned[k - 1][i], passed[k - 1][i])
            sym = (value + value.T) * 0.5
            right_ref[k * modes + i] = stack_rows(sym)
            left_ref[k * modes + i] = stack_cols(sym)


def taylor(real, imag, right, left):
    n = real.shape[0]
    out = dot(stack_cols(jnp.concatenate([real, imag], axis=0)), right)
    rp = [out[:n, k * n : (k + 1) * n] for k in range(ORDER)]
    ip = [out[n:, k * n : (k + 1) * n] for k in range(ORDER)]
    u_real, u_imag = real, imag
    stacked = [None] * ORDER
    for k in range(ORDER + 1):
        if k:
            turn = k % 4
            if turn == 1:
                u_real, u_imag = u_real - ip[k - 1], u_imag + rp[k - 1]
            elif turn == 2:
                u_real, u_imag = u_real - rp[k - 1], u_imag - ip[k - 1]
            elif turn == 3:
                u_real, u_imag = u_real + ip[k - 1], u_imag - rp[k - 1]
            else:
                u_real, u_imag = u_real + rp[k - 1], u_imag + ip[k - 1]
        j = ORDER - k
        if j:
            turn = j % 4
            if turn == 1:
                pair = (u_imag, -u_real)
            elif turn == 2:
                pair = (-u_real, -u_imag)
            elif turn == 3:
                pair = (-u_imag, u_real)
            else:
                pair = (u_real, u_imag)
            stacked[j - 1] = stack_rows(jnp.concatenate(pair, axis=1))
    done = dot(left, jnp.concatenate(stacked, axis=0))
    return u_real + done[:, :n], u_imag + done[:, n:]


def free_kernel(skip_parity, base, ints_ref, floats_ref, *refs):
    right_ref, left_ref, out_ref = refs[-3:]
    sources = refs[:-3]
    slots = out_ref.shape[0]
    parity = ints_ref[0]

    pair = 2 if slots % 2 == 0 else 1

    def body():
        right, left = right_ref[...], left_ref[...]

        @pl.loop(0, slots // pair)
        def _(step):
            states = []
            for u in range(pair):
                s = step * pair + u
                real, imag = sources[0][s, 0], sources[0][s, 1]
                if len(sources) > 1:
                    odd = parity > 0
                    real = jnp.where(odd, sources[1][s, 0], real)
                    imag = jnp.where(odd, sources[1][s, 1], imag)
                states.append((real, imag))
            for _ in range(SUBSTEPS):
                states = [taylor(real, imag, right, left) for real, imag in states]
            for u in range(pair):
                s = step * pair + u
                factor = floats_ref[base + s]
                out_ref[s, 0] = states[u][0] * factor
                out_ref[s, 1] = states[u][1] * factor

    if skip_parity is None:
        body()
    else:
        pl.when(parity != skip_parity)(body)


def sided(real, imag, right, left):
    n = real.shape[0]
    after = dot(stack_cols(jnp.concatenate([real, imag], axis=0)), right)
    before = dot(left, stack_rows(jnp.concatenate([real, imag], axis=1)))
    return after[:n], after[n:], before[:, :n], before[:, n:]


def fetch(groups, index, stage_ref, u):
    slots = groups[0].shape[0]
    for k, group in enumerate(groups):
        local = index - k * slots

        @pl.when(jnp.logical_and(local >= 0, local < slots))
        def _():
            stage_ref[u] = group[local]


def child_pair(stage, mode, weight, right_ref, left_ref):
    ra, ia, rb, ib = sided(stage[0], stage[1], right_ref[mode], left_ref[mode])
    return weight * (ib - ia), weight * (ra - rb)


def parent_pair(stage, mode, wa, wc, right_ref, left_ref):
    ra, ia, rb, ib = sided(stage[0], stage[1], right_ref[mode], left_ref[mode])
    return wa * (ib - ia) + wc * (rb + ra), wa * (ra - rb) + wc * (ib + ia)


def send_kernel(sender, spots, ints_ref, floats_ref, right_ref, left_ref, *refs):
    groups = refs[: -4]
    sum_ref, pick_ref, stage_ref, list_ref = refs[-4:]
    slots = groups[0].shape[0]
    total = slots * len(groups)

    @pl.when(ints_ref[0] == sender)
    def _():
        sum_ref[...] = jnp.zeros_like(sum_ref)
        for s in range(slots):
            fetch(groups, ints_ref[spots["below_parent"] + s], pick_ref, s)

        def collect(c, count):
            mine = ints_ref[spots["own_target"] + c] >= 0

            @pl.when(mine)
            def _():
                list_ref[count] = c

            return count + mine.astype(jnp.int32)

        count = lax.fori_loop(0, total, collect, jnp.int32(0))

        @pl.loop(0, (count + slots - 1) // slots)
        def _(batch):
            children = []
            for u in range(slots):
                place = batch * slots + u
                c = list_ref[jnp.minimum(place, count - 1)]
                fetch(groups, c, stage_ref, u)
                weight = jnp.where(place < count, floats_ref[spots["own_weight"] + c], 0.0)
                children.append((c, weight))
            terms = [
                child_pair(stage_ref[u], ints_ref[spots["own_mode"] + c], weight, right_ref, left_ref)
                for u, (c, weight) in enumerate(children)
            ]
            for (c, _), (real, imag) in zip(children, terms):
                target = ints_ref[spots["own_target"] + c]
                sum_ref[target, 0] = sum_ref[target, 0] + real
                sum_ref[target, 1] = sum_ref[target, 1] + imag


def join_kernel(receiver, spots, ints_ref, floats_ref, right_ref, left_ref, free_ref, sum_ref, pick_ref, out_ref):
    slots = free_ref.shape[0]

    @pl.when(ints_ref[0] == receiver)
    def _():
        terms = [
            parent_pair(
                pick_ref[s],
                ints_ref[spots["own_mode"] + s],
                floats_ref[spots["own_a"] + s],
                floats_ref[spots["own_c"] + s],
                right_ref,
                left_ref,
            )
            for s in range(slots)
        ]
        for s in range(slots):
            scale = floats_ref[spots["own_scale"] + s]
            out_ref[s, 0] = free_ref[s, 0] + scale * (sum_ref[s, 0] + terms[s][0])
            out_ref[s, 1] = free_ref[s, 1] + scale * (sum_ref[s, 1] + terms[s][1])

    @pl.when(ints_ref[0] != receiver)
    def _():
        out_ref[...] = free_ref[...]


def load_base(bases, acc_ref):
    slots = bases[0].shape[0]
    for k, base in enumerate(bases):
        acc_ref[pl.ds(k * slots, slots)] = base[...]


def store_outs(acc_ref, outs):
    slots = outs[0].shape[0]
    for k, out in enumerate(outs):
        out[...] = acc_ref[pl.ds(k * slots, slots)]


def children_kernel(receiver, spots, base_count, group_count, ints_ref, floats_ref, right_ref, left_ref, *refs):
    bases, groups = refs[:base_count], refs[base_count : base_count + group_count]
    outs, stage_ref = refs[base_count + group_count : -2], refs[-2]
    acc_ref = refs[-1] if len(outs) > 1 else outs[0]
    slots = groups[0].shape[0]
    load_base(bases, acc_ref)

    @pl.when(ints_ref[0] == receiver)
    def _():
        @pl.loop(0, group_count)
        def _(k):
            at = k * slots
            for j, group in enumerate(groups):

                @pl.when(k == j)
                def _():
                    stage_ref[...] = group[...]

            terms = []
            for s in range(slots):
                target = ints_ref[spots["below_parent"] + at + s]
                weight = floats_ref[spots["below_weight"] + at + s] * floats_ref[spots["own_scale"] + target]
                mode = ints_ref[spots["below_mode"] + at + s]
                terms.append((target, child_pair(stage_ref[s], mode, weight, right_ref, left_ref)))
            for target, (real, imag) in terms:
                acc_ref[target, 0] = acc_ref[target, 0] + real
                acc_ref[target, 1] = acc_ref[target, 1] + imag

    if len(outs) > 1:
        store_outs(acc_ref, outs)


def parents_kernel(receiver, spots, base_count, group_count, ints_ref, floats_ref, right_ref, left_ref, *refs):
    bases, groups = refs[:base_count], refs[base_count : base_count + group_count]
    outs, stage_ref = refs[base_count + group_count : -2], refs[-2]
    acc_ref = refs[-1] if len(outs) > 1 else outs[0]
    slots = groups[0].shape[0]
    load_base(bases, acc_ref)

    @pl.when(ints_ref[0] == receiver)
    def _():
        @pl.loop(0, group_count)
        def _(k):
            at = k * slots
            for s in range(slots):
                fetch(groups, ints_ref[spots["own_parent"] + at + s], stage_ref, s)
            terms = [
                parent_pair(
                    stage_ref[s],
                    ints_ref[spots["own_mode"] + at + s],
                    floats_ref[spots["own_a"] + at + s],
                    floats_ref[spots["own_c"] + at + s],
                    right_ref,
                    left_ref,
                )
                for s in range(slots)
            ]
            for s in range(slots):
                scale = floats_ref[spots["own_scale"] + at + s]
                acc_ref[at + s, 0] = acc_ref[at + s, 0] + scale * terms[s][0]
                acc_ref[at + s, 1] = acc_ref[at + s, 1] + scale * terms[s][1]

    if len(outs) > 1:
        store_outs(acc_ref, outs)


def call(kernel, out_shapes, limit, args, smem=2, us=1.0, scratch=()):
    specs = [pl.BlockSpec(memory_space=SMEM)] * smem
    specs += [pl.BlockSpec(memory_space=VMEM)] * (len(args) - smem)
    return pl.pallas_call(
        kernel,
        out_shape=out_shapes,
        in_specs=specs,
        out_specs=jax.tree.map(lambda _: pl.BlockSpec(memory_space=VMEM), out_shapes),
        scratch_shapes=scratch,
        compiler_params=pltpu.CompilerParams(vmem_limit_bytes=limit),
        cost_estimate=pl.CostEstimate(flops=int(us * 1.1e9), bytes_accessed=1 << 19, transcendentals=0),
    )(*args)


def shards(sizes, blocks, live_slots, parent_index, bath_mode, hamiltonian, coupling, correlation, damping, link_weight):
    depths, group = sizes
    slots, _, n, _ = blocks.shape
    modes = coupling.shape[0]
    depth = lax.axis_index("depth")
    here = lax.axis_index("mode")
    limit = 8 * group * slots * 2 * n * n * 4

    def place(d, m):
        return d * group + m

    def turn(value, k, parity=None):
        pairs = [
            (place(d, m), place(d, (m + k) % group))
            for d in range(depths)
            for m in range(group)
            if parity is None or d % 2 == parity
        ]
        return lax.ppermute(value, AXES, pairs)

    def shift(value, step, parity=None):
        pairs = [
            (place(d, m), place(d + step, m))
            for d in range(depths)
            for m in range(group)
            if 0 <= d + step < depths and (parity is None or d % 2 == parity)
        ]
        return lax.ppermute(value, AXES, pairs)

    first = [blocks] + [turn(blocks, k, 1) for k in range(1, group)]

    parity = (depth % 2).astype(jnp.int32)
    live = live_slots.astype(f32)
    local_mode = bath_mode - here * modes
    own_select = (local_mode[:, None] == jnp.arange(modes, dtype=jnp.int32)[None, :]).astype(f32)
    coeff = jnp.sum(own_select[:, :, None] * correlation[None], axis=1)
    packed = jnp.stack(
        [parent_index.astype(f32), local_mode.astype(f32), link_weight, live, damping, coeff[:, 0], coeff[:, 1]]
    )
    own = jnp.concatenate([packed] + [turn(packed, k) for k in range(1, group)], axis=1)
    below = shift(own, -1)
    back = jnp.repeat(jnp.arange(group, dtype=jnp.int32), slots) * modes

    def relative(parent):
        parent = parent.astype(jnp.int32)
        return ((here - parent // slots) % group) * slots + parent % slots

    own_parent = relative(own[0])
    ints, floats, spots = [jnp.full((8,), parity)], [], {}

    def put(parts, name, value):
        spots[name] = sum(part.shape[0] for part in parts)
        parts.append(value)

    put(ints, "own_parent", own_parent)
    put(ints, "own_target", jnp.where(own_parent < slots, own_parent, -1))
    put(ints, "own_mode", own[1].astype(jnp.int32) + back)
    put(ints, "below_parent", relative(below[0]))
    put(ints, "below_mode", below[1].astype(jnp.int32) + back)
    put(floats, "own_factor", own[3] * jnp.exp(-own[4] * (SUBSTEPS * substep)))
    put(floats, "own_weight", own[2] * own[3])
    put(floats, "own_scale", own[3] * couple_step)
    put(floats, "own_a", own[2] * own[5])
    put(floats, "own_c", own[2] * own[6])
    put(floats, "below_weight", below[2] * below[3])
    ints, floats = jnp.concatenate(ints), jnp.concatenate(floats)

    sds = jax.ShapeDtypeStruct
    one, whole = sds(blocks.shape, f32), sds((group * slots, 2, n, n), f32)
    stage, big = VMEM((slots, 2, n, n), f32), VMEM(whole.shape, f32)

    powers = call(
        powers_kernel, (sds((3 * n, ORDER * n), bf16), sds((n, 3 * ORDER * n), bf16)), limit, (hamiltonian,), smem=0, us=2
    )
    turned = [turn(coupling, k, 1) for k in range(1, group)]
    passed = [shift(value, -1, 1) for value in turned]
    operators = call(
        functools.partial(coupling_kernel, group, modes),
        (sds((group * modes, 3 * n, n), bf16), sds((group * modes, n, 3 * n), bf16)),
        limit,
        (ints[:8], coupling, *turned, *passed),
        smem=1,
        us=2,
    )

    def free(sources, k, skip=None):
        return call(
            functools.partial(free_kernel, skip, spots["own_factor"] + k * slots),
            one,
            limit,
            (ints, floats, *sources, *powers),
            us=5,
        )

    def send(groups, sender):
        return call(
            functools.partial(send_kernel, sender, spots),
            (one, one),
            limit,
            (ints, floats, *operators, *groups),
            us=2,
            scratch=[stage, SMEM((group * slots,), jnp.int32)],
        )

    def join(freed, sums, picks, receiver):
        return call(
            functools.partial(join_kernel, receiver, spots),
            one,
            limit,
            (ints, floats, *operators, freed, sums, picks),
            us=1,
        )

    def children(bases, groups, receiver, parts):
        return call(
            functools.partial(children_kernel, receiver, spots, len(bases), len(groups)),
            [one] * group if parts else [whole],
            limit,
            (ints, floats, *operators, *bases, *groups),
            us=4,
            scratch=[stage, big] if parts else [stage, VMEM((8, n), f32)],
        )

    def parents(bases, groups, receiver, parts):
        return call(
            functools.partial(parents_kernel, receiver, spots, len(bases), len(groups)),
            [one] * group if parts else [whole],
            limit,
            (ints, floats, *operators, *bases, *groups),
            us=4,
            scratch=[stage, big] if parts else [stage, VMEM((8, n), f32)],
        )

    ranks = range(group)
    sums, picks = send(first, 1)
    sums, picks = shift(sums, -1, 1), shift(picks, 1, 1)
    freed = [free([first[k]], k, skip=None if k == 0 else 0) for k in ranks]
    own_state = join(freed[0], sums, picks, 0)

    gathered = [own_state] + [turn(own_state, k, 0) for k in range(1, group)]
    from_above = [shift(value, 1, 0) for value in gathered]
    from_below = [shift(value, -1, 0) for value in gathered]
    freed = [free([gathered[k], freed[k]] if k else [gathered[k]], k) for k in ranks]
    states = children(parents(freed, from_above, 1, False), from_below, 1, True)

    from_below = [shift(value, -1, 1) for value in states]
    from_above = [shift(value, 1, 1) for value in states]
    freed = [free([states[k]], k, skip=None if k == 0 else 1) for k in ranks]
    states = parents(children(freed, from_below, 0, False), from_above, 0, True)

    sums, picks = send(states, 0)
    sums, picks = shift(sums, -1, 0), shift(picks, 1, 0)
    return join(free([states[0]], 0), sums, picks, 1)


def solution(mesh):
    sizes = (mesh.shape["depth"], mesh.shape["mode"])
    return jax.shard_map(
        lambda *args: shards(sizes, *args),
        mesh=mesh,
        in_specs=(
            P(("depth", "mode"), None, None, None),
            P(("depth", "mode")),
            P(("depth", "mode")),
            P(("depth", "mode")),
            P(),
            P("mode", None, None),
            P("mode", None),
            P(("depth", "mode")),
            P(("depth", "mode")),
        ),
        out_specs=P(("depth", "mode"), None, None, None),
        check_vma=False,
    )
```

```python
import functools
import math
import jax
import jax.numpy as jnp
from jax import lax
from jax.experimental import pallas as pl
from jax.experimental.pallas import tpu as pltpu
from jax.sharding import PartitionSpec as P

SUBSTEPS = 2
ORDER = 4
substep = 0.7
couple_step = 0.2

AXES = ("depth", "mode")
VMEM = pltpu.VMEM
SMEM = pltpu.SMEM
bf16 = jnp.bfloat16
f32 = jnp.float32


def split(value):
    high = value.astype(bf16)
    return high, (value - high.astype(f32)).astype(bf16)


def stack_rows(value):
    high, low = split(value)
    return jnp.concatenate([high, high, low], axis=0)


def stack_cols(value):
    high, low = split(value)
    return jnp.concatenate([high, low, high], axis=1)


def dot(first, second):
    return jnp.dot(first, second, preferred_element_type=f32)


def exact(first, second):
    return jnp.dot(first, second, preferred_element_type=f32, precision=lax.Precision.HIGHEST)


def powers_kernel(ham_ref, right_ref, left_ref):
    n = ham_ref.shape[0]
    ham = (ham_ref[...] + ham_ref[...].T) * 0.5
    power = ham
    for k in range(1, ORDER + 1):
        if k > 1:
            power = exact(power, ham)
        scaled = power * (substep**k / math.factorial(k))
        right_ref[:, (k - 1) * n : k * n] = stack_rows(scaled)
        left_ref[:, (k - 1) * 3 * n : k * 3 * n] = stack_cols(scaled)


def coupling_kernel(group, modes, ints_ref, *refs):
    right_ref, left_ref = refs[-2:]
    own, turned, passed = refs[0], refs[1:group], refs[group:-2]
    n = own.shape[-1]
    odd = ints_ref[0] > 0
    for k in range(group):
        for i in range(modes):
            if k == 0:
                value = own[i]
            else:
                value = turned[k - 1][i, :n]
                if passed:
                    value = jnp.where(odd, value, passed[k - 1][i, :n])
            sym = (value + value.T) * 0.5
            right_ref[k * modes + i] = stack_rows(sym)
            left_ref[k * modes + i] = stack_cols(sym)


def taylor(real, imag, right, left):
    n = real.shape[0]
    out = dot(stack_cols(jnp.concatenate([real, imag], axis=0)), right)
    rp = [out[:n, k * n : (k + 1) * n] for k in range(ORDER)]
    ip = [out[n:, k * n : (k + 1) * n] for k in range(ORDER)]
    u_real, u_imag = real, imag
    stacked = [None] * ORDER
    for k in range(ORDER + 1):
        if k:
            turn = k % 4
            if turn == 1:
                u_real, u_imag = u_real - ip[k - 1], u_imag + rp[k - 1]
            elif turn == 2:
                u_real, u_imag = u_real - rp[k - 1], u_imag - ip[k - 1]
            elif turn == 3:
                u_real, u_imag = u_real + ip[k - 1], u_imag - rp[k - 1]
            else:
                u_real, u_imag = u_real + rp[k - 1], u_imag + ip[k - 1]
        j = ORDER - k
        if j:
            turn = j % 4
            if turn == 1:
                pair = (u_imag, -u_real)
            elif turn == 2:
                pair = (-u_real, -u_imag)
            elif turn == 3:
                pair = (-u_imag, u_real)
            else:
                pair = (u_real, u_imag)
            stacked[j - 1] = stack_rows(jnp.concatenate(pair, axis=1))
    done = dot(left, jnp.concatenate(stacked, axis=0))
    return u_real + done[:, :n], u_imag + done[:, n:]


def free_kernel(run_parity, times, base, count, ints_ref, floats_ref, states_ref, right_ref, left_ref, out_ref):
    pair = 2 if count % 2 == 0 else 1

    @pl.when(ints_ref[0] == run_parity)
    def _():
        right, left = right_ref[...], left_ref[...]

        @pl.loop(0, count // pair)
        def _(step):
            for u in range(pair):
                out_ref[step * pair + u] = states_ref[step * pair + u]

            @pl.loop(0, times * SUBSTEPS)
            def _(turn):
                at = [step * pair + u for u in range(pair)]
                done = [taylor(out_ref[s, 0], out_ref[s, 1], right, left) for s in at]
                for s, (real, imag) in zip(at, done):
                    out_ref[s, 0] = real
                    out_ref[s, 1] = imag

            for u in range(pair):
                s = step * pair + u
                factor = floats_ref[base + s]
                scale = factor
                for _ in range(times - 1):
                    scale = scale * factor
                out_ref[s] = out_ref[s] * scale


def sided(real, imag, right, left):
    n = real.shape[0]
    after = dot(stack_cols(jnp.concatenate([real, imag], axis=0)), right)
    before = dot(left, stack_rows(jnp.concatenate([real, imag], axis=1)))
    return after[:n], after[n:], before[:, :n], before[:, n:]


def fetch(groups, index, stage_ref, u):
    slots = groups[0].shape[0]
    for k, group in enumerate(groups):
        local = index - k * slots

        @pl.when(jnp.logical_and(local >= 0, local < slots))
        def _():
            stage_ref[u] = group[local]


def child_pair(stage, mode, weight, right_ref, left_ref):
    ra, ia, rb, ib = sided(stage[0], stage[1], right_ref[mode], left_ref[mode])
    return weight * (ib - ia), weight * (ra - rb)


def parent_pair(stage, mode, wa, wc, right_ref, left_ref):
    ra, ia, rb, ib = sided(stage[0], stage[1], right_ref[mode], left_ref[mode])
    return wa * (ib - ia) + wc * (rb + ra), wa * (ra - rb) + wc * (ib + ia)


def part_of(parts, s):
    size = parts[0].shape[0]
    return parts[s // size], s % size


def send_kernel(sender, spots, sum_parts, pick_parts, ints_ref, floats_ref, right_ref, left_ref, *refs):
    acc_ref, stage_ref, list_ref = refs[-3:]
    outs = refs[-3 - sum_parts - pick_parts : -3]
    sums, picks = outs[:sum_parts], outs[sum_parts:]
    groups = refs[: -3 - sum_parts - pick_parts]
    slots = acc_ref.shape[0]
    total = sum(group.shape[0] for group in groups)

    @pl.when(ints_ref[0] == sender)
    def _():
        acc_ref[...] = jnp.zeros_like(acc_ref)
        for s in range(slots):
            pick, at = part_of(picks, s)
            fetch(groups, ints_ref[spots["below_parent"] + s], pick, at)

        def collect(c, count):
            mine = ints_ref[spots["own_target"] + c] >= 0

            @pl.when(mine)
            def _():
                list_ref[count] = c

            return count + mine.astype(jnp.int32)

        count = lax.fori_loop(0, total, collect, jnp.int32(0))

        @pl.loop(0, (count + slots - 1) // slots)
        def _(batch):
            children = []
            for u in range(slots):
                place = batch * slots + u
                c = list_ref[jnp.minimum(place, count - 1)]
                fetch(groups, c, stage_ref, u)
                weight = jnp.where(place < count, floats_ref[spots["own_weight"] + c], 0.0)
                children.append((c, weight))
            terms = [
                child_pair(stage_ref[u], ints_ref[spots["own_mode"] + c], weight, right_ref, left_ref)
                for u, (c, weight) in enumerate(children)
            ]
            for (c, _), (real, imag) in zip(children, terms):
                target = ints_ref[spots["own_target"] + c]
                acc_ref[target, 0] = acc_ref[target, 0] + real
                acc_ref[target, 1] = acc_ref[target, 1] + imag

        for s in range(slots):
            part, at = part_of(sums, s)
            part[at] = acc_ref[s]


def join_kernel(receiver, spots, sum_parts, pick_parts, ints_ref, floats_ref, right_ref, left_ref, *refs):
    out_ref = refs[-1]
    picks = refs[-1 - pick_parts : -1]
    sums = refs[-1 - pick_parts - sum_parts : -1 - pick_parts]
    frees = refs[: -1 - pick_parts - sum_parts]
    slots = out_ref.shape[0]

    @pl.when(ints_ref[0] == receiver)
    def _():
        terms = []
        for s in range(slots):
            pick, at = part_of(picks, s)
            terms.append(
                parent_pair(
                    pick[at],
                    ints_ref[spots["own_mode"] + s],
                    floats_ref[spots["own_a"] + s],
                    floats_ref[spots["own_c"] + s],
                    right_ref,
                    left_ref,
                )
            )
        for s in range(slots):
            scale = floats_ref[spots["own_scale"] + s]
            part, at = part_of(sums, s)
            out_ref[s, 0] = frees[0][s, 0] + scale * (part[at, 0] + terms[s][0])
            out_ref[s, 1] = frees[0][s, 1] + scale * (part[at, 1] + terms[s][1])

    if len(frees) > 1:

        @pl.when(ints_ref[0] != receiver)
        def _():
            out_ref[...] = frees[1][...]


def load_base(bases, acc_ref):
    size = bases[0].shape[0]
    for k, base in enumerate(bases):
        acc_ref[pl.ds(k * size, size)] = base[...]


def store_outs(acc_ref, outs):
    size = outs[0].shape[0]
    for k, out in enumerate(outs):
        out[...] = acc_ref[pl.ds(k * size, size)]


def side_kernel(side, receiver, spots, base_count, group_count, ints_ref, floats_ref, right_ref, left_ref, *refs):
    bases, groups = refs[:base_count], refs[base_count : base_count + group_count]
    outs, stage_ref = refs[base_count + group_count : -2], refs[-2]
    acc_ref = refs[-1] if len(outs) > 1 else outs[0]
    slots, size = stage_ref.shape[0], groups[0].shape[0]

    @pl.when(ints_ref[0] == receiver)
    def _():
        load_base(bases, acc_ref)

        @pl.loop(0, group_count * size // slots)
        def _(k):
            at = k * slots
            if side == "children":
                for j, group in enumerate(groups):
                    for i in range(size // slots):

                        @pl.when(k == j * (size // slots) + i)
                        def _():
                            stage_ref[...] = group[pl.ds(i * slots, slots)]

                terms = []
                for s in range(slots):
                    target = ints_ref[spots["below_parent"] + at + s]
                    weight = floats_ref[spots["below_weight"] + at + s] * floats_ref[spots["own_scale"] + target]
                    mode = ints_ref[spots["below_mode"] + at + s]
                    terms.append((target, child_pair(stage_ref[s], mode, weight, right_ref, left_ref)))
                for target, (real, imag) in terms:
                    acc_ref[target, 0] = acc_ref[target, 0] + real
                    acc_ref[target, 1] = acc_ref[target, 1] + imag
            else:
                for s in range(slots):
                    fetch(groups, ints_ref[spots["own_parent"] + at + s], stage_ref, s)
                terms = [
                    parent_pair(
                        stage_ref[s],
                        ints_ref[spots["own_mode"] + at + s],
                        floats_ref[spots["own_a"] + at + s],
                        floats_ref[spots["own_c"] + at + s],
                        right_ref,
                        left_ref,
                    )
                    for s in range(slots)
                ]
                for s in range(slots):
                    scale = floats_ref[spots["own_scale"] + at + s]
                    acc_ref[at + s, 0] = acc_ref[at + s, 0] + scale * terms[s][0]
                    acc_ref[at + s, 1] = acc_ref[at + s, 1] + scale * terms[s][1]

        if len(outs) > 1:
            store_outs(acc_ref, outs)


def call(kernel, out_shapes, limit, args, smem=2, us=1.0, scratch=()):
    specs = [pl.BlockSpec(memory_space=SMEM)] * smem
    specs += [pl.BlockSpec(memory_space=VMEM)] * (len(args) - smem)
    return pl.pallas_call(
        kernel,
        out_shape=out_shapes,
        in_specs=specs,
        out_specs=jax.tree.map(lambda _: pl.BlockSpec(memory_space=VMEM), out_shapes),
        scratch_shapes=scratch,
        compiler_params=pltpu.CompilerParams(vmem_limit_bytes=limit),
        cost_estimate=pl.CostEstimate(flops=int(us * 1.1e9), bytes_accessed=1 << 19, transcendentals=0),
    )(*args)


def turn_order(group):
    return sorted(range(1, group), key=lambda k: abs(k - group / 2))


def shards(sizes, blocks, live_slots, parent_index, bath_mode, hamiltonian, coupling, correlation, damping, link_weight):
    depths, group = sizes
    slots, _, n, _ = blocks.shape
    modes = coupling.shape[0]
    depth = lax.axis_index("depth")
    here = lax.axis_index("mode")
    total = group * slots
    limit = 8 * total * 2 * n * n * 4
    order = turn_order(group)
    split_hop = 2 if slots % 2 == 0 else 1

    def place(d, m):
        return d * group + m

    def turn(value, k, parity=None):
        pairs = [
            (place(d, m), place(d, (m + k) % group))
            for d in range(depths)
            for m in range(group)
            if parity is None or d % 2 == parity
        ]
        return lax.ppermute(value, AXES, pairs)

    def shift(value, step, parity=None):
        pairs = [
            (place(d, m), place(d + step, m))
            for d in range(depths)
            for m in range(group)
            if 0 <= d + step < depths and (parity is None or d % 2 == parity)
        ]
        return lax.ppermute(value, AXES, pairs)

    turned = {k: turn(blocks, k, 1) for k in order}
    first = [blocks] + [turned[k] for k in range(1, group)]

    parity = (depth % 2).astype(jnp.int32)
    live = live_slots.astype(f32)
    local_mode = bath_mode - here * modes
    own_select = (local_mode[:, None] == jnp.arange(modes, dtype=jnp.int32)[None, :]).astype(f32)
    coeff = jnp.sum(own_select[:, :, None] * correlation[None], axis=1)
    packed = jnp.stack(
        [parent_index.astype(f32), local_mode.astype(f32), link_weight, live, damping, coeff[:, 0], coeff[:, 1]]
    )
    rows = packed.shape[0]
    below_here = shift(packed, -1)
    above_here = shift(packed, 1, 0)

    near = jnp.concatenate([packed, above_here, below_here])
    lines = -(-near.size // (8 * n)) * 8
    note = jnp.zeros((modes, lines * n), f32).at[0, : near.size].set(near.reshape(-1)).reshape(modes, lines, n)
    payload = jnp.concatenate([coupling, note], axis=1)
    carried = {k: turn(payload, k, 1) for k in order}
    carried = [carried[k] for k in range(1, group)]

    def read(value):
        return value[0, n:].reshape(-1)[: near.size].reshape(3, rows, slots)

    back = jnp.repeat(jnp.arange(group, dtype=jnp.int32), slots) * modes

    def relative(parent):
        parent = parent.astype(jnp.int32)
        return ((here - parent // slots) % group) * slots + parent % slots

    spots = {}

    def tables(own_groups, below_groups):
        own = jnp.concatenate([packed] + own_groups, axis=1)
        below = jnp.concatenate([below_here] + below_groups, axis=1)
        ints, floats = [jnp.full((8,), parity)], []

        def put(parts, name, value):
            spots[name] = sum(part.shape[0] for part in parts)
            parts.append(value)

        own_parent = relative(own[0])
        put(ints, "own_parent", own_parent)
        put(ints, "own_target", jnp.where(own_parent < slots, own_parent, -1))
        put(ints, "own_mode", own[1].astype(jnp.int32) + back)
        put(ints, "below_parent", relative(below[0]))
        put(ints, "below_mode", below[1].astype(jnp.int32) + back)
        put(floats, "own_factor", own[3] * jnp.exp(-own[4] * (SUBSTEPS * substep)))
        put(floats, "own_weight", own[2] * own[3])
        put(floats, "own_scale", own[3] * couple_step)
        put(floats, "own_a", own[2] * own[5])
        put(floats, "own_c", own[2] * own[6])
        put(floats, "below_weight", below[2] * below[3])
        return jnp.concatenate(ints), jnp.concatenate(floats)

    own_factor = live * jnp.exp(-damping * (SUBSTEPS * substep))
    own_table = (jnp.full((8,), parity), own_factor)
    early = tables([read(c)[0] for c in carried], [read(c)[2] for c in carried])

    sds = jax.ShapeDtypeStruct
    one, half, whole = (sds((count, 2, n, n), f32) for count in (slots, total // 2, total))
    stage, big = VMEM((slots, 2, n, n), f32), VMEM(whole.shape, f32)
    operator_shapes = (sds((group * modes, 3 * n, n), bf16), sds((group * modes, n, 3 * n), bf16))

    powers = call(
        powers_kernel, (sds((3 * n, ORDER * n), bf16), sds((n, 3 * ORDER * n), bf16)), limit, (hamiltonian,), smem=0, us=1
    )
    early_operators = call(
        functools.partial(coupling_kernel, group, modes), operator_shapes, limit, (early[0], coupling, *carried), smem=1
    )

    def free(states, k, parity, times, table, count=None):
        count = slots if count is None else count
        base = 0 if table is own_table else spots["own_factor"] + k * slots
        return call(
            functools.partial(free_kernel, parity, times, base, count),
            sds((count, 2, n, n), f32),
            limit,
            (*table, states, *powers),
            us=4.7 * times,
        )

    def send(groups, sender, sum_parts, pick_parts, table, operators):
        shapes = [sds((slots // sum_parts, 2, n, n), f32)] * sum_parts
        shapes += [sds((slots // pick_parts, 2, n, n), f32)] * pick_parts
        outs = call(
            functools.partial(send_kernel, sender, spots, sum_parts, pick_parts),
            shapes,
            limit,
            (*table, *operators, *groups),
            us=2,
            scratch=[stage, stage, SMEM((total,), jnp.int32)],
        )
        return outs[:sum_parts], outs[sum_parts:]

    def join(frees, sums, picks, receiver, table, operators):
        return call(
            functools.partial(join_kernel, receiver, spots, len(sums), len(picks)),
            one,
            limit,
            (*table, *operators, *frees, *sums, *picks),
            us=1,
        )

    def side(kind, bases, groups, receiver, parts):
        return call(
            functools.partial(side_kernel, kind, receiver, spots, len(bases), len(groups)),
            [half] * 2 if parts else [whole],
            limit,
            (*late, *operators, *bases, *groups),
            us=3,
            scratch=[stage, big] if parts else [stage, VMEM((8, n), f32)],
        )

    ranks = range(group)
    free_even = free(blocks, 0, 0, 1, own_table)
    free_odd = [free(first[k], k, 1, 2, early if k else own_table) for k in ranks]
    sums, picks = send(first, 1, 1, split_hop, early, early_operators)
    send_outs = (*sums, *picks)
    picks = [shift(value, 1, 1) for value in picks]
    sums = [shift(value, -1, 1) for value in sums]
    freed_up = lax.optimization_barrier((*carried, *send_outs))[: group - 1]
    passed = [shift(value, -1, 1) for value in freed_up]
    own_state = join([free_even], sums, picks, 0, early, early_operators)

    odd = parity > 0
    late = tables(
        [jnp.where(odd, read(c)[0], read(p)[1]) for c, p in zip(carried, passed)],
        [jnp.where(odd, read(c)[2], read(p)[0]) for c, p in zip(carried, passed)],
    )
    operators = call(
        functools.partial(coupling_kernel, group, modes), operator_shapes, limit, (late[0], coupling, *carried, *passed), smem=1
    )

    turned = {k: turn(own_state, k, 0) for k in order}
    gathered = [own_state] + [turned[k] for k in range(1, group)]
    from_below = [shift(value, -1, 0) for value in gathered]
    from_above = [shift(value, 1, 0) for value in gathered]
    free_even = [free(gathered[k], k, 0, 2, late if k else own_table) for k in ranks]
    states = side("parents", free_odd, from_above, 1, False)
    states = side("children", states, from_below, 1, True)

    from_above = [shift(value, 1, 1) for value in states]
    from_below = [shift(value, -1, 1) for value in states]
    last_odd = free(states[0], 0, 1, 2, own_table, slots)
    states = side("children", free_even, from_below, 0, False)
    states = side("parents", states, from_above, 0, True)

    sums, picks = send(states, 0, split_hop, 1, late, operators)
    sums = [shift(value, -1, 0) for value in sums]
    picks = [shift(value, 1, 0) for value in picks]
    last_even = free(states[0], 0, 0, 1, own_table, slots)
    return join([last_odd, last_even], sums, picks, 1, late, operators)


def solution(mesh):
    sizes = (mesh.shape["depth"], mesh.shape["mode"])

    def whole(*args):
        return shards(sizes, *args)

    return jax.shard_map(
        whole,
        mesh=mesh,
        in_specs=(
            P(("depth", "mode"), None, None, None),
            P(("depth", "mode")),
            P(("depth", "mode")),
            P(("depth", "mode")),
            P(),
            P("mode", None, None),
            P("mode", None),
            P(("depth", "mode")),
            P(("depth", "mode")),
        ),
        out_specs=P(("depth", "mode"), None, None, None),
        check_vma=False,
    )
```

```python
import functools
import math
import jax
import jax.numpy as jnp
from jax import lax
from jax.experimental import pallas as pl
from jax.experimental.pallas import tpu as pltpu
from jax.sharding import PartitionSpec as P

SUBSTEPS = 2
ORDER = 4
substep = 0.7
couple_step = 0.2

AXES = ("depth", "mode")
VMEM = pltpu.VMEM
SMEM = pltpu.SMEM
bf16 = jnp.bfloat16
f32 = jnp.float32

PARENT, MODE, LIVE, FACTOR, WEIGHT, WEIGHT_A, WEIGHT_C = range(7)
ROWS, LANES = 8, 128


def split(value):
    high = value.astype(bf16)
    return high, (value - high.astype(f32)).astype(bf16)


def stack_rows(value):
    high, low = split(value)
    return jnp.concatenate([high, high, low], axis=0)


def stack_cols(value):
    high, low = split(value)
    return jnp.concatenate([high, low, high], axis=1)


def dot(first, second):
    return jnp.dot(first, second, preferred_element_type=f32)


def exact(first, second):
    return jnp.dot(first, second, preferred_element_type=f32, precision=lax.Precision.HIGHEST)


def odd_depth():
    return lax.rem(lax.axis_index("depth"), 2)


def pack_kernel(live_ref, parent_ref, mode_ref, damping_ref, weight_ref, corr_ref, blocks_ref, coupling_ref, out_ref, table_ref):
    slots, modes = blocks_ref.shape[0], coupling_ref.shape[0]
    out_ref[pl.ds(0, 2 * slots)] = blocks_ref[...].reshape(2 * slots, *blocks_ref.shape[2:])
    out_ref[pl.ds(2 * slots + 1, modes)] = coupling_ref[...]
    row = lax.broadcasted_iota(jnp.int32, (ROWS, LANES), 0)
    lane = lax.broadcasted_iota(jnp.int32, (ROWS, LANES), 1)
    table = jnp.zeros((ROWS, LANES), f32)
    first_mode = lax.axis_index("mode") * modes
    for s in range(slots):
        mode = mode_ref[s] - first_mode
        live = live_ref[s].astype(f32)
        weight = weight_ref[s]
        values = {
            PARENT: parent_ref[s].astype(f32),
            MODE: mode.astype(f32),
            LIVE: live,
            FACTOR: damping_ref[s] * (-SUBSTEPS * substep),
            WEIGHT: weight * live,
            WEIGHT_A: weight * corr_ref[mode, 0],
            WEIGHT_C: weight * corr_ref[mode, 1],
        }
        for at, value in values.items():
            table = jnp.where(jnp.logical_and(row == at, lane == s), value, table)
    live_row = table[LIVE : LIVE + 1]
    table = jnp.where(row == FACTOR, live_row * jnp.exp(table), table)
    table_ref[...] = table
    out_ref[2 * slots] = jnp.zeros(out_ref.shape[1:], f32)
    out_ref[2 * slots, :ROWS, :LANES] = table


def powers_kernel(ham_ref, right_ref, left_ref):
    n = ham_ref.shape[0]
    ham = (ham_ref[...] + ham_ref[...].T) * 0.5
    power = ham
    for k in range(1, ORDER + 1):
        if k > 1:
            power = exact(power, ham)
        scaled = power * (substep**k / math.factorial(k))
        right_ref[:, (k - 1) * n : k * n] = stack_rows(scaled)
        left_ref[:, (k - 1) * 3 * n : k * 3 * n] = stack_cols(scaled)


def pull(sources, smem_ref, sem_ref):
    copies = [pltpu.make_async_copy(source, smem_ref.at[i], sem_ref.at[i]) for i, source in enumerate(sources)]
    for copy in copies:
        copy.start()
    for copy in copies:
        copy.wait()


def table_at(ref, slab):
    return ref.at[slab, pl.ds(0, ROWS), pl.ds(0, LANES)]


def operators_kernel(group, modes, skip, parity, own_ref, *refs):
    sources, outs = refs[: -2 - (parity is None)], refs[-2 - (parity is None) :]
    right_ref, left_ref = outs[0], outs[1]

    def fill(value_of):
        for k in range(group):
            for i in range(modes):
                value = own_ref[i] if k == 0 else value_of(k, i)
                sym = (value + value.T) * 0.5
                right_ref[k * modes + i] = stack_rows(sym)
                left_ref[k * modes + i] = stack_cols(sym)
                if parity is None and k:
                    outs[2][(k - 1) * modes + i] = value

    if parity is None:
        fill(lambda k, i: sources[k - 1][skip + i])
    else:
        pl.when(odd_depth() == parity)(lambda: fill(lambda k, i: sources[0][(k - 1) * modes + i]))


def taylor(real, imag, right, left):
    n = real.shape[0]
    out = dot(stack_cols(jnp.concatenate([real, imag], axis=0)), right)
    rp = [out[:n, k * n : (k + 1) * n] for k in range(ORDER)]
    ip = [out[n:, k * n : (k + 1) * n] for k in range(ORDER)]
    u_real, u_imag = real, imag
    stacked = [None] * ORDER
    for k in range(ORDER + 1):
        if k:
            turn = k % 4
            if turn == 1:
                u_real, u_imag = u_real - ip[k - 1], u_imag + rp[k - 1]
            elif turn == 2:
                u_real, u_imag = u_real - rp[k - 1], u_imag - ip[k - 1]
            elif turn == 3:
                u_real, u_imag = u_real + ip[k - 1], u_imag - rp[k - 1]
            else:
                u_real, u_imag = u_real + rp[k - 1], u_imag + ip[k - 1]
        j = ORDER - k
        if j:
            turn = j % 4
            if turn == 1:
                pair = (u_imag, -u_real)
            elif turn == 2:
                pair = (-u_real, -u_imag)
            elif turn == 3:
                pair = (-u_imag, u_real)
            else:
                pair = (u_real, u_imag)
            stacked[j - 1] = stack_rows(jnp.concatenate(pair, axis=1))
    done = dot(left, jnp.concatenate(stacked, axis=0))
    return u_real + done[:, :n], u_imag + done[:, n:]


def free_kernel(run_parity, times, slots, states_ref, right_ref, left_ref, out_ref):
    pair = 2 if slots % 2 == 0 else 1

    @pl.when(odd_depth() == run_parity)
    def _():
        right, left = right_ref[...], left_ref[...]
        out_ref[...] = states_ref[pl.ds(0, 2 * slots)]

        @pl.loop(0, slots // pair)
        def _(step):
            @pl.loop(0, times * SUBSTEPS)
            def _(turn):
                at = [2 * (step * pair + u) for u in range(pair)]
                done = [taylor(out_ref[s], out_ref[s + 1], right, left) for s in at]
                for s, (real, imag) in zip(at, done):
                    out_ref[s] = real
                    out_ref[s + 1] = imag

        factors = states_ref[2 * slots, FACTOR : FACTOR + 1, :LANES]
        for s in range(slots):
            scale = factors[:, s : s + 1] ** times
            out_ref[2 * s] = out_ref[2 * s] * scale
            out_ref[2 * s + 1] = out_ref[2 * s + 1] * scale


def sided(real, imag, right, left):
    n = real.shape[0]
    after = dot(stack_cols(jnp.concatenate([real, imag], axis=0)), right)
    before = dot(left, stack_rows(jnp.concatenate([real, imag], axis=1)))
    return after[:n], after[n:], before[:, :n], before[:, n:]


class Layout:
    def __init__(self, refs, slots, group):
        self.refs, self.slots, self.group = refs, slots, group
        self.held = group // len(refs)
        self.stride = 2 * slots + 1

    def base(self, k):
        return self.refs[k // self.held], (k % self.held) * self.stride

    def table(self, k):
        ref, base = self.base(k)
        return table_at(ref, base + 2 * self.slots)

    def fetch(self, index, stage_ref, at):
        for k in range(self.group):
            ref, base = self.base(k)
            local = index - k * self.slots

            @pl.when(jnp.logical_and(local >= 0, local < self.slots))
            def _():
                stage_ref[pl.ds(at, 2)] = ref[pl.ds(base + 2 * local, 2)]


def entry(tab, row, c, slots):
    if isinstance(c, int):
        return tab[c // slots, row, c % slots]
    return tab[lax.div(c, slots), row, lax.rem(c, slots)]


def operator_of(tab, c, slots, modes):
    back = c // slots if isinstance(c, int) else lax.div(c, slots)
    return back * modes + entry(tab, MODE, c, slots).astype(jnp.int32)


def parent_of(tab, c, slots, group):
    parent = entry(tab, PARENT, c, slots).astype(jnp.int32)
    back = lax.rem(lax.axis_index("mode") - lax.div(parent, slots) + group, group)
    return back * slots + lax.rem(parent, slots)


def child_pair(stage_ref, at, mode, weight, right_ref, left_ref):
    ra, ia, rb, ib = sided(stage_ref[at], stage_ref[at + 1], right_ref[mode], left_ref[mode])
    return weight * (ib - ia), weight * (ra - rb)


def parent_pair(stage_ref, at, mode, wa, wc, right_ref, left_ref):
    ra, ia, rb, ib = sided(stage_ref[at], stage_ref[at + 1], right_ref[mode], left_ref[mode])
    return wa * (ib - ia) + wc * (rb + ra), wa * (ra - rb) + wc * (ib + ia)


def part_of(parts, s):
    size = parts[0].shape[0] // 2
    return parts[s // size], 2 * (s % size)


def send_kernel(sender, slots, group, modes, sum_parts, pick_parts, near_ref, right_ref, left_ref, *refs):
    acc_ref, stage_ref, list_ref, tab, sem_ref = refs[-5:]
    tabs_ref = refs[-6]
    outs = refs[-6 - sum_parts - pick_parts : -6]
    sums, picks = outs[:sum_parts], outs[sum_parts:]
    groups = Layout(refs[: -6 - sum_parts - pick_parts], slots, group)

    @pl.when(odd_depth() == sender)
    def _():
        pull([groups.table(k) for k in range(group)] + [near_ref], tab, sem_ref)
        for k in range(group):
            ref, base = groups.base(k)
            tabs_ref[k] = ref[base + 2 * slots, :ROWS, :LANES]
        acc_ref[...] = jnp.zeros_like(acc_ref)
        for s in range(slots):
            pick, at = part_of(picks, s)
            groups.fetch(parent_of(tab, group * slots + s, slots, group), pick, at)

        def collect(c, count):
            mine = parent_of(tab, c, slots, group) < slots

            @pl.when(mine)
            def _():
                list_ref[count] = c

            return count + mine.astype(jnp.int32)

        count = lax.fori_loop(0, group * slots, collect, jnp.int32(0))

        @pl.loop(0, lax.div(count + slots - 1, slots))
        def _(batch):
            children = []
            for u in range(slots):
                place = batch * slots + u
                c = list_ref[jnp.minimum(place, count - 1)]
                groups.fetch(c, stage_ref, 2 * u)
                children.append((c, jnp.where(place < count, entry(tab, WEIGHT, c, slots), 0.0)))
            terms = [
                child_pair(stage_ref, 2 * u, operator_of(tab, c, slots, modes), weight, right_ref, left_ref)
                for u, (c, weight) in enumerate(children)
            ]
            for (c, _), (real, imag) in zip(children, terms):
                target = 2 * parent_of(tab, c, slots, group)
                acc_ref[target] = acc_ref[target] + real
                acc_ref[target + 1] = acc_ref[target + 1] + imag

        for s in range(slots):
            part, at = part_of(sums, s)
            part[pl.ds(at, 2)] = acc_ref[pl.ds(2 * s, 2)]


def join_kernel(receiver, slots, modes, sum_parts, pick_parts, own_ref, right_ref, left_ref, *refs):
    out_ref, tab, sem_ref = refs[-3:]
    picks = refs[-3 - pick_parts : -3]
    sums = refs[-3 - pick_parts - sum_parts : -3 - pick_parts]
    frees = refs[: -3 - pick_parts - sum_parts]
    final = len(frees) > 1

    def store(at, value):
        if final:
            out_ref[at // 2, at % 2] = value
        else:
            out_ref[at] = value

    @pl.when(odd_depth() == receiver)
    def _():
        pull([own_ref], tab, sem_ref)
        terms = []
        for s in range(slots):
            pick, at = part_of(picks, s)
            wa, wc = tab[0, WEIGHT_A, s], tab[0, WEIGHT_C, s]
            terms.append(parent_pair(pick, at, operator_of(tab, s, slots, modes), wa, wc, right_ref, left_ref))
        for s in range(slots):
            scale = tab[0, LIVE, s] * couple_step
            part, at = part_of(sums, s)
            for i in range(2):
                store(2 * s + i, frees[0][2 * s + i] + scale * (part[at + i] + terms[s][i]))
        if not final:
            out_ref[2 * slots] = jnp.zeros(out_ref.shape[1:], f32)
            out_ref[2 * slots, :ROWS, :LANES] = own_ref[...]

    if final:

        @pl.when(odd_depth() != receiver)
        def _():
            for at in range(2 * slots):
                store(at, frees[1][at])


def side_kernel(side, receiver, slots, group, modes, base_count, group_count, tab_count, right_ref, left_ref, *refs):
    stage_ref, tab, sem_ref = refs[-3:]
    bases = refs[:base_count]
    groups = Layout(refs[base_count : base_count + group_count], slots, group)
    tab_refs = refs[base_count + group_count : base_count + group_count + tab_count]
    outs = refs[base_count + group_count + tab_count : -3]
    second = len(outs) > 2 or base_count == 1
    if second:
        out = Layout(outs, slots, group)

        def at_slot(k):
            return out.base(k)

    else:
        acc_ref, tabs_ref = outs

        def at_slot(k):
            return acc_ref, 2 * slots * k

    own_tables = [tab_refs[0].at[k] for k in range(group)]
    if tab_count > 1:
        gathered = Layout(tab_refs, slots, group)
        own_tables = [gathered.table(k) for k in range(group)]

    @pl.when(odd_depth() == receiver)
    def _():
        below = [groups.table(k) for k in range(group)] if side == "children" else []
        pull(own_tables + below, tab, sem_ref)
        for k in range(group):
            ref, base = at_slot(k)
            if base_count == 1:
                ref[pl.ds(base, 2 * slots)] = bases[0][pl.ds(2 * slots * k, 2 * slots)]
            else:
                ref[pl.ds(base, 2 * slots)] = bases[k][...]
            if second:
                ref[base + 2 * slots] = jnp.zeros(ref.shape[1:], f32)
                ref[base + 2 * slots, :ROWS, :LANES] = tab_refs[0][k]
            elif tab_count > 1:
                source, origin = gathered.base(k)
                tabs_ref[k] = source[origin + 2 * slots, :ROWS, :LANES]

        def add(index, pair):
            for k in range(group):
                ref, base = at_slot(k)
                local = index - k * slots

                @pl.when(jnp.logical_and(local >= 0, local < slots))
                def _():
                    for i in range(2):
                        ref[base + 2 * local + i] = ref[base + 2 * local + i] + pair[i]

        @pl.loop(0, group)
        def _(k):
            at = k * slots
            targets, terms = [], []
            for s in range(slots):
                c = at + s
                if side == "children":
                    groups.fetch(c, stage_ref, 2 * s)
                else:
                    groups.fetch(parent_of(tab, c, slots, group), stage_ref, 2 * s)
            for s in range(slots):
                c = at + s
                if side == "children":
                    b = c + group * slots
                    target = parent_of(tab, b, slots, group)
                    weight = entry(tab, WEIGHT, b, slots) * (entry(tab, LIVE, target, slots) * couple_step)
                    mode = operator_of(tab, b, slots, modes) - group * modes
                    terms.append(child_pair(stage_ref, 2 * s, mode, weight, right_ref, left_ref))
                else:
                    target = c
                    scale = entry(tab, LIVE, c, slots) * couple_step
                    wa, wc = entry(tab, WEIGHT_A, c, slots) * scale, entry(tab, WEIGHT_C, c, slots) * scale
                    mode = operator_of(tab, c, slots, modes)
                    terms.append(parent_pair(stage_ref, 2 * s, mode, wa, wc, right_ref, left_ref))
                targets.append(target)
            for target, pair in zip(targets, terms):
                if second:
                    add(target, pair)
                else:
                    acc_ref[2 * target] = acc_ref[2 * target] + pair[0]
                    acc_ref[2 * target + 1] = acc_ref[2 * target + 1] + pair[1]


def call(kernel, out_shapes, limit, args, smem=0, us=1.0, scratch=()):
    specs = [pl.BlockSpec(memory_space=SMEM)] * smem
    specs += [pl.BlockSpec(memory_space=VMEM)] * (len(args) - smem)
    return pl.pallas_call(
        kernel,
        out_shape=out_shapes,
        in_specs=specs,
        out_specs=jax.tree.map(lambda _: pl.BlockSpec(memory_space=VMEM), out_shapes),
        scratch_shapes=scratch,
        compiler_params=pltpu.CompilerParams(vmem_limit_bytes=limit),
        cost_estimate=pl.CostEstimate(flops=int(us * 1.1e9), bytes_accessed=1 << 19, transcendentals=0),
    )(*args)


def turn_order(group):
    return sorted(range(1, group), key=lambda k: abs(k - group / 2))


def shards(sizes, blocks, live_slots, parent_index, bath_mode, hamiltonian, coupling, correlation, damping, link_weight):
    depths, group = sizes
    slots, _, n, _ = blocks.shape
    modes = coupling.shape[0]
    total = group * slots
    limit = 8 * total * 2 * n * n * 4
    order = turn_order(group)
    split_hop = 2 if slots % 2 == 0 else 1
    ranks = range(group)

    def place(d, m):
        return d * group + m

    def turn(value, k, parity):
        pairs = [(place(d, m), place(d, (m + k) % group)) for d in range(parity, depths, 2) for m in ranks]
        return lax.ppermute(value, AXES, pairs)

    def shift(value, step, parity=None):
        pairs = [
            (place(d, m), place(d + step, m))
            for d in range(depths)
            for m in ranks
            if 0 <= d + step < depths and (parity is None or d % 2 == parity)
        ]
        return lax.ppermute(value, AXES, pairs)

    def slabs(count):
        return jax.ShapeDtypeStruct((count, n, n), f32)

    def sds(*shape, dtype=f32):
        return jax.ShapeDtypeStruct(shape, dtype)

    own, plain = 2 * slots + 1, 2 * slots
    table_shape = sds(ROWS, LANES)
    stage = VMEM((plain, n, n), f32)

    def tables(count):
        return [SMEM((count, ROWS, LANES), f32), pltpu.SemaphoreType.DMA((count,))]

    operator_shapes = (sds(group * modes, 3 * n, n, dtype=bf16), sds(group * modes, n, 3 * n, dtype=bf16))

    packed, own_table = call(
        pack_kernel,
        (slabs(own + modes), table_shape),
        limit,
        (live_slots, parent_index, bath_mode, damping, link_weight, correlation, blocks, coupling),
        smem=6,
    )
    turned = {k: turn(packed, k, 1) for k in order}
    first = [packed] + [turned[k] for k in range(1, group)]
    near_table = shift(own_table, -1)
    powers = call(
        powers_kernel, (sds(3 * n, ORDER * n, dtype=bf16), sds(n, 3 * ORDER * n, dtype=bf16)), limit, (hamiltonian,)
    )
    *operators_odd, raw = call(
        functools.partial(operators_kernel, group, modes, own, None),
        (*operator_shapes, slabs((group - 1) * modes)),
        limit,
        (coupling, *first[1:]),
    )

    def free(states, parity, times):
        return call(
            functools.partial(free_kernel, parity, times, slots), slabs(plain), limit, (states, *powers), us=4.7 * times
        )

    def send(groups, sender, sum_parts, pick_parts, operators):
        shapes = [slabs(plain // sum_parts)] * sum_parts + [slabs(plain // pick_parts)] * pick_parts
        outs = call(
            functools.partial(send_kernel, sender, slots, group, modes, sum_parts, pick_parts),
            [*shapes, sds(group, ROWS, LANES)],
            limit,
            (near_table, *operators, *groups),
            us=2,
            scratch=[stage, stage, SMEM((total,), jnp.int32), *tables(group + 1)],
        )
        return outs[:sum_parts], outs[sum_parts:-1], outs[-1]

    def join(frees, sums, picks, receiver, operators):
        return call(
            functools.partial(join_kernel, receiver, slots, modes, len(sums), len(picks)),
            sds(*blocks.shape) if len(frees) > 1 else slabs(own),
            limit,
            (own_table, *operators, *frees, *sums, *picks),
            scratch=tables(1),
        )

    def side(kind, bases, groups, tabs, receiver, operators):
        second = len(bases) == 1
        halves = 2 if group % 2 == 0 else 1
        return call(
            functools.partial(side_kernel, kind, receiver, slots, group, modes, len(bases), len(groups), len(tabs)),
            [slabs(group * own // halves)] * halves if second else [slabs(2 * total), sds(group, ROWS, LANES)],
            limit,
            (*operators, *bases, *groups, *tabs),
            us=3,
            scratch=[stage, *tables(2 * group if kind == "children" else group)],
        )

    free_even = free(packed, 0, 1)
    free_odd = [free(first[k], 1, 2) for k in ranks]
    sums, picks, tabs_odd = send(first, 1, 1, split_hop, operators_odd)
    picks = [shift(value, 1, 1) for value in picks]
    sums = [shift(value, -1, 1) for value in sums]
    own_state = join([free_even], sums, picks, 0, operators_odd)

    turned = {k: turn(own_state, k, 0) for k in order}
    gathered = [own_state] + [turned[k] for k in range(1, group)]
    from_below = [shift(value, -1, 0) for value in gathered]
    from_above = [shift(value, 1, 0) for value in gathered]
    free_even = [free(gathered[k], 0, 2) for k in ranks]
    passed = shift(raw, -1, 1)
    operators_even = call(
        functools.partial(operators_kernel, group, modes, own, 0), operator_shapes, limit, (coupling, passed)
    )
    states, _ = side("parents", free_odd, from_above, [tabs_odd], 1, operators_odd)
    states = side("children", [states], from_below, [tabs_odd], 1, operators_odd)

    from_above = [shift(value, 1, 1) for value in states]
    from_below = [shift(value, -1, 1) for value in states]
    last_odd = free(states[0], 1, 2)
    states, tabs_even = side("children", free_even, from_below, gathered, 0, operators_even)
    states = side("parents", [states], from_above, [tabs_even], 0, operators_even)

    sums, picks, _ = send(states, 0, split_hop, 1, operators_even)
    sums = [shift(value, -1, 0) for value in sums]
    picks = [shift(value, 1, 0) for value in picks]
    last_even = free(states[0], 0, 1)
    return join([last_odd, last_even], sums, picks, 1, operators_odd)


def solution(mesh):
    sizes = (mesh.shape["depth"], mesh.shape["mode"])

    def whole(*args):
        return shards(sizes, *args)

    return jax.shard_map(
        whole,
        mesh=mesh,
        in_specs=(
            P(("depth", "mode"), None, None, None),
            P(("depth", "mode")),
            P(("depth", "mode")),
            P(("depth", "mode")),
            P(),
            P("mode", None, None),
            P("mode", None),
            P(("depth", "mode")),
            P(("depth", "mode")),
        ),
        out_specs=P(("depth", "mode"), None, None, None),
        check_vma=False,
    )
```

```python
import functools
import math
import jax
import jax.numpy as jnp
from jax import lax
from jax.experimental import pallas as pl
from jax.experimental.pallas import tpu as pltpu
from jax.sharding import PartitionSpec as P

SUBSTEPS = 2
ORDER = 4
substep = 0.7
couple_step = 0.2

AXES = ("depth", "mode")
VMEM = pltpu.VMEM
SMEM = pltpu.SMEM
bf16 = jnp.bfloat16
f32 = jnp.float32

PARENT, MODE, LIVE, FACTOR, WEIGHT, WEIGHT_A, WEIGHT_C = range(7)
ROWS, LANES = 8, 128
PACK_LIMIT = 56 << 20


def split(value):
    high = value.astype(bf16)
    return high, (value - high.astype(f32)).astype(bf16)


def stack_rows(value):
    high, low = split(value)
    return jnp.concatenate([high, high, low], axis=0)


def stack_cols(value):
    high, low = split(value)
    return jnp.concatenate([high, low, high], axis=1)


def dot(first, second):
    return jnp.dot(first, second, preferred_element_type=f32)


def exact(first, second):
    return jnp.dot(first, second, preferred_element_type=f32, precision=lax.Precision.HIGHEST)


def odd_depth():
    return lax.rem(lax.axis_index("depth"), 2)


def rows(at, n, count=1):
    if not isinstance(at, int):
        at = pl.multiple_of(at, ROWS)
    return pl.ds(at, count * n)


def pack_kernel(live_ref, parent_ref, mode_ref, damping_ref, weight_ref, corr_ref, blocks_ref, coupling_ref, out_ref, table_ref):
    slots, n = live_ref.shape[0], blocks_ref.shape[1]
    size = blocks_ref.shape[0]
    out_ref[pl.ds(0, size)] = blocks_ref[...]
    out_ref[pl.ds(size + ROWS, coupling_ref.shape[0])] = coupling_ref[...]
    row = lax.broadcasted_iota(jnp.int32, (ROWS, n), 0)
    lane = lax.broadcasted_iota(jnp.int32, (ROWS, n), 1)
    table = jnp.zeros((ROWS, n), f32)
    first_mode = lax.axis_index("mode") * corr_ref.shape[0]
    for s in range(slots):
        mode = mode_ref[s] - first_mode
        live = live_ref[s].astype(f32)
        weight = weight_ref[s]
        values = {
            PARENT: parent_ref[s].astype(f32),
            MODE: mode.astype(f32),
            LIVE: live,
            FACTOR: damping_ref[s] * (-SUBSTEPS * substep),
            WEIGHT: weight * live,
            WEIGHT_A: weight * corr_ref[mode, 0],
            WEIGHT_C: weight * corr_ref[mode, 1],
        }
        for at, value in values.items():
            table = jnp.where(jnp.logical_and(row == at, lane == s), value, table)
    live_row = table[LIVE : LIVE + 1]
    table = jnp.where(row == FACTOR, live_row * jnp.exp(table), table)
    table_ref[...] = table
    out_ref[pl.ds(size, ROWS)] = table


def powers_kernel(ham_ref, right_ref, left_ref):
    n = ham_ref.shape[0]
    ham = (ham_ref[...] + ham_ref[...].T) * 0.5
    power = ham
    for k in range(1, ORDER + 1):
        if k > 1:
            power = exact(power, ham)
        scaled = power * (substep**k / math.factorial(k))
        right_ref[:, (k - 1) * n : k * n] = stack_rows(scaled)
        left_ref[:, (k - 1) * 3 * n : k * 3 * n] = stack_cols(scaled)


class Layout:
    def __init__(self, refs, slots, group):
        self.refs, self.slots, self.group = refs, slots, group
        self.n = refs[0].shape[1]
        self.relay = len(refs) == group + 1
        self.held = 1 if self.relay else group // len(refs)
        self.size = 2 * slots * self.n
        self.stride = self.size + ROWS

    def places(self, k):
        if self.relay and k in (1, self.group - 1):
            edge = lax.axis_index("mode") == (0 if k == 1 else self.group - 1)
            return [(jnp.logical_not(edge), self.refs[k], 0), (edge, self.refs[-1], 0)]
        return [(None, self.refs[k // self.held], (k % self.held) * self.stride)]

    def each(self, k, body):
        for condition, ref, base in self.places(k):
            if condition is None:
                body(ref, base)
            else:
                pl.when(condition)(functools.partial(body, ref, base))

    def table(self, k):
        return [
            (condition, ref.at[pl.ds(base + self.size, ROWS), pl.ds(0, LANES)]) for condition, ref, base in self.places(k)
        ]

    def copy_table(self, k, target_ref, at):
        def body(ref, base):
            target_ref[at] = ref[pl.ds(base + self.size, ROWS)]

        self.each(k, body)

    def fetch(self, index, stage_ref, at):
        for k in range(self.group):
            local = index - k * self.slots
            inside = jnp.logical_and(local >= 0, local < self.slots)
            for condition, ref, base in self.places(k):
                here = inside if condition is None else jnp.logical_and(inside, condition)

                @pl.when(here)
                def _():
                    stage_ref[rows(at * self.n, self.n, 2)] = ref[rows(base + 2 * local * self.n, self.n, 2)]


def pull(sources, smem_ref, sem_ref):
    copies = []
    for i, source in enumerate(sources):
        for condition, ref in source if isinstance(source, list) else [(None, source)]:
            copy = pltpu.make_async_copy(ref, smem_ref.at[i], sem_ref.at[i])
            if condition is None:
                copy.start()
            else:
                pl.when(condition)(copy.start)
        copies.append(copy)
    for copy in copies:
        copy.wait()


def narrow(ref):
    return ref.at[pl.ds(0, ROWS), pl.ds(0, LANES)]


def operators_kernel(slots, group, modes, parity, own_ref, *refs):
    outs = refs[-2 - (parity is None) :]
    sources = refs[: -len(outs)]
    right_ref, left_ref = outs[0], outs[1]
    n = own_ref.shape[1]

    def put(at, value):
        sym = (value + value.T) * 0.5
        right_ref[at] = stack_rows(sym)
        left_ref[at] = stack_cols(sym)

    def own():
        for i in range(modes):
            put(i, own_ref[rows(i * n, n)])

    if parity is None:
        own()
        groups = Layout(sources, slots, group)
        for k in range(1, group):

            def body(ref, base, k=k):
                for i in range(modes):
                    value = ref[rows(base + groups.stride + i * n, n)]
                    put(k * modes + i, value)
                    outs[2][rows(((k - 1) * modes + i) * n, n)] = value

            groups.each(k, body)
    else:

        @pl.when(odd_depth() == parity)
        def _():
            own()
            for at in range(modes, group * modes):
                put(at, sources[0][rows((at - modes) * n, n)])


def taylor(real, imag, right, left):
    n = real.shape[0]
    out = dot(stack_cols(jnp.concatenate([real, imag], axis=0)), right)
    rp = [out[:n, k * n : (k + 1) * n] for k in range(ORDER)]
    ip = [out[n:, k * n : (k + 1) * n] for k in range(ORDER)]
    u_real, u_imag = real, imag
    stacked = [None] * ORDER
    for k in range(ORDER + 1):
        if k:
            turn = k % 4
            if turn == 1:
                u_real, u_imag = u_real - ip[k - 1], u_imag + rp[k - 1]
            elif turn == 2:
                u_real, u_imag = u_real - rp[k - 1], u_imag - ip[k - 1]
            elif turn == 3:
                u_real, u_imag = u_real + ip[k - 1], u_imag - rp[k - 1]
            else:
                u_real, u_imag = u_real + rp[k - 1], u_imag + ip[k - 1]
        j = ORDER - k
        if j:
            turn = j % 4
            if turn == 1:
                pair = (u_imag, -u_real)
            elif turn == 2:
                pair = (-u_real, -u_imag)
            elif turn == 3:
                pair = (-u_imag, u_real)
            else:
                pair = (u_real, u_imag)
            stacked[j - 1] = stack_rows(jnp.concatenate(pair, axis=1))
    done = dot(left, jnp.concatenate(stacked, axis=0))
    return u_real + done[:, :n], u_imag + done[:, n:]


def free_kernel(run_parity, times, slots, group, k, right_ref, left_ref, *refs):
    out_ref = refs[-1]
    pair = 2 if slots % 2 == 0 else 1
    n = out_ref.shape[1]
    size = 2 * slots * n
    edge = lax.axis_index("mode") == (0 if k == 1 else group - 1)

    def each(body):
        if len(refs) == 2:
            body(refs[0])
        else:
            pl.when(jnp.logical_not(edge))(lambda: body(refs[0]))
            pl.when(edge)(lambda: body(refs[1]))

    @pl.when(odd_depth() == run_parity)
    def _():
        right, left = right_ref[...], left_ref[...]

        def load(ref):
            out_ref[...] = ref[pl.ds(0, size)]

        each(load)

        @pl.loop(0, slots // pair)
        def _(step):
            @pl.loop(0, times * SUBSTEPS)
            def _(turn):
                at = [(rows(2 * s * n, n), rows((2 * s + 1) * n, n)) for s in [step * pair + u for u in range(pair)]]
                done = [taylor(out_ref[r], out_ref[i], right, left) for r, i in at]
                for (r, i), (real, imag) in zip(at, done):
                    out_ref[r] = real
                    out_ref[i] = imag

        def damp(ref):
            factors = ref[pl.ds(size, ROWS)][FACTOR : FACTOR + 1]
            for s in range(slots):
                scale = factors[:, s : s + 1] ** times
                at = rows(2 * s * n, n, 2)
                out_ref[at] = out_ref[at] * scale

        each(damp)


def sided(real, imag, right, left):
    n = real.shape[0]
    after = dot(stack_cols(jnp.concatenate([real, imag], axis=0)), right)
    before = dot(left, stack_rows(jnp.concatenate([real, imag], axis=1)))
    return after[:n], after[n:], before[:, :n], before[:, n:]


def entry(tab, row, c, slots):
    if isinstance(c, int):
        return tab[c // slots, row, c % slots]
    return tab[lax.div(c, slots), row, lax.rem(c, slots)]


def operator_of(tab, c, slots, modes):
    back = c // slots if isinstance(c, int) else lax.div(c, slots)
    return back * modes + entry(tab, MODE, c, slots).astype(jnp.int32)


def parent_of(tab, c, slots, group):
    parent = entry(tab, PARENT, c, slots).astype(jnp.int32)
    back = lax.rem(lax.axis_index("mode") - lax.div(parent, slots) + group, group)
    return back * slots + lax.rem(parent, slots)


def child_pair(stage_ref, at, mode, weight, right_ref, left_ref):
    n = stage_ref.shape[1]
    ra, ia, rb, ib = sided(stage_ref[rows(at * n, n)], stage_ref[rows((at + 1) * n, n)], right_ref[mode], left_ref[mode])
    return weight * (ib - ia), weight * (ra - rb)


def parent_pair(stage_ref, at, mode, wa, wc, right_ref, left_ref):
    n = stage_ref.shape[1]
    ra, ia, rb, ib = sided(stage_ref[rows(at * n, n)], stage_ref[rows((at + 1) * n, n)], right_ref[mode], left_ref[mode])
    return wa * (ib - ia) + wc * (rb + ra), wa * (ra - rb) + wc * (ib + ia)


def add_pair(acc_ref, at, pair):
    n = acc_ref.shape[1]
    for i in range(2):
        where = rows(at + i * n, n)
        acc_ref[where] = acc_ref[where] + pair[i]


def part_of(parts, s):
    size = parts[0].shape[0] // (2 * parts[0].shape[1])
    return parts[s // size], 2 * (s % size)


def send_kernel(sender, slots, group, modes, sum_parts, pick_parts, near_ref, right_ref, left_ref, *refs):
    acc_ref, stage_ref, list_ref, tab, sem_ref = refs[-5:]
    tabs_ref = refs[-6]
    n = acc_ref.shape[1]
    outs = refs[-6 - sum_parts - pick_parts : -6]
    sums, picks = outs[:sum_parts], outs[sum_parts:]
    groups = Layout(refs[: -6 - sum_parts - pick_parts], slots, group)

    @pl.when(odd_depth() == sender)
    def _():
        pull([groups.table(k) for k in range(group)] + [narrow(near_ref)], tab, sem_ref)
        for k in range(group):
            groups.copy_table(k, tabs_ref, k)
        acc_ref[...] = jnp.zeros_like(acc_ref)
        for s in range(slots):
            pick, at = part_of(picks, s)
            groups.fetch(parent_of(tab, group * slots + s, slots, group), pick, at)

        def collect(c, count):
            mine = parent_of(tab, c, slots, group) < slots

            @pl.when(mine)
            def _():
                list_ref[count] = c

            return count + mine.astype(jnp.int32)

        count = lax.fori_loop(0, group * slots, collect, jnp.int32(0))

        @pl.loop(0, lax.div(count + slots - 1, slots))
        def _(batch):
            children = []
            for u in range(slots):
                place = batch * slots + u
                c = list_ref[jnp.minimum(place, count - 1)]
                groups.fetch(c, stage_ref, 2 * u)
                children.append((c, jnp.where(place < count, entry(tab, WEIGHT, c, slots), 0.0)))
            terms = [
                child_pair(stage_ref, 2 * u, operator_of(tab, c, slots, modes), weight, right_ref, left_ref)
                for u, (c, weight) in enumerate(children)
            ]
            for (c, _), pair in zip(children, terms):
                add_pair(acc_ref, 2 * parent_of(tab, c, slots, group) * n, pair)

        for s in range(slots):
            part, at = part_of(sums, s)
            part[rows(at * n, n, 2)] = acc_ref[rows(2 * s * n, n, 2)]


def join_kernel(receiver, slots, modes, sum_parts, pick_parts, own_ref, right_ref, left_ref, *refs):
    out_ref, tab, sem_ref = refs[-3:]
    picks = refs[-3 - pick_parts : -3]
    sums = refs[-3 - pick_parts - sum_parts : -3 - pick_parts]
    frees = refs[: -3 - pick_parts - sum_parts]
    n = frees[0].shape[1]
    final = len(frees) > 1

    @pl.when(odd_depth() == receiver)
    def _():
        pull([narrow(own_ref)], tab, sem_ref)
        terms = []
        for s in range(slots):
            pick, at = part_of(picks, s)
            wa, wc = tab[0, WEIGHT_A, s], tab[0, WEIGHT_C, s]
            terms.append(parent_pair(pick, at, operator_of(tab, s, slots, modes), wa, wc, right_ref, left_ref))
        for s in range(slots):
            scale = tab[0, LIVE, s] * couple_step
            part, at = part_of(sums, s)
            for i in range(2):
                here = rows((2 * s + i) * n, n)
                out_ref[here] = frees[0][here] + scale * (part[rows((at + i) * n, n)] + terms[s][i])
        if not final:
            out_ref[pl.ds(2 * slots * n, ROWS)] = own_ref[...]

    if final:

        @pl.when(odd_depth() != receiver)
        def _():
            out_ref[...] = frees[1][...]


def side_kernel(side, receiver, slots, group, modes, base_count, group_count, tab_count, right_ref, left_ref, *refs):
    stage_ref, tab, sem_ref = refs[-3:]
    bases = refs[:base_count]
    groups = Layout(refs[base_count : base_count + group_count], slots, group)
    tab_refs = refs[base_count + group_count : base_count + group_count + tab_count]
    outs = refs[base_count + group_count + tab_count : -3]
    second = base_count == 1
    n = stage_ref.shape[1]
    size = 2 * slots * n
    gathered = Layout(tab_refs, slots, group) if tab_count > 1 else None
    own_tables = [gathered.table(k) if gathered else tab_refs[0].at[k, pl.ds(0, ROWS), pl.ds(0, LANES)] for k in range(group)]
    held = group // len(outs) if second else group
    stride = size + ROWS if second else size

    def spot(k):
        return outs[k // held], (k % held) * stride

    @pl.when(odd_depth() == receiver)
    def _():
        below = [groups.table(k) for k in range(group)] if side == "children" else []
        pull(own_tables + below, tab, sem_ref)
        for k in range(group):
            ref, base = spot(k)
            ref[pl.ds(base, size)] = bases[0][pl.ds(k * size, size)] if second else bases[k][...]
            if second:
                ref[pl.ds(base + size, ROWS)] = tab_refs[0][k]
            elif gathered:
                gathered.copy_table(k, outs[1], k)
            else:
                outs[1][k] = tab_refs[0][k]

        def add(index, pair):
            if not second:
                add_pair(outs[0], 2 * index * n, pair)
                return
            for half, ref in enumerate(outs):
                local = index - half * held * slots
                at = lax.div(local, slots) * stride + lax.rem(local, slots) * (2 * n)

                @pl.when(jnp.logical_and(local >= 0, local < held * slots))
                def _():
                    add_pair(ref, at, pair)

        @pl.loop(0, group)
        def _(k):
            at = k * slots
            targets, terms = [], []
            for s in range(slots):
                c = at + s
                groups.fetch(c if side == "children" else parent_of(tab, c, slots, group), stage_ref, 2 * s)
            for s in range(slots):
                c = at + s
                if side == "children":
                    b = c + group * slots
                    target = parent_of(tab, b, slots, group)
                    weight = entry(tab, WEIGHT, b, slots) * (entry(tab, LIVE, target, slots) * couple_step)
                    mode = operator_of(tab, b, slots, modes) - group * modes
                    terms.append(child_pair(stage_ref, 2 * s, mode, weight, right_ref, left_ref))
                else:
                    target = c
                    scale = entry(tab, LIVE, c, slots) * couple_step
                    wa, wc = entry(tab, WEIGHT_A, c, slots) * scale, entry(tab, WEIGHT_C, c, slots) * scale
                    mode = operator_of(tab, c, slots, modes)
                    terms.append(parent_pair(stage_ref, 2 * s, mode, wa, wc, right_ref, left_ref))
                targets.append(target)
            for target, pair in zip(targets, terms):
                add(target, pair)


def call(kernel, out_shapes, limit, args, smem=0, us=1.0, scratch=()):
    specs = [pl.BlockSpec(memory_space=SMEM)] * smem
    specs += [pl.BlockSpec(memory_space=VMEM)] * (len(args) - smem)
    return pl.pallas_call(
        kernel,
        out_shape=out_shapes,
        in_specs=specs,
        out_specs=jax.tree.map(lambda _: pl.BlockSpec(memory_space=VMEM), out_shapes),
        scratch_shapes=scratch,
        compiler_params=pltpu.CompilerParams(vmem_limit_bytes=limit),
        cost_estimate=pl.CostEstimate(flops=int(us * 1.1e9), bytes_accessed=1 << 19, transcendentals=0),
    )(*args)


def turn_order(group):
    return sorted(range(1, group), key=lambda k: abs(k - group / 2))


def has_relay(group):
    return group - 2 == 2


def shards(sizes, blocks, live_slots, parent_index, bath_mode, hamiltonian, coupling, correlation, damping, link_weight):
    depths, group = sizes
    slots, _, n, _ = blocks.shape
    modes = coupling.shape[0]
    total = group * slots
    limit = 8 * total * 2 * n * n * 4
    order = turn_order(group)
    split_hop = 2 if slots % 2 == 0 else 1
    ranks = range(group)
    relay = has_relay(group)

    def place(d, m):
        return d * group + m

    def permute(value, pairs):
        return lax.ppermute(value, AXES, pairs)

    def gather(value, parity):
        def turn(k):
            wraps = {1: group - 1, group - 1: 0}
            pairs = [
                (place(d, m), place(d, (m + k) % group))
                for d in range(parity, depths, 2)
                for m in ranks
                if not (relay and wraps.get(k) == m)
            ]
            return permute(value, pairs)

        turned = {k: turn(k) for k in order}
        groups = [value] + [turned[k] for k in range(1, group)]
        if relay:
            pairs = [
                (place(d, source), place(d, target))
                for d in range(parity, depths, 2)
                for source, target in ((1, 0), (group - 2, group - 1))
            ]
            groups.append(permute(turned[2], pairs))
        return groups

    def shift(value, step, parity=None, k=None):
        def sent(m):
            if not relay or k is None:
                return True
            edge = {1: 0, group - 1: group - 1}
            return m in edge.values() if k == group else edge.get(k) != m

        pairs = [
            (place(d, m), place(d + step, m))
            for d in range(depths)
            for m in ranks
            if 0 <= d + step < depths and (parity is None or d % 2 == parity) and sent(m)
        ]
        return permute(value, pairs)

    def mats(count, tables=0):
        return jax.ShapeDtypeStruct((count * n + tables * ROWS, n), f32)

    def sds(*shape, dtype=f32):
        return jax.ShapeDtypeStruct(shape, dtype)

    plain = 2 * slots
    stage = VMEM((plain * n, n), f32)

    def tables(count):
        return [SMEM((count, ROWS, LANES), f32), pltpu.SemaphoreType.DMA((count,))]

    operator_shapes = (sds(group * modes, 3 * n, n, dtype=bf16), sds(group * modes, n, 3 * n, dtype=bf16))
    couplings = coupling.reshape(modes * n, n)

    packed, own_table = call(
        pack_kernel,
        (mats(plain + modes, 1), sds(ROWS, n)),
        PACK_LIMIT,
        (live_slots, parent_index, bath_mode, damping, link_weight, correlation, blocks.reshape(plain * n, n), couplings),
        smem=6,
    )
    first = gather(packed, 1)
    near_table = shift(own_table, -1)
    powers = call(
        powers_kernel, (sds(3 * n, ORDER * n, dtype=bf16), sds(n, 3 * ORDER * n, dtype=bf16)), limit, (hamiltonian,)
    )
    *operators_odd, raw = call(
        functools.partial(operators_kernel, slots, group, modes, None),
        (*operator_shapes, mats((group - 1) * modes)),
        limit,
        (couplings, *first),
    )

    def free(groups, k, parity, times):
        sources = [groups[k]]
        if len(groups) == group + 1 and k in (1, group - 1):
            sources.append(groups[group])
        return call(
            functools.partial(free_kernel, parity, times, slots, group, k),
            mats(plain),
            limit,
            (*powers, *sources),
            us=4.7 * times,
        )

    def send(groups, sender, sum_parts, pick_parts, operators):
        shapes = [mats(plain // sum_parts)] * sum_parts + [mats(plain // pick_parts)] * pick_parts
        outs = call(
            functools.partial(send_kernel, sender, slots, group, modes, sum_parts, pick_parts),
            [*shapes, sds(group, ROWS, n)],
            limit,
            (near_table, *operators, *groups),
            us=2,
            scratch=[stage, stage, SMEM((total,), jnp.int32), *tables(group + 1)],
        )
        return outs[:sum_parts], outs[sum_parts:-1], outs[-1]

    def join(frees, sums, picks, receiver, operators):
        return call(
            functools.partial(join_kernel, receiver, slots, modes, len(sums), len(picks)),
            mats(plain) if len(frees) > 1 else mats(plain, 1),
            limit,
            (own_table, *operators, *frees, *sums, *picks),
            scratch=tables(1),
        )

    def side(kind, bases, groups, tabs, receiver, operators):
        second = len(bases) == 1
        halves = 2 if group % 2 == 0 else 1
        return call(
            functools.partial(side_kernel, kind, receiver, slots, group, modes, len(bases), len(groups), len(tabs)),
            [mats(2 * total // halves, group // halves)] * halves if second else [mats(2 * total), sds(group, ROWS, n)],
            limit,
            (*operators, *bases, *groups, *tabs),
            us=3,
            scratch=[stage, *tables(2 * group if kind == "children" else group)],
        )

    free_even = free([packed], 0, 0, 1)
    free_odd = [free(first, k, 1, 2) for k in ranks]
    sums, picks, tabs_odd = send(first, 1, 1, split_hop, operators_odd)
    picks = [shift(value, 1, 1) for value in picks]
    sums = [shift(value, -1, 1) for value in sums]
    own_state = join([free_even], sums, picks, 0, operators_odd)

    gathered = gather(own_state, 0)
    from_below = [shift(value, -1, 0, k) for k, value in enumerate(gathered)]
    from_above = [shift(value, 1, 0, k) for k, value in enumerate(gathered)]
    free_even = [free(gathered, k, 0, 2) for k in ranks]
    states, _ = side("parents", free_odd, from_above, [tabs_odd], 1, operators_odd)
    states = side("children", [states], from_below, [tabs_odd], 1, operators_odd)

    from_above = [shift(value, 1, 1) for value in states]
    from_below = [shift(value, -1, 1) for value in states]
    passed = shift(raw, -1, 1)
    operators_even = call(
        functools.partial(operators_kernel, slots, group, modes, 0), operator_shapes, limit, (couplings, passed)
    )
    last_odd = free(states[:1], 0, 1, 2)
    states, tabs_even = side("children", free_even, from_below, gathered, 0, operators_even)
    states = side("parents", [states], from_above, [tabs_even], 0, operators_even)

    sums, picks, _ = send(states, 0, split_hop, 1, operators_even)
    sums = [shift(value, -1, 0) for value in sums]
    picks = [shift(value, 1, 0) for value in picks]
    last_even = free(states[:1], 0, 0, 1)
    return join([last_odd, last_even], sums, picks, 1, operators_odd).reshape(blocks.shape)


def solution(mesh):
    sizes = (mesh.shape["depth"], mesh.shape["mode"])

    def whole(*args):
        return shards(sizes, *args)

    return jax.shard_map(
        whole,
        mesh=mesh,
        in_specs=(
            P(("depth", "mode"), None, None, None),
            P(("depth", "mode")),
            P(("depth", "mode")),
            P(("depth", "mode")),
            P(),
            P("mode", None, None),
            P("mode", None),
            P(("depth", "mode")),
            P(("depth", "mode")),
        ),
        out_specs=P(("depth", "mode"), None, None, None),
        check_vma=False,
    )
```

```python
import functools
import math
import jax
import jax.numpy as jnp
from jax import lax
from jax.experimental import pallas as pl
from jax.experimental.pallas import tpu as pltpu
from jax.sharding import PartitionSpec as P

SUBSTEPS = 2
ORDER = 4
substep = 0.7
couple_step = 0.2

AXES = ("depth", "mode")
VMEM = pltpu.VMEM
SMEM = pltpu.SMEM
bf16 = jnp.bfloat16
f32 = jnp.float32

PARENT, MODE, LIVE, FACTOR, WEIGHT, WEIGHT_A, WEIGHT_C = range(7)
ROWS, LANES = 8, 128
PACK_LIMIT = 56 << 20


def split(value):
    high = value.astype(bf16)
    return high, (value - high.astype(f32)).astype(bf16)


def stack_rows(value):
    high, low = split(value)
    return jnp.concatenate([high, high, low], axis=0)


def stack_cols(value):
    high, low = split(value)
    return jnp.concatenate([high, low, high], axis=1)


def dot(first, second):
    return jnp.dot(first, second, preferred_element_type=f32)


def exact(first, second):
    return jnp.dot(first, second, preferred_element_type=f32, precision=lax.Precision.HIGHEST)


def odd_depth():
    return lax.rem(lax.axis_index("depth"), 2)


def rows(at, n, count=1):
    if not isinstance(at, int):
        at = pl.multiple_of(at, ROWS)
    return pl.ds(at, count * n)


def pack_kernel(live_ref, parent_ref, mode_ref, damping_ref, weight_ref, corr_ref, blocks_ref, coupling_ref, out_ref, table_ref):
    slots, n = live_ref.shape[0], blocks_ref.shape[1]
    size = blocks_ref.shape[0]
    out_ref[pl.ds(0, size)] = blocks_ref[...]
    out_ref[pl.ds(size + ROWS, coupling_ref.shape[0])] = coupling_ref[...]
    row = lax.broadcasted_iota(jnp.int32, (ROWS, n), 0)
    lane = lax.broadcasted_iota(jnp.int32, (ROWS, n), 1)
    table = jnp.zeros((ROWS, n), f32)
    first_mode = lax.axis_index("mode") * corr_ref.shape[0]
    for s in range(slots):
        mode = mode_ref[s] - first_mode
        live = live_ref[s].astype(f32)
        weight = weight_ref[s]
        values = {
            PARENT: parent_ref[s].astype(f32),
            MODE: mode.astype(f32),
            LIVE: live,
            FACTOR: damping_ref[s] * (-SUBSTEPS * substep),
            WEIGHT: weight * live,
            WEIGHT_A: weight * corr_ref[mode, 0],
            WEIGHT_C: weight * corr_ref[mode, 1],
        }
        for at, value in values.items():
            table = jnp.where(jnp.logical_and(row == at, lane == s), value, table)
    live_row = table[LIVE : LIVE + 1]
    table = jnp.where(row == FACTOR, live_row * jnp.exp(table), table)
    table_ref[...] = table
    out_ref[pl.ds(size, ROWS)] = table


def powers_kernel(ham_ref, right_ref, left_ref):
    n = ham_ref.shape[0]
    ham = (ham_ref[...] + ham_ref[...].T) * 0.5
    power = ham
    for k in range(1, ORDER + 1):
        if k > 1:
            power = exact(power, ham)
        scaled = power * (substep**k / math.factorial(k))
        right_ref[:, (k - 1) * n : k * n] = stack_rows(scaled)
        left_ref[:, (k - 1) * 3 * n : k * 3 * n] = stack_cols(scaled)


class Layout:
    def __init__(self, refs, slots, group):
        self.refs, self.slots, self.group = refs, slots, group
        self.n = refs[0].shape[1]
        self.held = group // len(refs)
        self.size = 2 * slots * self.n
        self.stride = self.size + ROWS

    def base(self, k):
        return self.refs[k // self.held], (k % self.held) * self.stride

    def table(self, k):
        ref, base = self.base(k)
        return ref.at[pl.ds(base + self.size, ROWS), pl.ds(0, LANES)]

    def copy_table(self, k, target_ref, at):
        ref, base = self.base(k)
        target_ref[at] = ref[pl.ds(base + self.size, ROWS)]

    def fetch(self, index, stage_ref, at):
        for k in range(self.group):
            ref, base = self.base(k)
            local = index - k * self.slots

            @pl.when(jnp.logical_and(local >= 0, local < self.slots))
            def _():
                stage_ref[rows(at * self.n, self.n, 2)] = ref[rows(base + 2 * local * self.n, self.n, 2)]


def pull(sources, smem_ref, sem_ref):
    copies = [pltpu.make_async_copy(ref, smem_ref.at[i], sem_ref.at[i]) for i, ref in enumerate(sources)]
    for copy in copies:
        copy.start()
    for copy in copies:
        copy.wait()


def narrow(ref):
    return ref.at[pl.ds(0, ROWS), pl.ds(0, LANES)]


def operators_kernel(slots, group, modes, parity, own_ref, *refs):
    outs = refs[-2 - (parity is None) :]
    sources = refs[: -len(outs)]
    right_ref, left_ref = outs[0], outs[1]
    n = own_ref.shape[1]

    def put(at, value):
        sym = (value + value.T) * 0.5
        right_ref[at] = stack_rows(sym)
        left_ref[at] = stack_cols(sym)

    def own():
        for i in range(modes):
            put(i, own_ref[rows(i * n, n)])

    if parity is None:
        own()
        groups = Layout(sources, slots, group)
        for k in range(1, group):
            ref, base = groups.base(k)
            for i in range(modes):
                value = ref[rows(base + groups.stride + i * n, n)]
                put(k * modes + i, value)
                outs[2][rows(((k - 1) * modes + i) * n, n)] = value
    else:

        @pl.when(odd_depth() == parity)
        def _():
            own()
            for at in range(modes, group * modes):
                put(at, sources[0][rows((at - modes) * n, n)])


def taylor(real, imag, right, left):
    n = real.shape[0]
    out = dot(stack_cols(jnp.concatenate([real, imag], axis=0)), right)
    rp = [out[:n, k * n : (k + 1) * n] for k in range(ORDER)]
    ip = [out[n:, k * n : (k + 1) * n] for k in range(ORDER)]
    u_real, u_imag = real, imag
    stacked = [None] * ORDER
    for k in range(ORDER + 1):
        if k:
            turn = k % 4
            if turn == 1:
                u_real, u_imag = u_real - ip[k - 1], u_imag + rp[k - 1]
            elif turn == 2:
                u_real, u_imag = u_real - rp[k - 1], u_imag - ip[k - 1]
            elif turn == 3:
                u_real, u_imag = u_real + ip[k - 1], u_imag - rp[k - 1]
            else:
                u_real, u_imag = u_real + rp[k - 1], u_imag + ip[k - 1]
        j = ORDER - k
        if j:
            turn = j % 4
            if turn == 1:
                pair = (u_imag, -u_real)
            elif turn == 2:
                pair = (-u_real, -u_imag)
            elif turn == 3:
                pair = (-u_imag, u_real)
            else:
                pair = (u_real, u_imag)
            stacked[j - 1] = stack_rows(jnp.concatenate(pair, axis=1))
    done = dot(left, jnp.concatenate(stacked, axis=0))
    return u_real + done[:, :n], u_imag + done[:, n:]


def free_kernel(run_parity, times, slots, first, states_ref, right_ref, left_ref, out_ref):
    n = out_ref.shape[1]
    count = out_ref.shape[0] // (2 * n)
    pair = 2 if count % 2 == 0 else 1

    @pl.when(odd_depth() == run_parity)
    def _():
        right, left = right_ref[...], left_ref[...]
        out_ref[...] = states_ref[pl.ds(2 * first * n, 2 * count * n)]

        @pl.loop(0, count // pair)
        def _(step):
            @pl.loop(0, times * SUBSTEPS)
            def _(turn):
                at = [(rows(2 * s * n, n), rows((2 * s + 1) * n, n)) for s in [step * pair + u for u in range(pair)]]
                done = [taylor(out_ref[r], out_ref[i], right, left) for r, i in at]
                for (r, i), (real, imag) in zip(at, done):
                    out_ref[r] = real
                    out_ref[i] = imag

        factors = states_ref[pl.ds(2 * slots * n, ROWS)][FACTOR : FACTOR + 1]
        for s in range(count):
            scale = factors[:, first + s : first + s + 1] ** times
            at = rows(2 * s * n, n, 2)
            out_ref[at] = out_ref[at] * scale


def sided(real, imag, right, left):
    n = real.shape[0]
    after = dot(stack_cols(jnp.concatenate([real, imag], axis=0)), right)
    before = dot(left, stack_rows(jnp.concatenate([real, imag], axis=1)))
    return after[:n], after[n:], before[:, :n], before[:, n:]


def entry(tab, row, c, slots):
    if isinstance(c, int):
        return tab[c // slots, row, c % slots]
    return tab[lax.div(c, slots), row, lax.rem(c, slots)]


def operator_of(tab, c, slots, modes):
    back = c // slots if isinstance(c, int) else lax.div(c, slots)
    return back * modes + entry(tab, MODE, c, slots).astype(jnp.int32)


def parent_of(tab, c, slots):
    parent = entry(tab, PARENT, c, slots).astype(jnp.int32)
    back = lax.bitwise_xor(lax.axis_index("mode"), lax.div(parent, slots))
    return back * slots + lax.rem(parent, slots)


def child_pair(stage_ref, at, mode, weight, right_ref, left_ref):
    n = stage_ref.shape[1]
    ra, ia, rb, ib = sided(stage_ref[rows(at * n, n)], stage_ref[rows((at + 1) * n, n)], right_ref[mode], left_ref[mode])
    return weight * (ib - ia), weight * (ra - rb)


def parent_pair(stage_ref, at, mode, wa, wc, right_ref, left_ref):
    n = stage_ref.shape[1]
    ra, ia, rb, ib = sided(stage_ref[rows(at * n, n)], stage_ref[rows((at + 1) * n, n)], right_ref[mode], left_ref[mode])
    return wa * (ib - ia) + wc * (rb + ra), wa * (ra - rb) + wc * (ib + ia)


def add_pair(acc_ref, at, pair):
    n = acc_ref.shape[1]
    for i in range(2):
        where = rows(at + i * n, n)
        acc_ref[where] = acc_ref[where] + pair[i]


def part_of(parts, s):
    size = parts[0].shape[0] // (2 * parts[0].shape[1])
    return parts[s // size], 2 * (s % size)


def send_kernel(sender, slots, group, modes, sum_parts, pick_parts, near_ref, right_ref, left_ref, *refs):
    acc_ref, stage_ref, list_ref, tab, sem_ref = refs[-5:]
    tabs_ref = refs[-6]
    n = acc_ref.shape[1]
    outs = refs[-6 - sum_parts - pick_parts : -6]
    sums, picks = outs[:sum_parts], outs[sum_parts:]
    groups = Layout(refs[: -6 - sum_parts - pick_parts], slots, group)

    @pl.when(odd_depth() == sender)
    def _():
        pull([groups.table(k) for k in range(group)] + [narrow(near_ref)], tab, sem_ref)
        for k in range(group):
            groups.copy_table(k, tabs_ref, k)
        acc_ref[...] = jnp.zeros_like(acc_ref)
        for s in range(slots):
            pick, at = part_of(picks, s)
            groups.fetch(parent_of(tab, group * slots + s, slots), pick, at)

        def collect(c, count):
            mine = parent_of(tab, c, slots) < slots

            @pl.when(mine)
            def _():
                list_ref[count] = c

            return count + mine.astype(jnp.int32)

        count = lax.fori_loop(0, group * slots, collect, jnp.int32(0))

        @pl.loop(0, lax.div(count + slots - 1, slots))
        def _(batch):
            children = []
            for u in range(slots):
                place = batch * slots + u
                c = list_ref[jnp.minimum(place, count - 1)]
                groups.fetch(c, stage_ref, 2 * u)
                children.append((c, jnp.where(place < count, entry(tab, WEIGHT, c, slots), 0.0)))
            terms = [
                child_pair(stage_ref, 2 * u, operator_of(tab, c, slots, modes), weight, right_ref, left_ref)
                for u, (c, weight) in enumerate(children)
            ]
            for (c, _), pair in zip(children, terms):
                add_pair(acc_ref, 2 * parent_of(tab, c, slots) * n, pair)

        for s in range(slots):
            part, at = part_of(sums, s)
            part[rows(at * n, n, 2)] = acc_ref[rows(2 * s * n, n, 2)]


def join_kernel(receiver, slots, modes, sum_parts, pick_parts, own_ref, right_ref, left_ref, *refs):
    out_ref, tab, sem_ref = refs[-3:]
    picks = refs[-3 - pick_parts : -3]
    sums = refs[-3 - pick_parts - sum_parts : -3 - pick_parts]
    frees = refs[: -3 - pick_parts - sum_parts]
    n = frees[0].shape[1]
    final = len(frees) > 1

    @pl.when(odd_depth() == receiver)
    def _():
        pull([narrow(own_ref)], tab, sem_ref)
        terms = []
        for s in range(slots):
            pick, at = part_of(picks, s)
            wa, wc = tab[0, WEIGHT_A, s], tab[0, WEIGHT_C, s]
            terms.append(parent_pair(pick, at, operator_of(tab, s, slots, modes), wa, wc, right_ref, left_ref))
        for s in range(slots):
            scale = tab[0, LIVE, s] * couple_step
            part, at = part_of(sums, s)
            for i in range(2):
                here = rows((2 * s + i) * n, n)
                out_ref[here] = frees[0][here] + scale * (part[rows((at + i) * n, n)] + terms[s][i])
        if not final:
            out_ref[pl.ds(2 * slots * n, ROWS)] = own_ref[...]

    if final:

        @pl.when(odd_depth() != receiver)
        def _():
            out_ref[...] = frees[1][...]


def side_kernel(side, receiver, slots, group, modes, span, base_count, group_count, tab_count, right_ref, left_ref, *refs):
    stage_ref, tab, sem_ref = refs[-3:]
    start, count = span
    bases = refs[:base_count]
    groups = Layout(refs[base_count : base_count + group_count], slots, count)
    tab_refs = refs[base_count + group_count : base_count + group_count + tab_count]
    outs = refs[base_count + group_count + tab_count : -3]
    second = len(outs[-1].shape) == 2
    n = stage_ref.shape[1]
    size = 2 * slots * n
    gathered = Layout(tab_refs, slots, group) if tab_count > 1 else None
    own_tables = [gathered.table(k) if gathered else tab_refs[0].at[k, pl.ds(0, ROWS), pl.ds(0, LANES)] for k in range(group)]
    held = group // len(outs) if second else group
    stride = size + ROWS if second else size

    @pl.when(odd_depth() == receiver)
    def _():
        below = [groups.table(k) for k in range(count)] if side == "children" else []
        pull(own_tables + below, tab, sem_ref)
        if second:
            for k in range(group):
                ref, base = outs[k // held], (k % held) * stride
                ref[pl.ds(base, size)] = bases[0][pl.ds(k * size, size)]
                ref[pl.ds(base + size, ROWS)] = tab_refs[0][k]
        else:
            offset = 0
            for base in bases:
                outs[0][pl.ds(offset, base.shape[0])] = base[...]
                offset += base.shape[0]
            for k in range(group):
                if gathered:
                    gathered.copy_table(k, outs[1], k)
                else:
                    outs[1][k] = tab_refs[0][k]

        def add(index, pair):
            if not second:
                add_pair(outs[0], 2 * index * n, pair)
                return
            for half, ref in enumerate(outs):
                local = index - half * held * slots
                at = lax.div(local, slots) * stride + lax.rem(local, slots) * (2 * n)

                @pl.when(jnp.logical_and(local >= 0, local < held * slots))
                def _():
                    add_pair(ref, at, pair)

        @pl.loop(0, count)
        def _(k):
            at = k * slots
            targets, terms = [], []
            for s in range(slots):
                c = at + s
                groups.fetch(c if side == "children" else parent_of(tab, c, slots), stage_ref, 2 * s)
            for s in range(slots):
                c = at + s
                if side == "children":
                    b = c + group * slots
                    target = parent_of(tab, b, slots)
                    weight = entry(tab, WEIGHT, b, slots) * (entry(tab, LIVE, target, slots) * couple_step)
                    mode = operator_of(tab, b, slots, modes) + (start - group) * modes
                    terms.append(child_pair(stage_ref, 2 * s, mode, weight, right_ref, left_ref))
                else:
                    target = c
                    scale = entry(tab, LIVE, c, slots) * couple_step
                    wa, wc = entry(tab, WEIGHT_A, c, slots) * scale, entry(tab, WEIGHT_C, c, slots) * scale
                    mode = operator_of(tab, c, slots, modes)
                    terms.append(parent_pair(stage_ref, 2 * s, mode, wa, wc, right_ref, left_ref))
                targets.append(target)
            for target, pair in zip(targets, terms):
                add(target, pair)


def call(kernel, out_shapes, limit, args, smem=0, us=1.0, scratch=()):
    specs = [pl.BlockSpec(memory_space=SMEM)] * smem
    specs += [pl.BlockSpec(memory_space=VMEM)] * (len(args) - smem)
    return pl.pallas_call(
        kernel,
        out_shape=out_shapes,
        in_specs=specs,
        out_specs=jax.tree.map(lambda _: pl.BlockSpec(memory_space=VMEM), out_shapes),
        scratch_shapes=scratch,
        compiler_params=pltpu.CompilerParams(vmem_limit_bytes=limit),
        cost_estimate=pl.CostEstimate(flops=int(us * 1.1e9), bytes_accessed=1 << 19, transcendentals=0),
    )(*args)


def turn_order(group):
    return sorted(range(1, group), key=lambda k: (bin(k).count("1"), -k))


def shards(sizes, blocks, live_slots, parent_index, bath_mode, hamiltonian, coupling, correlation, damping, link_weight):
    depths, group = sizes
    slots, _, n, _ = blocks.shape
    modes = coupling.shape[0]
    total = group * slots
    limit = 8 * total * 2 * n * n * 4
    order = turn_order(group)
    split_hop = 2 if slots % 2 == 0 else 1
    ranks = range(group)

    def place(d, m):
        return d * group + m

    def permute(value, pairs):
        return lax.ppermute(value, AXES, pairs)

    def gather(value, parity):
        held = {0: value}
        for k in order:
            step = k & -k
            pairs = [(place(d, m), place(d, m ^ step)) for d in range(parity, depths, 2) for m in ranks]
            held[k] = permute(held[k ^ step], pairs)
        return [held[k] for k in ranks]

    def shift(value, step, parity=None):
        pairs = [
            (place(d, m), place(d + step, m))
            for d in range(depths)
            for m in ranks
            if 0 <= d + step < depths and (parity is None or d % 2 == parity)
        ]
        return permute(value, pairs)

    def mats(count, tables=0):
        return jax.ShapeDtypeStruct((count * n + tables * ROWS, n), f32)

    def sds(*shape, dtype=f32):
        return jax.ShapeDtypeStruct(shape, dtype)

    plain = 2 * slots
    stage = VMEM((plain * n, n), f32)

    def tables(count):
        return [SMEM((count, ROWS, LANES), f32), pltpu.SemaphoreType.DMA((count,))]

    operator_shapes = (sds(group * modes, 3 * n, n, dtype=bf16), sds(group * modes, n, 3 * n, dtype=bf16))
    couplings = coupling.reshape(modes * n, n)

    packed, own_table = call(
        pack_kernel,
        (mats(plain + modes, 1), sds(ROWS, n)),
        PACK_LIMIT,
        (live_slots, parent_index, bath_mode, damping, link_weight, correlation, blocks.reshape(plain * n, n), couplings),
        smem=6,
    )
    first = gather(packed, 1)
    near_table = shift(own_table, -1)
    powers = call(
        powers_kernel, (sds(3 * n, ORDER * n, dtype=bf16), sds(n, 3 * ORDER * n, dtype=bf16)), limit, (hamiltonian,)
    )
    *operators_odd, raw = call(
        functools.partial(operators_kernel, slots, group, modes, None),
        (*operator_shapes, mats((group - 1) * modes)),
        limit,
        (couplings, *first),
    )

    def free(states, parity, times, part=0, parts=1):
        count = slots // parts
        return call(
            functools.partial(free_kernel, parity, times, slots, part * count),
            mats(2 * count),
            limit,
            (states, *powers),
            us=4.5 * times / parts,
        )

    def free_parts(states, parity, times):
        return [free(states, parity, times, part, split_hop) for part in range(split_hop)]

    def send(groups, sender, sum_parts, pick_parts, operators):
        shapes = [mats(plain // sum_parts)] * sum_parts + [mats(plain // pick_parts)] * pick_parts
        outs = call(
            functools.partial(send_kernel, sender, slots, group, modes, sum_parts, pick_parts),
            [*shapes, sds(group, ROWS, n)],
            limit,
            (near_table, *operators, *groups),
            us=2,
            scratch=[stage, stage, SMEM((total,), jnp.int32), *tables(group + 1)],
        )
        return outs[:sum_parts], outs[sum_parts:-1], outs[-1]

    def join(frees, sums, picks, receiver, operators):
        return call(
            functools.partial(join_kernel, receiver, slots, modes, len(sums), len(picks)),
            mats(plain) if len(frees) > 1 else mats(plain, 1),
            limit,
            (own_table, *operators, *frees, *sums, *picks),
            scratch=tables(1),
        )

    def side(kind, bases, groups, tabs, receiver, operators, second=False, span=None):
        halves = 2 if group % 2 == 0 else 1
        span = (0, group) if span is None else span
        return call(
            functools.partial(side_kernel, kind, receiver, slots, group, modes, span, len(bases), len(groups), len(tabs)),
            [mats(2 * total // halves, group // halves)] * halves if second else [mats(2 * total), sds(group, ROWS, n)],
            limit,
            (*operators, *bases, *groups, *tabs),
            us=3,
            scratch=[stage, *tables(group + (span[1] if kind == "children" else 0))],
        )

    free_even = free(packed, 0, 1)
    free_odd = [part for k in ranks for part in free_parts(first[k], 1, 2)]
    sums, picks, tabs_odd = send(first, 1, 1, split_hop, operators_odd)
    picks = [shift(value, 1, 1) for value in picks]
    sums = [shift(value, -1, 1) for value in sums]
    own_state = join([free_even], sums, picks, 0, operators_odd)

    gathered = gather(own_state, 0)
    from_below = [shift(value, -1, 0) for value in gathered]
    from_above = [shift(value, 1, 0) for value in gathered]
    free_even = [part for k in ranks for part in free_parts(gathered[k], 0, 2)]
    states, _ = side("parents", free_odd, from_above, [tabs_odd], 1, operators_odd)
    ready = group - 1
    states, _ = side("children", [states], from_below[:ready], [tabs_odd], 1, operators_odd, span=(0, ready))
    states = side("children", [states], from_below[ready:], [tabs_odd], 1, operators_odd, second=True, span=(ready, 1))

    from_above = [shift(value, 1, 1) for value in states]
    from_below = [shift(value, -1, 1) for value in states]
    passed = shift(raw, -1, 1)
    operators_even = call(
        functools.partial(operators_kernel, slots, group, modes, 0), operator_shapes, limit, (couplings, passed)
    )
    last_odd = free(states[0], 1, 2)
    states, tabs_even = side("children", free_even, from_below, gathered, 0, operators_even)
    states = side("parents", [states], from_above, [tabs_even], 0, operators_even, second=True)

    sums, picks, _ = send(states, 0, split_hop, 1, operators_even)
    sums = [shift(value, -1, 0) for value in sums]
    picks = [shift(value, 1, 0) for value in picks]
    last_even = free(states[0], 0, 1)
    return join([last_odd, last_even], sums, picks, 1, operators_odd).reshape(blocks.shape)


def solution(mesh):
    sizes = (mesh.shape["depth"], mesh.shape["mode"])

    def whole(*args):
        return shards(sizes, *args)

    return jax.shard_map(
        whole,
        mesh=mesh,
        in_specs=(
            P(("depth", "mode"), None, None, None),
            P(("depth", "mode")),
            P(("depth", "mode")),
            P(("depth", "mode")),
            P(),
            P("mode", None, None),
            P("mode", None),
            P(("depth", "mode")),
            P(("depth", "mode")),
        ),
        out_specs=P(("depth", "mode"), None, None, None),
        check_vma=False,
    )
```

```python
import functools
import math
import jax
import jax.numpy as jnp
from jax import lax
from jax.experimental import pallas as pl
from jax.experimental.pallas import tpu as pltpu
from jax.sharding import PartitionSpec as P

SUBSTEPS = 2
ORDER = 4
substep = 0.7
couple_step = 0.2

AXES = ("depth", "mode")
VMEM = pltpu.VMEM
SMEM = pltpu.SMEM
bf16 = jnp.bfloat16
f32 = jnp.float32

PARENT, MODE, LIVE, FACTOR, WEIGHT, WEIGHT_A, WEIGHT_C = range(7)
ROWS, LANES = 8, 128
PACK_LIMIT = 56 << 20


def split(value):
    high = value.astype(bf16)
    return high, (value - high.astype(f32)).astype(bf16)


def stack_rows(value):
    high, low = split(value)
    return jnp.concatenate([high, high, low], axis=0)


def stack_cols(value):
    high, low = split(value)
    return jnp.concatenate([high, low, high], axis=1)


def dot(first, second):
    return jnp.dot(first, second, preferred_element_type=f32)


def exact(first, second):
    return jnp.dot(first, second, preferred_element_type=f32, precision=lax.Precision.HIGHEST)


def odd_depth():
    return lax.rem(lax.axis_index("depth"), 2)


def rows(at, n, count=1):
    if not isinstance(at, int):
        at = pl.multiple_of(at, ROWS)
    return pl.ds(at, count * n)


def pack_kernel(live_ref, parent_ref, mode_ref, damping_ref, weight_ref, corr_ref, blocks_ref, coupling_ref, out_ref, table_ref):
    slots, n = live_ref.shape[0], blocks_ref.shape[1]
    size = blocks_ref.shape[0]
    out_ref[pl.ds(0, size)] = blocks_ref[...]
    out_ref[pl.ds(size + ROWS, coupling_ref.shape[0])] = coupling_ref[...]
    row = lax.broadcasted_iota(jnp.int32, (ROWS, n), 0)
    lane = lax.broadcasted_iota(jnp.int32, (ROWS, n), 1)
    table = jnp.zeros((ROWS, n), f32)
    first_mode = lax.axis_index("mode") * corr_ref.shape[0]
    for s in range(slots):
        mode = mode_ref[s] - first_mode
        live = live_ref[s].astype(f32)
        weight = weight_ref[s]
        values = {
            PARENT: parent_ref[s].astype(f32),
            MODE: mode.astype(f32),
            LIVE: live,
            FACTOR: damping_ref[s] * (-SUBSTEPS * substep),
            WEIGHT: weight * live,
            WEIGHT_A: weight * corr_ref[mode, 0],
            WEIGHT_C: weight * corr_ref[mode, 1],
        }
        for at, value in values.items():
            table = jnp.where(jnp.logical_and(row == at, lane == s), value, table)
    live_row = table[LIVE : LIVE + 1]
    table = jnp.where(row == FACTOR, live_row * jnp.exp(table), table)
    table_ref[...] = table
    out_ref[pl.ds(size, ROWS)] = table


def powers_kernel(ham_ref, right_ref, left_ref):
    n = ham_ref.shape[0]
    ham = (ham_ref[...] + ham_ref[...].T) * 0.5
    power = ham
    for k in range(1, ORDER + 1):
        if k > 1:
            power = exact(power, ham)
        scaled = power * (substep**k / math.factorial(k))
        right_ref[:, (k - 1) * n : k * n] = stack_rows(scaled)
        left_ref[:, (k - 1) * 3 * n : k * 3 * n] = stack_cols(scaled)


class Layout:
    def __init__(self, refs, slots, group):
        self.refs, self.slots, self.group = refs, slots, group
        self.n = refs[0].shape[1]
        self.held = group // len(refs)
        self.size = 2 * slots * self.n
        self.stride = self.size + ROWS

    def base(self, k):
        return self.refs[k // self.held], (k % self.held) * self.stride

    def table(self, k):
        ref, base = self.base(k)
        return ref.at[pl.ds(base + self.size, ROWS), pl.ds(0, LANES)]

    def copy_table(self, k, target_ref, at):
        ref, base = self.base(k)
        target_ref[at] = ref[pl.ds(base + self.size, ROWS)]

    def fetch(self, index, stage_ref, at):
        for k in range(self.group):
            ref, base = self.base(k)
            local = index - k * self.slots

            @pl.when(jnp.logical_and(local >= 0, local < self.slots))
            def _():
                stage_ref[rows(at * self.n, self.n, 2)] = ref[rows(base + 2 * local * self.n, self.n, 2)]


def pull(sources, smem_ref, sem_ref):
    copies = [pltpu.make_async_copy(ref, smem_ref.at[i], sem_ref.at[i]) for i, ref in enumerate(sources)]
    for copy in copies:
        copy.start()
    for copy in copies:
        copy.wait()


def narrow(ref):
    return ref.at[pl.ds(0, ROWS), pl.ds(0, LANES)]


def operators_kernel(slots, group, modes, parity, own_ref, *refs):
    outs = refs[-2 - (parity is None) :]
    sources = refs[: -len(outs)]
    right_ref, left_ref = outs[0], outs[1]
    n = own_ref.shape[1]

    def put(at, value):
        sym = (value + value.T) * 0.5
        right_ref[at] = stack_rows(sym)
        left_ref[at] = stack_cols(sym)

    def own():
        for i in range(modes):
            put(i, own_ref[rows(i * n, n)])

    if parity is None:
        own()
        groups = Layout(sources, slots, group)
        for k in range(1, group):
            ref, base = groups.base(k)
            for i in range(modes):
                value = ref[rows(base + groups.stride + i * n, n)]
                put(k * modes + i, value)
                outs[2][rows(((k - 1) * modes + i) * n, n)] = value
    else:

        @pl.when(odd_depth() == parity)
        def _():
            own()
            for at in range(modes, group * modes):
                put(at, sources[0][rows((at - modes) * n, n)])


def taylor(real, imag, right, left):
    n = real.shape[0]
    out = dot(stack_cols(jnp.concatenate([real, imag], axis=0)), right)
    rp = [out[:n, k * n : (k + 1) * n] for k in range(ORDER)]
    ip = [out[n:, k * n : (k + 1) * n] for k in range(ORDER)]
    u_real, u_imag = real, imag
    stacked = [None] * ORDER
    for k in range(ORDER + 1):
        if k:
            turn = k % 4
            if turn == 1:
                u_real, u_imag = u_real - ip[k - 1], u_imag + rp[k - 1]
            elif turn == 2:
                u_real, u_imag = u_real - rp[k - 1], u_imag - ip[k - 1]
            elif turn == 3:
                u_real, u_imag = u_real + ip[k - 1], u_imag - rp[k - 1]
            else:
                u_real, u_imag = u_real + rp[k - 1], u_imag + ip[k - 1]
        j = ORDER - k
        if j:
            turn = j % 4
            if turn == 1:
                pair = (u_imag, -u_real)
            elif turn == 2:
                pair = (-u_real, -u_imag)
            elif turn == 3:
                pair = (-u_imag, u_real)
            else:
                pair = (u_real, u_imag)
            stacked[j - 1] = stack_rows(jnp.concatenate(pair, axis=1))
    done = dot(left, jnp.concatenate(stacked, axis=0))
    return u_real + done[:, :n], u_imag + done[:, n:]


def free_kernel(run_parity, times, slots, first, states_ref, right_ref, left_ref, out_ref):
    n = out_ref.shape[1]
    count = out_ref.shape[0] // (2 * n)
    pair = 2 if count % 2 == 0 else 1

    @pl.when(odd_depth() == run_parity)
    def _():
        right, left = right_ref[...], left_ref[...]
        out_ref[...] = states_ref[pl.ds(2 * first * n, 2 * count * n)]

        @pl.loop(0, count // pair)
        def _(step):
            @pl.loop(0, times * SUBSTEPS)
            def _(turn):
                at = [(rows(2 * s * n, n), rows((2 * s + 1) * n, n)) for s in [step * pair + u for u in range(pair)]]
                done = [taylor(out_ref[r], out_ref[i], right, left) for r, i in at]
                for (r, i), (real, imag) in zip(at, done):
                    out_ref[r] = real
                    out_ref[i] = imag

        factors = states_ref[pl.ds(2 * slots * n, ROWS)][FACTOR : FACTOR + 1]
        for s in range(count):
            scale = factors[:, first + s : first + s + 1] ** times
            at = rows(2 * s * n, n, 2)
            out_ref[at] = out_ref[at] * scale


def sided(real, imag, right, left):
    n = real.shape[0]
    after = dot(stack_cols(jnp.concatenate([real, imag], axis=0)), right)
    before = dot(left, stack_rows(jnp.concatenate([real, imag], axis=1)))
    return after[:n], after[n:], before[:, :n], before[:, n:]


def entry(tab, row, c, slots):
    if isinstance(c, int):
        return tab[c // slots, row, c % slots]
    return tab[lax.div(c, slots), row, lax.rem(c, slots)]


def operator_of(tab, c, slots, modes):
    back = c // slots if isinstance(c, int) else lax.div(c, slots)
    return back * modes + entry(tab, MODE, c, slots).astype(jnp.int32)


def parent_of(tab, c, slots):
    parent = entry(tab, PARENT, c, slots).astype(jnp.int32)
    back = lax.bitwise_xor(lax.axis_index("mode"), lax.div(parent, slots))
    return back * slots + lax.rem(parent, slots)


def child_pair(stage_ref, at, mode, weight, right_ref, left_ref):
    n = stage_ref.shape[1]
    ra, ia, rb, ib = sided(stage_ref[rows(at * n, n)], stage_ref[rows((at + 1) * n, n)], right_ref[mode], left_ref[mode])
    return weight * (ib - ia), weight * (ra - rb)


def parent_pair(stage_ref, at, mode, wa, wc, right_ref, left_ref):
    n = stage_ref.shape[1]
    ra, ia, rb, ib = sided(stage_ref[rows(at * n, n)], stage_ref[rows((at + 1) * n, n)], right_ref[mode], left_ref[mode])
    return wa * (ib - ia) + wc * (rb + ra), wa * (ra - rb) + wc * (ib + ia)


def add_pair(acc_ref, at, pair):
    n = acc_ref.shape[1]
    for i in range(2):
        where = rows(at + i * n, n)
        acc_ref[where] = acc_ref[where] + pair[i]


def part_of(parts, s):
    size = parts[0].shape[0] // (2 * parts[0].shape[1])
    return parts[s // size], 2 * (s % size)


def pick_kernel(sender, slots, group, parts, near_ref, *refs):
    tab, sem_ref = refs[-2:]
    picks = refs[-2 - parts : -2]
    groups = Layout(refs[: -2 - parts], slots, group)

    @pl.when(odd_depth() == sender)
    def _():
        pull([narrow(near_ref)], tab, sem_ref)
        for s in range(slots):
            pick, at = part_of(picks, s)
            groups.fetch(parent_of(tab, s, slots), pick, at)


def send_kernel(sender, slots, group, modes, parts, right_ref, left_ref, *refs):
    acc_ref, stage_ref, list_ref, tab, sem_ref = refs[-5:]
    tabs_ref = refs[-6]
    n = acc_ref.shape[1]
    sums = refs[-6 - parts : -6]
    groups = Layout(refs[: -6 - parts], slots, group)

    @pl.when(odd_depth() == sender)
    def _():
        pull([groups.table(k) for k in range(group)], tab, sem_ref)
        for k in range(group):
            groups.copy_table(k, tabs_ref, k)
        acc_ref[...] = jnp.zeros_like(acc_ref)

        def collect(c, count):
            mine = parent_of(tab, c, slots) < slots

            @pl.when(mine)
            def _():
                list_ref[count] = c

            return count + mine.astype(jnp.int32)

        count = lax.fori_loop(0, group * slots, collect, jnp.int32(0))

        @pl.loop(0, lax.div(count + slots - 1, slots))
        def _(batch):
            children = []
            for u in range(slots):
                place = batch * slots + u
                c = list_ref[jnp.minimum(place, count - 1)]
                groups.fetch(c, stage_ref, 2 * u)
                children.append((c, jnp.where(place < count, entry(tab, WEIGHT, c, slots), 0.0)))
            terms = [
                child_pair(stage_ref, 2 * u, operator_of(tab, c, slots, modes), weight, right_ref, left_ref)
                for u, (c, weight) in enumerate(children)
            ]
            for (c, _), pair in zip(children, terms):
                add_pair(acc_ref, 2 * parent_of(tab, c, slots) * n, pair)

        for s in range(slots):
            part, at = part_of(sums, s)
            part[rows(at * n, n, 2)] = acc_ref[rows(2 * s * n, n, 2)]


def join_kernel(receiver, slots, modes, sum_parts, pick_parts, own_ref, right_ref, left_ref, *refs):
    out_ref, tab, sem_ref = refs[-3:]
    picks = refs[-3 - pick_parts : -3]
    sums = refs[-3 - pick_parts - sum_parts : -3 - pick_parts]
    frees = refs[: -3 - pick_parts - sum_parts]
    n = frees[0].shape[1]
    final = len(frees) > 1

    @pl.when(odd_depth() == receiver)
    def _():
        pull([narrow(own_ref)], tab, sem_ref)
        terms = []
        for s in range(slots):
            pick, at = part_of(picks, s)
            wa, wc = tab[0, WEIGHT_A, s], tab[0, WEIGHT_C, s]
            terms.append(parent_pair(pick, at, operator_of(tab, s, slots, modes), wa, wc, right_ref, left_ref))
        for s in range(slots):
            scale = tab[0, LIVE, s] * couple_step
            part, at = part_of(sums, s)
            for i in range(2):
                here = rows((2 * s + i) * n, n)
                out_ref[here] = frees[0][here] + scale * (part[rows((at + i) * n, n)] + terms[s][i])
        if not final:
            out_ref[pl.ds(2 * slots * n, ROWS)] = own_ref[...]

    if final:

        @pl.when(odd_depth() != receiver)
        def _():
            out_ref[...] = frees[1][...]


def side_kernel(side, receiver, slots, group, modes, span, base_count, group_count, tab_count, right_ref, left_ref, *refs):
    stage_ref, tab, sem_ref = refs[-3:]
    start, count = span
    bases = refs[:base_count]
    groups = Layout(refs[base_count : base_count + group_count], slots, count)
    tab_refs = refs[base_count + group_count : base_count + group_count + tab_count]
    outs = refs[base_count + group_count + tab_count : -3]
    second = len(outs[-1].shape) == 2
    n = stage_ref.shape[1]
    size = 2 * slots * n
    gathered = Layout(tab_refs, slots, group) if tab_count > 1 else None
    own_tables = [gathered.table(k) if gathered else tab_refs[0].at[k, pl.ds(0, ROWS), pl.ds(0, LANES)] for k in range(group)]
    held = group // len(outs) if second else group
    stride = size + ROWS if second else size

    @pl.when(odd_depth() == receiver)
    def _():
        below = [groups.table(k) for k in range(count)] if side == "children" else []
        pull(own_tables + below, tab, sem_ref)
        if second:
            for k in range(group):
                ref, base = outs[k // held], (k % held) * stride
                ref[pl.ds(base, size)] = bases[0][pl.ds(k * size, size)]
                ref[pl.ds(base + size, ROWS)] = tab_refs[0][k]
        else:
            offset = 0
            for base in bases:
                outs[0][pl.ds(offset, base.shape[0])] = base[...]
                offset += base.shape[0]
            for k in range(group):
                if gathered:
                    gathered.copy_table(k, outs[1], k)
                else:
                    outs[1][k] = tab_refs[0][k]

        def add(index, pair):
            if not second:
                add_pair(outs[0], 2 * index * n, pair)
                return
            for half, ref in enumerate(outs):
                local = index - half * held * slots
                at = lax.div(local, slots) * stride + lax.rem(local, slots) * (2 * n)

                @pl.when(jnp.logical_and(local >= 0, local < held * slots))
                def _():
                    add_pair(ref, at, pair)

        @pl.loop(0, count)
        def _(k):
            at = k * slots
            targets, terms = [], []
            for s in range(slots):
                c = at + s
                groups.fetch(c if side == "children" else parent_of(tab, c, slots), stage_ref, 2 * s)
            for s in range(slots):
                c = at + s
                if side == "children":
                    b = c + group * slots
                    target = parent_of(tab, b, slots)
                    weight = entry(tab, WEIGHT, b, slots) * (entry(tab, LIVE, target, slots) * couple_step)
                    mode = operator_of(tab, b, slots, modes) + (start - group) * modes
                    terms.append(child_pair(stage_ref, 2 * s, mode, weight, right_ref, left_ref))
                else:
                    target = c
                    scale = entry(tab, LIVE, c, slots) * couple_step
                    wa, wc = entry(tab, WEIGHT_A, c, slots) * scale, entry(tab, WEIGHT_C, c, slots) * scale
                    mode = operator_of(tab, c, slots, modes)
                    terms.append(parent_pair(stage_ref, 2 * s, mode, wa, wc, right_ref, left_ref))
                targets.append(target)
            for target, pair in zip(targets, terms):
                add(target, pair)


def call(kernel, out_shapes, limit, args, smem=0, us=1.0, scratch=()):
    specs = [pl.BlockSpec(memory_space=SMEM)] * smem
    specs += [pl.BlockSpec(memory_space=VMEM)] * (len(args) - smem)
    return pl.pallas_call(
        kernel,
        out_shape=out_shapes,
        in_specs=specs,
        out_specs=jax.tree.map(lambda _: pl.BlockSpec(memory_space=VMEM), out_shapes),
        scratch_shapes=scratch,
        compiler_params=pltpu.CompilerParams(vmem_limit_bytes=limit),
        cost_estimate=pl.CostEstimate(flops=int(us * 1.1e9), bytes_accessed=1 << 19, transcendentals=0),
    )(*args)


def turn_order(group):
    return sorted(range(1, group), key=lambda k: (bin(k).count("1"), -k))


def shards(sizes, blocks, live_slots, parent_index, bath_mode, hamiltonian, coupling, correlation, damping, link_weight):
    depths, group = sizes
    slots, _, n, _ = blocks.shape
    modes = coupling.shape[0]
    total = group * slots
    limit = 8 * total * 2 * n * n * 4
    order = turn_order(group)
    split_hop = 2 if slots % 2 == 0 else 1
    ranks = range(group)

    def place(d, m):
        return d * group + m

    def permute(value, pairs):
        return lax.ppermute(value, AXES, pairs)

    def gather(value, parity):
        held = {0: value}
        for k in order:
            step = k & -k
            pairs = [(place(d, m), place(d, m ^ step)) for d in range(parity, depths, 2) for m in ranks]
            held[k] = permute(held[k ^ step], pairs)
        return [held[k] for k in ranks]

    def shift(value, step, parity=None):
        pairs = [
            (place(d, m), place(d + step, m))
            for d in range(depths)
            for m in ranks
            if 0 <= d + step < depths and (parity is None or d % 2 == parity)
        ]
        return permute(value, pairs)

    def mats(count, tables=0):
        return jax.ShapeDtypeStruct((count * n + tables * ROWS, n), f32)

    def sds(*shape, dtype=f32):
        return jax.ShapeDtypeStruct(shape, dtype)

    plain = 2 * slots
    stage = VMEM((plain * n, n), f32)

    def tables(count):
        return [SMEM((count, ROWS, LANES), f32), pltpu.SemaphoreType.DMA((count,))]

    operator_shapes = (sds(group * modes, 3 * n, n, dtype=bf16), sds(group * modes, n, 3 * n, dtype=bf16))
    couplings = coupling.reshape(modes * n, n)

    packed, own_table = call(
        pack_kernel,
        (mats(plain + modes, 1), sds(ROWS, n)),
        PACK_LIMIT,
        (live_slots, parent_index, bath_mode, damping, link_weight, correlation, blocks.reshape(plain * n, n), couplings),
        smem=6,
    )
    first = gather(packed, 1)
    near_table = shift(own_table, -1)
    powers = call(
        powers_kernel, (sds(3 * n, ORDER * n, dtype=bf16), sds(n, 3 * ORDER * n, dtype=bf16)), limit, (hamiltonian,)
    )
    *operators_odd, raw = call(
        functools.partial(operators_kernel, slots, group, modes, None),
        (*operator_shapes, mats((group - 1) * modes)),
        limit,
        (couplings, *first),
    )

    def free(states, parity, times, part=0, parts=1):
        count = slots // parts
        return call(
            functools.partial(free_kernel, parity, times, slots, part * count),
            mats(2 * count),
            limit,
            (states, *powers),
            us=4.5 * times / parts,
        )

    def free_parts(states, parity, times):
        return [free(states, parity, times, part, split_hop) for part in range(split_hop)]

    def pick(groups, sender, parts):
        return call(
            functools.partial(pick_kernel, sender, slots, group, parts),
            [mats(plain // parts)] * parts,
            limit,
            (near_table, *groups),
            scratch=tables(1),
        )

    def send(groups, sender, parts, operators):
        outs = call(
            functools.partial(send_kernel, sender, slots, group, modes, parts),
            [mats(plain // parts)] * parts + [sds(group, ROWS, n)],
            limit,
            (*operators, *groups),
            us=2,
            scratch=[stage, stage, SMEM((total,), jnp.int32), *tables(group)],
        )
        return outs[:parts], outs[-1]

    def join(frees, sums, picks, receiver, operators):
        return call(
            functools.partial(join_kernel, receiver, slots, modes, len(sums), len(picks)),
            mats(plain) if len(frees) > 1 else mats(plain, 1),
            limit,
            (own_table, *operators, *frees, *sums, *picks),
            scratch=tables(1),
        )

    def side(kind, bases, groups, tabs, receiver, operators, second=False, span=None):
        halves = 2 if group % 2 == 0 else 1
        span = (0, group) if span is None else span
        return call(
            functools.partial(side_kernel, kind, receiver, slots, group, modes, span, len(bases), len(groups), len(tabs)),
            [mats(2 * total // halves, group // halves)] * halves if second else [mats(2 * total), sds(group, ROWS, n)],
            limit,
            (*operators, *bases, *groups, *tabs),
            us=3,
            scratch=[stage, *tables(group + (span[1] if kind == "children" else 0))],
        )

    free_even = free(packed, 0, 1)
    free_odd = [part for k in ranks for part in free_parts(first[k], 1, 2)]
    picks = [shift(value, 1, 1) for value in pick(first, 1, split_hop)]
    sums, tabs_odd = send(first, 1, 1, operators_odd)
    sums = [shift(value, -1, 1) for value in sums]
    own_state = join([free_even], sums, picks, 0, operators_odd)

    gathered = gather(own_state, 0)
    from_below = [shift(value, -1, 0) for value in gathered]
    from_above = [shift(value, 1, 0) for value in gathered]
    free_even = [part for k in ranks for part in free_parts(gathered[k], 0, 2)]
    ready = group - 1
    states, _ = side("children", free_odd, from_below[:ready], [tabs_odd], 1, operators_odd, span=(0, ready))
    states, _ = side("parents", [states], from_above, [tabs_odd], 1, operators_odd)
    states = side("children", [states], from_below[ready:], [tabs_odd], 1, operators_odd, second=True, span=(ready, 1))

    from_above = [shift(value, 1, 1) for value in states]
    from_below = [shift(value, -1, 1) for value in states]
    passed = shift(raw, -1, 1)
    operators_even = call(
        functools.partial(operators_kernel, slots, group, modes, 0), operator_shapes, limit, (couplings, passed)
    )
    last_odd = free(states[0], 1, 2)
    states, tabs_even = side("children", free_even, from_below, gathered, 0, operators_even)
    states = side("parents", [states], from_above, [tabs_even], 0, operators_even, second=True)

    sums, _ = send(states, 0, split_hop, operators_even)
    sums = [shift(value, -1, 0) for value in sums]
    picks = [shift(value, 1, 0) for value in pick(states, 0, 1)]
    last_even = free(states[0], 0, 1)
    return join([last_odd, last_even], sums, picks, 1, operators_odd).reshape(blocks.shape)


def solution(mesh):
    sizes = (mesh.shape["depth"], mesh.shape["mode"])

    def whole(*args):
        return shards(sizes, *args)

    return jax.shard_map(
        whole,
        mesh=mesh,
        in_specs=(
            P(("depth", "mode"), None, None, None),
            P(("depth", "mode")),
            P(("depth", "mode")),
            P(("depth", "mode")),
            P(),
            P("mode", None, None),
            P("mode", None),
            P(("depth", "mode")),
            P(("depth", "mode")),
        ),
        out_specs=P(("depth", "mode"), None, None, None),
        check_vma=False,
    )
```

```python
import functools
import math
import jax
import jax.numpy as jnp
from jax import lax
from jax.experimental import pallas as pl
from jax.experimental.pallas import tpu as pltpu
from jax.sharding import PartitionSpec as P

SUBSTEPS = 2
ORDER = 4
substep = 0.7
couple_step = 0.2

AXES = ("depth", "mode")
VMEM = pltpu.VMEM
SMEM = pltpu.SMEM
bf16 = jnp.bfloat16
f32 = jnp.float32

PARENT, MODE, LIVE, FACTOR, WEIGHT, WEIGHT_A, WEIGHT_C = range(7)
ROWS, LANES = 8, 128
PACK_LIMIT = 56 << 20


def split(value):
    high = value.astype(bf16)
    return high, (value - high.astype(f32)).astype(bf16)


def stack_rows(value):
    high, low = split(value)
    return jnp.concatenate([high, high, low], axis=0)


def stack_cols(value):
    high, low = split(value)
    return jnp.concatenate([high, low, high], axis=1)


def dot(first, second):
    return jnp.dot(first, second, preferred_element_type=f32)


def exact(first, second):
    return jnp.dot(first, second, preferred_element_type=f32, precision=lax.Precision.HIGHEST)


def odd_depth():
    return lax.rem(lax.axis_index("depth"), 2)


def rows(at, n, count=1):
    if not isinstance(at, int):
        at = pl.multiple_of(at, ROWS)
    return pl.ds(at, count * n)


def pack_kernel(live_ref, parent_ref, mode_ref, damping_ref, weight_ref, corr_ref, coupling_ref, out_ref, table_ref):
    slots, n = live_ref.shape[0], coupling_ref.shape[1]
    out_ref[pl.ds(ROWS, coupling_ref.shape[0])] = coupling_ref[...]
    row = lax.broadcasted_iota(jnp.int32, (ROWS, n), 0)
    lane = lax.broadcasted_iota(jnp.int32, (ROWS, n), 1)
    table = jnp.zeros((ROWS, n), f32)
    first_mode = lax.axis_index("mode") * corr_ref.shape[0]
    for s in range(slots):
        mode = mode_ref[s] - first_mode
        live = live_ref[s].astype(f32)
        weight = weight_ref[s]
        values = {
            PARENT: parent_ref[s].astype(f32),
            MODE: mode.astype(f32),
            LIVE: live,
            FACTOR: damping_ref[s] * (-SUBSTEPS * substep),
            WEIGHT: weight * live,
            WEIGHT_A: weight * corr_ref[mode, 0],
            WEIGHT_C: weight * corr_ref[mode, 1],
        }
        for at, value in values.items():
            table = jnp.where(jnp.logical_and(row == at, lane == s), value, table)
    live_row = table[LIVE : LIVE + 1]
    table = jnp.where(row == FACTOR, live_row * jnp.exp(table), table)
    table_ref[...] = table
    out_ref[pl.ds(0, ROWS)] = table


def powers_kernel(ham_ref, right_ref, left_ref):
    n = ham_ref.shape[0]
    ham = (ham_ref[...] + ham_ref[...].T) * 0.5
    power = ham
    for k in range(1, ORDER + 1):
        if k > 1:
            power = exact(power, ham)
        scaled = power * (substep**k / math.factorial(k))
        right_ref[:, (k - 1) * n : k * n] = stack_rows(scaled)
        left_ref[:, (k - 1) * 3 * n : k * 3 * n] = stack_cols(scaled)


def single(group):
    return [[k] for k in range(group)]


def joined(group):
    return [[0], list(range(2, group)), [1]]


class Layout:
    def __init__(self, refs, slots, split, notes=()):
        self.refs, self.slots, self.split, self.notes = refs, slots, split, notes
        self.group = sum(len(held) for held in split)
        self.n = refs[0].shape[1]
        self.size = 2 * slots * self.n
        self.stride = self.size + ROWS

    def base(self, k):
        for ref, held in zip(self.refs, self.split):
            if k in held:
                return ref, held.index(k) * self.stride

    def table_rows(self, k):
        if self.notes:
            return self.notes[k], pl.ds(0, ROWS)
        ref, base = self.base(k)
        return ref, pl.ds(base + self.size, ROWS)

    def table(self, k):
        ref, where = self.table_rows(k)
        return ref.at[where, pl.ds(0, LANES)]

    def copy_table(self, k, target_ref, at):
        ref, where = self.table_rows(k)
        target_ref[at] = ref[where]

    def fetch(self, index, stage_ref, at):
        for k in range(self.group):
            ref, base = self.base(k)
            local = index - k * self.slots

            @pl.when(jnp.logical_and(local >= 0, local < self.slots))
            def _():
                stage_ref[rows(at * self.n, self.n, 2)] = ref[rows(base + 2 * local * self.n, self.n, 2)]


def pull(sources, smem_ref, sem_ref):
    copies = [pltpu.make_async_copy(ref, smem_ref.at[i], sem_ref.at[i]) for i, ref in enumerate(sources)]
    for copy in copies:
        copy.start()
    for copy in copies:
        copy.wait()


def narrow(ref):
    return ref.at[pl.ds(0, ROWS), pl.ds(0, LANES)]


def operators_kernel(group, modes, parity, own_ref, *refs):
    outs = refs[-2 - (parity is None) :]
    sources = refs[: -len(outs)]
    right_ref, left_ref = outs[0], outs[1]
    n = own_ref.shape[1]

    def put(at, value):
        sym = (value + value.T) * 0.5
        right_ref[at] = stack_rows(sym)
        left_ref[at] = stack_cols(sym)

    def own():
        for i in range(modes):
            put(i, own_ref[rows(i * n, n)])

    if parity is None:
        own()
        for k in range(1, group):
            for i in range(modes):
                value = sources[k][rows(ROWS + i * n, n)]
                put(k * modes + i, value)
                outs[2][rows(((k - 1) * modes + i) * n, n)] = value
    else:

        @pl.when(odd_depth() == parity)
        def _():
            own()
            for at in range(modes, group * modes):
                put(at, sources[0][rows((at - modes) * n, n)])


def taylor(real, imag, right, left):
    n = real.shape[0]
    out = dot(stack_cols(jnp.concatenate([real, imag], axis=0)), right)
    rp = [out[:n, k * n : (k + 1) * n] for k in range(ORDER)]
    ip = [out[n:, k * n : (k + 1) * n] for k in range(ORDER)]
    u_real, u_imag = real, imag
    stacked = [None] * ORDER
    for k in range(ORDER + 1):
        if k:
            turn = k % 4
            if turn == 1:
                u_real, u_imag = u_real - ip[k - 1], u_imag + rp[k - 1]
            elif turn == 2:
                u_real, u_imag = u_real - rp[k - 1], u_imag - ip[k - 1]
            elif turn == 3:
                u_real, u_imag = u_real + ip[k - 1], u_imag - rp[k - 1]
            else:
                u_real, u_imag = u_real + rp[k - 1], u_imag + ip[k - 1]
        j = ORDER - k
        if j:
            turn = j % 4
            if turn == 1:
                pair = (u_imag, -u_real)
            elif turn == 2:
                pair = (-u_real, -u_imag)
            elif turn == 3:
                pair = (-u_imag, u_real)
            else:
                pair = (u_real, u_imag)
            stacked[j - 1] = stack_rows(jnp.concatenate(pair, axis=1))
    done = dot(left, jnp.concatenate(stacked, axis=0))
    return u_real + done[:, :n], u_imag + done[:, n:]


def free_kernel(run_parity, times, first, table_row, states_ref, table_ref, right_ref, left_ref, *refs):
    out_ref = refs[-1]
    n = out_ref.shape[1]
    ahead = first if len(refs) > 1 else 0
    count = out_ref.shape[0] // (2 * n) - ahead
    pair = 2 if count % 2 == 0 else 1

    @pl.when(odd_depth() == run_parity)
    def _():
        right, left = right_ref[...], left_ref[...]
        if ahead:
            out_ref[pl.ds(0, 2 * ahead * n)] = refs[0][...]
        out_ref[pl.ds(2 * ahead * n, 2 * count * n)] = states_ref[pl.ds(2 * first * n, 2 * count * n)]

        @pl.loop(0, count // pair)
        def _(step):
            @pl.loop(0, times * SUBSTEPS)
            def _(turn):
                blocks = [ahead + step * pair + u for u in range(pair)]
                at = [(rows(2 * s * n, n), rows((2 * s + 1) * n, n)) for s in blocks]
                done = [taylor(out_ref[r], out_ref[i], right, left) for r, i in at]
                for (r, i), (real, imag) in zip(at, done):
                    out_ref[r] = real
                    out_ref[i] = imag

        factors = table_ref[pl.ds(table_row, ROWS)][FACTOR : FACTOR + 1]
        for s in range(count):
            scale = factors[:, first + s : first + s + 1] ** times
            at = rows(2 * (ahead + s) * n, n, 2)
            out_ref[at] = out_ref[at] * scale


def sided(real, imag, right, left):
    n = real.shape[0]
    after = dot(stack_cols(jnp.concatenate([real, imag], axis=0)), right)
    before = dot(left, stack_rows(jnp.concatenate([real, imag], axis=1)))
    return after[:n], after[n:], before[:, :n], before[:, n:]


def entry(tab, row, c, slots):
    if isinstance(c, int):
        return tab[c // slots, row, c % slots]
    return tab[lax.div(c, slots), row, lax.rem(c, slots)]


def operator_of(tab, c, slots, modes):
    back = c // slots if isinstance(c, int) else lax.div(c, slots)
    return back * modes + entry(tab, MODE, c, slots).astype(jnp.int32)


def parent_of(tab, c, slots):
    parent = entry(tab, PARENT, c, slots).astype(jnp.int32)
    back = lax.bitwise_xor(lax.axis_index("mode"), lax.div(parent, slots))
    return back * slots + lax.rem(parent, slots)


def child_pair(stage_ref, at, mode, weight, right_ref, left_ref):
    n = stage_ref.shape[1]
    ra, ia, rb, ib = sided(stage_ref[rows(at * n, n)], stage_ref[rows((at + 1) * n, n)], right_ref[mode], left_ref[mode])
    return weight * (ib - ia), weight * (ra - rb)


def parent_pair(stage_ref, at, mode, wa, wc, right_ref, left_ref):
    n = stage_ref.shape[1]
    ra, ia, rb, ib = sided(stage_ref[rows(at * n, n)], stage_ref[rows((at + 1) * n, n)], right_ref[mode], left_ref[mode])
    return wa * (ib - ia) + wc * (rb + ra), wa * (ra - rb) + wc * (ib + ia)


def add_pair(acc_ref, at, pair):
    n = acc_ref.shape[1]
    for i in range(2):
        where = rows(at + i * n, n)
        acc_ref[where] = acc_ref[where] + pair[i]


def part_of(parts, s):
    size = parts[0].shape[0] // (2 * parts[0].shape[1])
    return parts[s // size], 2 * (s % size)


def pick_kernel(sender, slots, split, parts, near_ref, *refs):
    tab, sem_ref = refs[-2:]
    picks = refs[-2 - parts : -2]
    groups = Layout(refs[: -2 - parts], slots, split)

    @pl.when(odd_depth() == sender)
    def _():
        pull([narrow(near_ref)], tab, sem_ref)
        for s in range(slots):
            pick, at = part_of(picks, s)
            groups.fetch(parent_of(tab, s, slots), pick, at)


def send_kernel(sender, slots, group, split, modes, parts, noted, right_ref, left_ref, *refs):
    acc_ref, stage_ref, list_ref, tab, sem_ref = refs[-5:]
    tabs_ref = refs[-6]
    n = acc_ref.shape[1]
    sums = refs[-6 - parts : -6]
    held = refs[: -6 - parts]
    groups = Layout(held[: len(split)], slots, split, held[len(split) :] if noted else ())

    @pl.when(odd_depth() == sender)
    def _():
        pull([groups.table(k) for k in range(group)], tab, sem_ref)
        for k in range(group):
            groups.copy_table(k, tabs_ref, k)
        acc_ref[...] = jnp.zeros_like(acc_ref)

        def collect(c, count):
            mine = parent_of(tab, c, slots) < slots

            @pl.when(mine)
            def _():
                list_ref[count] = c

            return count + mine.astype(jnp.int32)

        count = lax.fori_loop(0, group * slots, collect, jnp.int32(0))

        @pl.loop(0, lax.div(count + slots - 1, slots))
        def _(batch):
            children = []
            for u in range(slots):
                place = batch * slots + u
                c = list_ref[jnp.minimum(place, count - 1)]
                groups.fetch(c, stage_ref, 2 * u)
                children.append((c, jnp.where(place < count, entry(tab, WEIGHT, c, slots), 0.0)))
            terms = [
                child_pair(stage_ref, 2 * u, operator_of(tab, c, slots, modes), weight, right_ref, left_ref)
                for u, (c, weight) in enumerate(children)
            ]
            for (c, _), pair in zip(children, terms):
                add_pair(acc_ref, 2 * parent_of(tab, c, slots) * n, pair)

        for s in range(slots):
            part, at = part_of(sums, s)
            part[rows(at * n, n, 2)] = acc_ref[rows(2 * s * n, n, 2)]


def join_kernel(receiver, slots, modes, sum_parts, pick_parts, own_ref, right_ref, left_ref, *refs):
    out_ref, tab, sem_ref = refs[-3:]
    picks = refs[-3 - pick_parts : -3]
    sums = refs[-3 - pick_parts - sum_parts : -3 - pick_parts]
    frees = refs[: -3 - pick_parts - sum_parts]
    n = frees[0].shape[1]
    final = len(frees) > 1

    @pl.when(odd_depth() == receiver)
    def _():
        pull([narrow(own_ref)], tab, sem_ref)
        terms = []
        for s in range(slots):
            pick, at = part_of(picks, s)
            wa, wc = tab[0, WEIGHT_A, s], tab[0, WEIGHT_C, s]
            terms.append(parent_pair(pick, at, operator_of(tab, s, slots, modes), wa, wc, right_ref, left_ref))
        for s in range(slots):
            scale = tab[0, LIVE, s] * couple_step
            part, at = part_of(sums, s)
            for i in range(2):
                here = rows((2 * s + i) * n, n)
                out_ref[here] = frees[0][here] + scale * (part[rows((at + i) * n, n)] + terms[s][i])
        if not final:
            out_ref[pl.ds(2 * slots * n, ROWS)] = own_ref[...]

    if final:

        @pl.when(odd_depth() != receiver)
        def _():
            out_ref[...] = frees[1][...]


def side_kernel(side, receiver, slots, group, modes, span, split, base_count, group_count, tab_count, right_ref, left_ref, *refs):
    stage_ref, tab, sem_ref = refs[-3:]
    start, step, count = span
    bases = refs[:base_count]
    groups = Layout(refs[base_count : base_count + group_count], slots, split)
    tab_refs = refs[base_count + group_count : base_count + group_count + tab_count]
    outs = refs[base_count + group_count + tab_count : -3]
    second = len(outs[-1].shape) == 2
    n = stage_ref.shape[1]
    size = 2 * slots * n
    gathered = Layout(tab_refs, slots, single(group)) if tab_count > 1 else None
    own_tables = [gathered.table(k) if gathered else tab_refs[0].at[k, pl.ds(0, ROWS), pl.ds(0, LANES)] for k in range(group)]
    out = Layout(outs, slots, joined(group)) if second else None

    @pl.when(odd_depth() == receiver)
    def _():
        below = [groups.table(k) for k in range(count)] if side == "children" else []
        pull(own_tables + below, tab, sem_ref)
        if second:
            for k in range(group):
                ref, base = out.base(k)
                ref[pl.ds(base, size)] = bases[0][pl.ds(k * size, size)]
                ref[pl.ds(base + size, ROWS)] = tab_refs[0][k]
        else:
            offset = 0
            for base in bases:
                outs[0][pl.ds(offset, base.shape[0])] = base[...]
                offset += base.shape[0]
            for k in range(group):
                if gathered:
                    gathered.copy_table(k, outs[1], k)
                else:
                    outs[1][k] = tab_refs[0][k]

        def add(index, pair):
            if not second:
                add_pair(outs[0], 2 * index * n, pair)
                return
            for ref, held in zip(outs, out.split):
                local = index - held[0] * slots
                at = lax.div(local, slots) * out.stride + lax.rem(local, slots) * (2 * n)

                @pl.when(jnp.logical_and(local >= 0, local < len(held) * slots))
                def _():
                    add_pair(ref, at, pair)

        @pl.loop(0, count)
        def _(k):
            at = k * slots
            targets, terms = [], []
            for s in range(slots):
                c = at + s
                groups.fetch(c if side == "children" else parent_of(tab, c, slots), stage_ref, 2 * s)
            for s in range(slots):
                c = at + s
                if side == "children":
                    b = c + group * slots
                    target = parent_of(tab, b, slots)
                    weight = entry(tab, WEIGHT, b, slots) * (entry(tab, LIVE, target, slots) * couple_step)
                    mode = entry(tab, MODE, b, slots).astype(jnp.int32) + (start + k * step) * modes
                    terms.append(child_pair(stage_ref, 2 * s, mode, weight, right_ref, left_ref))
                else:
                    target = c
                    scale = entry(tab, LIVE, c, slots) * couple_step
                    wa, wc = entry(tab, WEIGHT_A, c, slots) * scale, entry(tab, WEIGHT_C, c, slots) * scale
                    mode = operator_of(tab, c, slots, modes)
                    terms.append(parent_pair(stage_ref, 2 * s, mode, wa, wc, right_ref, left_ref))
                targets.append(target)
            for target, pair in zip(targets, terms):
                add(target, pair)


def call(kernel, out_shapes, limit, args, smem=0, us=1.0, scratch=()):
    specs = [pl.BlockSpec(memory_space=SMEM)] * smem
    specs += [pl.BlockSpec(memory_space=VMEM)] * (len(args) - smem)
    return pl.pallas_call(
        kernel,
        out_shape=out_shapes,
        in_specs=specs,
        out_specs=jax.tree.map(lambda _: pl.BlockSpec(memory_space=VMEM), out_shapes),
        scratch_shapes=scratch,
        compiler_params=pltpu.CompilerParams(vmem_limit_bytes=limit),
        cost_estimate=pl.CostEstimate(flops=int(us * 1.1e9), bytes_accessed=1 << 19, transcendentals=0),
    )(*args)


def turn_order(group):
    return sorted(range(1, group), key=lambda k: (bin(k).count("1"), -k))


def shards(sizes, blocks, live_slots, parent_index, bath_mode, hamiltonian, coupling, correlation, damping, link_weight):
    depths, group = sizes
    slots, _, n, _ = blocks.shape
    modes = coupling.shape[0]
    total = group * slots
    limit = 8 * total * 2 * n * n * 4
    order = turn_order(group)
    split_hop = 2 if slots % 2 == 0 else 1
    ranks = range(group)

    def place(d, m):
        return d * group + m

    def permute(value, pairs):
        return lax.ppermute(value, AXES, pairs)

    def gather(value, parity):
        held = {0: value}
        for k in order:
            step = k & -k
            pairs = [(place(d, m), place(d, m ^ step)) for d in range(parity, depths, 2) for m in ranks]
            held[k] = permute(held[k ^ step], pairs)
        return [held[k] for k in ranks]

    def shift(value, step, parity=None):
        pairs = [
            (place(d, m), place(d + step, m))
            for d in range(depths)
            for m in ranks
            if 0 <= d + step < depths and (parity is None or d % 2 == parity)
        ]
        return permute(value, pairs)

    def neighbour(value, parity):
        pairs = [(place(d, m), place(d, m ^ 1)) for d in range(parity, depths, 2) for m in ranks]
        return permute(value, pairs)

    def mats(count, tables=0):
        return jax.ShapeDtypeStruct((count * n + tables * ROWS, n), f32)

    def sds(*shape, dtype=f32):
        return jax.ShapeDtypeStruct(shape, dtype)

    plain = 2 * slots
    stage = VMEM((plain * n, n), f32)

    def tables(count):
        return [SMEM((count, ROWS, LANES), f32), pltpu.SemaphoreType.DMA((count,))]

    operator_shapes = (sds(group * modes, 3 * n, n, dtype=bf16), sds(group * modes, n, 3 * n, dtype=bf16))
    couplings = coupling.reshape(modes * n, n)

    states = blocks.reshape(plain * n, n)
    first = gather(states, 1)
    packed, own_table = call(
        pack_kernel,
        (mats(modes, 1), sds(ROWS, n)),
        PACK_LIMIT,
        (live_slots, parent_index, bath_mode, damping, link_weight, correlation, couplings),
        smem=6,
    )
    notes = gather(packed, 1)
    near_table = shift(own_table, -1)
    powers = call(
        powers_kernel, (sds(3 * n, ORDER * n, dtype=bf16), sds(n, 3 * ORDER * n, dtype=bf16)), limit, (hamiltonian,)
    )
    *operators_odd, raw = call(
        functools.partial(operators_kernel, group, modes, None),
        (*operator_shapes, mats((group - 1) * modes)),
        limit,
        (couplings, *notes),
    )

    def free(states, parity, times, part=0, parts=1, prior=None, note=None):
        count = slots // parts
        table, row = (states, plain * n) if note is None else (note, 0)
        return call(
            functools.partial(free_kernel, parity, times, part * count, row),
            mats(2 * count * (1 if prior is None else part + 1)),
            limit,
            (states, table, *powers) if prior is None else (states, table, *powers, prior),
            us=4.5 * times / parts,
        )

    def free_parts(states, parity, times, note):
        return [free(states, parity, times, part, split_hop, note=note) for part in range(split_hop)]

    def free_chain(states, parity, times):
        done = None
        for part in range(split_hop):
            done = free(states, parity, times, part, split_hop, done)
        return done

    splits = {group: single(group), len(joined(group)): joined(group)}

    def pick(groups, sender, parts):
        return call(
            functools.partial(pick_kernel, sender, slots, splits[len(groups)], parts),
            [mats(plain // parts)] * parts,
            limit,
            (near_table, *groups),
            scratch=tables(1),
        )

    def send(groups, sender, parts, operators, notes=()):
        outs = call(
            functools.partial(send_kernel, sender, slots, group, splits[len(groups)], modes, parts, bool(notes)),
            [mats(plain // parts)] * parts + [sds(group, ROWS, n)],
            limit,
            (*operators, *groups, *notes),
            us=2,
            scratch=[stage, stage, SMEM((total,), jnp.int32), *tables(group)],
        )
        return outs[:parts], outs[-1]

    def join(frees, sums, picks, receiver, operators):
        return call(
            functools.partial(join_kernel, receiver, slots, modes, len(sums), len(picks)),
            mats(plain) if len(frees) > 1 else mats(plain, 1),
            limit,
            (own_table, *operators, *frees, *sums, *picks),
            scratch=tables(1),
        )

    def side(kind, bases, groups, tabs, receiver, operators, second=False, span=None):
        split = splits[len(groups)] if span is None else single(len(groups))
        span = (0, 1, group) if span is None else span
        return call(
            functools.partial(
                side_kernel, kind, receiver, slots, group, modes, span, split, len(bases), len(groups), len(tabs)
            ),
            [mats(plain * len(held), len(held)) for held in joined(group)]
            if second
            else [mats(2 * total), sds(group, ROWS, n)],
            limit,
            (*operators, *bases, *groups, *tabs),
            us=3,
            scratch=[stage, *tables(group + (span[2] if kind == "children" else 0))],
        )

    free_even = free(states, 0, 1, note=packed)
    free_odd = [part for k in ranks for part in free_parts(first[k], 1, 2, notes[k])]
    picks = [shift(value, 1, 1) for value in pick(first, 1, split_hop)]
    sums, tabs_odd = send(first, 1, 1, operators_odd, notes)
    sums = [shift(value, -1, 1) for value in sums]
    passed = shift(raw, -1, 1)
    operators_even = call(
        functools.partial(operators_kernel, group, modes, 0), operator_shapes, limit, (couplings, passed)
    )
    own_state = join([free_even], sums, picks, 0, operators_odd)

    gathered = gather(own_state, 0)
    from_below = [shift(value, -1, 0) for value in gathered[:-1]]
    from_below.append(neighbour(from_below[group - 2], 1))
    from_above = [shift(value, 1, 0) for value in gathered]
    free_own = free_chain(gathered[0], 0, 2)
    free_even = [free_own, neighbour(free_own, 0)] + [free(gathered[k], 0, 2) for k in range(2, group)]
    evens, odds = (0, 2, group // 2), (1, 2, group // 2)
    states, _ = side("children", free_odd, from_below[::2], [tabs_odd], 1, operators_odd, span=evens)
    states, _ = side("parents", [states], from_above, [tabs_odd], 1, operators_odd)
    states = side("children", [states], from_below[1::2], [tabs_odd], 1, operators_odd, second=True, span=odds)

    from_above = [shift(value, 1, 1) for value in states[:2]]
    from_above.append(neighbour(from_above[0], 0))
    from_below = [shift(value, -1, 1) for value in states]
    last_odd = free(states[0], 1, 2)
    states, tabs_even = side("children", free_even, from_below, gathered, 0, operators_even)
    states = side("parents", [states], from_above, [tabs_even], 0, operators_even, second=True)

    sums, _ = send(states, 0, split_hop, operators_even)
    sums = [shift(value, -1, 0) for value in sums]
    picks = [shift(value, 1, 0) for value in pick(states, 0, 1)]
    last_even = free(states[0], 0, 1)
    return join([last_odd, last_even], sums, picks, 1, operators_odd).reshape(blocks.shape)


def solution(mesh):
    sizes = (mesh.shape["depth"], mesh.shape["mode"])

    def whole(*args):
        return shards(sizes, *args)

    return jax.shard_map(
        whole,
        mesh=mesh,
        in_specs=(
            P(("depth", "mode"), None, None, None),
            P(("depth", "mode")),
            P(("depth", "mode")),
            P(("depth", "mode")),
            P(),
            P("mode", None, None),
            P("mode", None),
            P(("depth", "mode")),
            P(("depth", "mode")),
        ),
        out_specs=P(("depth", "mode"), None, None, None),
        check_vma=False,
    )
```

```python
import functools
import math
import jax
import jax.numpy as jnp
from jax import lax
from jax.experimental import pallas as pl
from jax.experimental.pallas import tpu as pltpu
from jax.sharding import PartitionSpec as P

SUBSTEPS = 2
ORDER = 4
substep = 0.7
couple_step = 0.2

AXES = ("depth", "mode")
VMEM = pltpu.VMEM
SMEM = pltpu.SMEM
bf16 = jnp.bfloat16
f32 = jnp.float32

PARENT, MODE, LIVE, FACTOR, WEIGHT, WEIGHT_A, WEIGHT_C = range(7)
ROWS, LANES = 8, 128
PACK_LIMIT = 56 << 20


def split(value):
    high = value.astype(bf16)
    return high, (value - high.astype(f32)).astype(bf16)


def stack_rows(value):
    high, low = split(value)
    return jnp.concatenate([high, high, low], axis=0)


def stack_cols(value):
    high, low = split(value)
    return jnp.concatenate([high, low, high], axis=1)


def dot(first, second):
    return jnp.dot(first, second, preferred_element_type=f32)


def exact(first, second):
    return jnp.dot(first, second, preferred_element_type=f32, precision=lax.Precision.HIGHEST)


def odd_depth():
    return lax.rem(lax.axis_index("depth"), 2)


def rows(at, n, count=1):
    if not isinstance(at, int):
        at = pl.multiple_of(at, ROWS)
    return pl.ds(at, count * n)


def pack_kernel(live_ref, parent_ref, mode_ref, damping_ref, weight_ref, corr_ref, blocks_ref, coupling_ref, out_ref, table_ref):
    slots, n = live_ref.shape[0], blocks_ref.shape[1]
    size = blocks_ref.shape[0]
    out_ref[pl.ds(0, size)] = blocks_ref[...]
    out_ref[pl.ds(size + ROWS, coupling_ref.shape[0])] = coupling_ref[...]
    row = lax.broadcasted_iota(jnp.int32, (ROWS, n), 0)
    lane = lax.broadcasted_iota(jnp.int32, (ROWS, n), 1)
    table = jnp.zeros((ROWS, n), f32)
    first_mode = lax.axis_index("mode") * corr_ref.shape[0]
    for s in range(slots):
        mode = mode_ref[s] - first_mode
        live = live_ref[s].astype(f32)
        weight = weight_ref[s]
        values = {
            PARENT: parent_ref[s].astype(f32),
            MODE: mode.astype(f32),
            LIVE: live,
            FACTOR: damping_ref[s] * (-SUBSTEPS * substep),
            WEIGHT: weight * live,
            WEIGHT_A: weight * corr_ref[mode, 0],
            WEIGHT_C: weight * corr_ref[mode, 1],
        }
        for at, value in values.items():
            table = jnp.where(jnp.logical_and(row == at, lane == s), value, table)
    live_row = table[LIVE : LIVE + 1]
    table = jnp.where(row == FACTOR, live_row * jnp.exp(table), table)
    table_ref[...] = table
    out_ref[pl.ds(size, ROWS)] = table


def powers_kernel(ham_ref, right_ref, left_ref):
    n = ham_ref.shape[0]
    ham = (ham_ref[...] + ham_ref[...].T) * 0.5
    power = ham
    for k in range(1, ORDER + 1):
        if k > 1:
            power = exact(power, ham)
        scaled = power * (substep**k / math.factorial(k))
        right_ref[:, (k - 1) * n : k * n] = stack_rows(scaled)
        left_ref[:, (k - 1) * 3 * n : k * 3 * n] = stack_cols(scaled)


def single(group):
    return [[k] for k in range(group)]


def joined(group):
    return [[0], list(range(2, group)), [1]]


class Layout:
    def __init__(self, refs, slots, split):
        self.refs, self.slots, self.split = refs, slots, split
        self.group = sum(len(held) for held in split)
        self.n = refs[0].shape[1]
        self.size = 2 * slots * self.n
        self.stride = self.size + ROWS

    def base(self, k):
        for ref, held in zip(self.refs, self.split):
            if k in held:
                return ref, held.index(k) * self.stride

    def table(self, k):
        ref, base = self.base(k)
        return ref.at[pl.ds(base + self.size, ROWS), pl.ds(0, LANES)]

    def copy_table(self, k, target_ref, at):
        ref, base = self.base(k)
        target_ref[at] = ref[pl.ds(base + self.size, ROWS)]

    def fetch(self, index, stage_ref, at):
        for k in range(self.group):
            ref, base = self.base(k)
            local = index - k * self.slots

            @pl.when(jnp.logical_and(local >= 0, local < self.slots))
            def _():
                stage_ref[rows(at * self.n, self.n, 2)] = ref[rows(base + 2 * local * self.n, self.n, 2)]


def pull(sources, smem_ref, sem_ref):
    copies = [pltpu.make_async_copy(ref, smem_ref.at[i], sem_ref.at[i]) for i, ref in enumerate(sources)]
    for copy in copies:
        copy.start()
    for copy in copies:
        copy.wait()


def narrow(ref):
    return ref.at[pl.ds(0, ROWS), pl.ds(0, LANES)]


def operators_kernel(slots, group, modes, parity, own_ref, *refs):
    outs = refs[-2 - (parity is None) :]
    sources = refs[: -len(outs)]
    right_ref, left_ref = outs[0], outs[1]
    n = own_ref.shape[1]

    def put(at, value):
        sym = (value + value.T) * 0.5
        right_ref[at] = stack_rows(sym)
        left_ref[at] = stack_cols(sym)

    def own():
        for i in range(modes):
            put(i, own_ref[rows(i * n, n)])

    if parity is None:
        own()
        groups = Layout(sources, slots, single(group))
        for k in range(1, group):
            ref, base = groups.base(k)
            for i in range(modes):
                value = ref[rows(base + groups.stride + i * n, n)]
                put(k * modes + i, value)
                outs[2][rows(((k - 1) * modes + i) * n, n)] = value
    else:

        @pl.when(odd_depth() == parity)
        def _():
            own()
            for at in range(modes, group * modes):
                put(at, sources[0][rows((at - modes) * n, n)])


def taylor(real, imag, right, left):
    n = real.shape[0]
    out = dot(stack_cols(jnp.concatenate([real, imag], axis=0)), right)
    rp = [out[:n, k * n : (k + 1) * n] for k in range(ORDER)]
    ip = [out[n:, k * n : (k + 1) * n] for k in range(ORDER)]
    u_real, u_imag = real, imag
    stacked = [None] * ORDER
    for k in range(ORDER + 1):
        if k:
            turn = k % 4
            if turn == 1:
                u_real, u_imag = u_real - ip[k - 1], u_imag + rp[k - 1]
            elif turn == 2:
                u_real, u_imag = u_real - rp[k - 1], u_imag - ip[k - 1]
            elif turn == 3:
                u_real, u_imag = u_real + ip[k - 1], u_imag - rp[k - 1]
            else:
                u_real, u_imag = u_real + rp[k - 1], u_imag + ip[k - 1]
        j = ORDER - k
        if j:
            turn = j % 4
            if turn == 1:
                pair = (u_imag, -u_real)
            elif turn == 2:
                pair = (-u_real, -u_imag)
            elif turn == 3:
                pair = (-u_imag, u_real)
            else:
                pair = (u_real, u_imag)
            stacked[j - 1] = stack_rows(jnp.concatenate(pair, axis=1))
    done = dot(left, jnp.concatenate(stacked, axis=0))
    return u_real + done[:, :n], u_imag + done[:, n:]


def free_kernel(run_parity, times, slots, first, states_ref, right_ref, left_ref, *refs):
    out_ref = refs[-1]
    n = out_ref.shape[1]
    ahead = first if len(refs) > 1 else 0
    count = out_ref.shape[0] // (2 * n) - ahead
    pair = 2 if count % 2 == 0 else 1

    @pl.when(odd_depth() == run_parity)
    def _():
        right, left = right_ref[...], left_ref[...]
        if ahead:
            out_ref[pl.ds(0, 2 * ahead * n)] = refs[0][...]
        out_ref[pl.ds(2 * ahead * n, 2 * count * n)] = states_ref[pl.ds(2 * first * n, 2 * count * n)]

        @pl.loop(0, count // pair)
        def _(step):
            @pl.loop(0, times * SUBSTEPS)
            def _(turn):
                blocks = [ahead + step * pair + u for u in range(pair)]
                at = [(rows(2 * s * n, n), rows((2 * s + 1) * n, n)) for s in blocks]
                done = [taylor(out_ref[r], out_ref[i], right, left) for r, i in at]
                for (r, i), (real, imag) in zip(at, done):
                    out_ref[r] = real
                    out_ref[i] = imag

        factors = states_ref[pl.ds(2 * slots * n, ROWS)][FACTOR : FACTOR + 1]
        for s in range(count):
            scale = factors[:, first + s : first + s + 1] ** times
            at = rows(2 * (ahead + s) * n, n, 2)
            out_ref[at] = out_ref[at] * scale


def sided(real, imag, right, left):
    n = real.shape[0]
    after = dot(stack_cols(jnp.concatenate([real, imag], axis=0)), right)
    before = dot(left, stack_rows(jnp.concatenate([real, imag], axis=1)))
    return after[:n], after[n:], before[:, :n], before[:, n:]


def entry(tab, row, c, slots):
    if isinstance(c, int):
        return tab[c // slots, row, c % slots]
    return tab[lax.div(c, slots), row, lax.rem(c, slots)]


def operator_of(tab, c, slots, modes):
    back = c // slots if isinstance(c, int) else lax.div(c, slots)
    return back * modes + entry(tab, MODE, c, slots).astype(jnp.int32)


def parent_of(tab, c, slots):
    parent = entry(tab, PARENT, c, slots).astype(jnp.int32)
    back = lax.bitwise_xor(lax.axis_index("mode"), lax.div(parent, slots))
    return back * slots + lax.rem(parent, slots)


def child_pair(stage_ref, at, mode, weight, right_ref, left_ref):
    n = stage_ref.shape[1]
    ra, ia, rb, ib = sided(stage_ref[rows(at * n, n)], stage_ref[rows((at + 1) * n, n)], right_ref[mode], left_ref[mode])
    return weight * (ib - ia), weight * (ra - rb)


def parent_pair(stage_ref, at, mode, wa, wc, right_ref, left_ref):
    n = stage_ref.shape[1]
    ra, ia, rb, ib = sided(stage_ref[rows(at * n, n)], stage_ref[rows((at + 1) * n, n)], right_ref[mode], left_ref[mode])
    return wa * (ib - ia) + wc * (rb + ra), wa * (ra - rb) + wc * (ib + ia)


def add_pair(acc_ref, at, pair):
    n = acc_ref.shape[1]
    for i in range(2):
        where = rows(at + i * n, n)
        acc_ref[where] = acc_ref[where] + pair[i]


def part_of(parts, s):
    size = parts[0].shape[0] // (2 * parts[0].shape[1])
    return parts[s // size], 2 * (s % size)


def pick_kernel(sender, slots, split, parts, near_ref, *refs):
    tab, sem_ref = refs[-2:]
    picks = refs[-2 - parts : -2]
    groups = Layout(refs[: -2 - parts], slots, split)

    @pl.when(odd_depth() == sender)
    def _():
        pull([narrow(near_ref)], tab, sem_ref)
        for s in range(slots):
            pick, at = part_of(picks, s)
            groups.fetch(parent_of(tab, s, slots), pick, at)


def send_kernel(sender, slots, group, split, modes, parts, right_ref, left_ref, *refs):
    acc_ref, stage_ref, list_ref, tab, sem_ref = refs[-5:]
    tabs_ref = refs[-6]
    n = acc_ref.shape[1]
    sums = refs[-6 - parts : -6]
    groups = Layout(refs[: -6 - parts], slots, split)

    @pl.when(odd_depth() == sender)
    def _():
        pull([groups.table(k) for k in range(group)], tab, sem_ref)
        for k in range(group):
            groups.copy_table(k, tabs_ref, k)
        acc_ref[...] = jnp.zeros_like(acc_ref)

        def collect(c, count):
            mine = parent_of(tab, c, slots) < slots

            @pl.when(mine)
            def _():
                list_ref[count] = c

            return count + mine.astype(jnp.int32)

        count = lax.fori_loop(0, group * slots, collect, jnp.int32(0))

        @pl.loop(0, lax.div(count + slots - 1, slots))
        def _(batch):
            children = []
            for u in range(slots):
                place = batch * slots + u
                c = list_ref[jnp.minimum(place, count - 1)]
                groups.fetch(c, stage_ref, 2 * u)
                children.append((c, jnp.where(place < count, entry(tab, WEIGHT, c, slots), 0.0)))
            terms = [
                child_pair(stage_ref, 2 * u, operator_of(tab, c, slots, modes), weight, right_ref, left_ref)
                for u, (c, weight) in enumerate(children)
            ]
            for (c, _), pair in zip(children, terms):
                add_pair(acc_ref, 2 * parent_of(tab, c, slots) * n, pair)

        for s in range(slots):
            part, at = part_of(sums, s)
            part[rows(at * n, n, 2)] = acc_ref[rows(2 * s * n, n, 2)]


def join_kernel(receiver, slots, modes, sum_parts, pick_parts, own_ref, right_ref, left_ref, *refs):
    out_ref, tab, sem_ref = refs[-3:]
    picks = refs[-3 - pick_parts : -3]
    sums = refs[-3 - pick_parts - sum_parts : -3 - pick_parts]
    frees = refs[: -3 - pick_parts - sum_parts]
    n = frees[0].shape[1]
    final = len(frees) > 1

    @pl.when(odd_depth() == receiver)
    def _():
        pull([narrow(own_ref)], tab, sem_ref)
        terms = []
        for s in range(slots):
            pick, at = part_of(picks, s)
            wa, wc = tab[0, WEIGHT_A, s], tab[0, WEIGHT_C, s]
            terms.append(parent_pair(pick, at, operator_of(tab, s, slots, modes), wa, wc, right_ref, left_ref))
        for s in range(slots):
            scale = tab[0, LIVE, s] * couple_step
            part, at = part_of(sums, s)
            for i in range(2):
                here = rows((2 * s + i) * n, n)
                out_ref[here] = frees[0][here] + scale * (part[rows((at + i) * n, n)] + terms[s][i])
        if not final:
            out_ref[pl.ds(2 * slots * n, ROWS)] = own_ref[...]

    if final:

        @pl.when(odd_depth() != receiver)
        def _():
            out_ref[...] = frees[1][...]


def side_kernel(side, receiver, slots, group, modes, span, split, base_count, group_count, tab_count, right_ref, left_ref, *refs):
    stage_ref, tab, sem_ref = refs[-3:]
    start, step, count = span
    bases = refs[:base_count]
    groups = Layout(refs[base_count : base_count + group_count], slots, split)
    tab_refs = refs[base_count + group_count : base_count + group_count + tab_count]
    outs = refs[base_count + group_count + tab_count : -3]
    second = len(outs[-1].shape) == 2
    n = stage_ref.shape[1]
    size = 2 * slots * n
    gathered = Layout(tab_refs, slots, single(group)) if tab_count > 1 else None
    own_tables = [gathered.table(k) if gathered else tab_refs[0].at[k, pl.ds(0, ROWS), pl.ds(0, LANES)] for k in range(group)]
    out = Layout(outs, slots, joined(group)) if second else None

    @pl.when(odd_depth() == receiver)
    def _():
        below = [groups.table(k) for k in range(count)] if side == "children" else []
        pull(own_tables + below, tab, sem_ref)
        if second:
            for k in range(group):
                ref, base = out.base(k)
                ref[pl.ds(base, size)] = bases[0][pl.ds(k * size, size)]
                ref[pl.ds(base + size, ROWS)] = tab_refs[0][k]
        else:
            offset = 0
            for base in bases:
                outs[0][pl.ds(offset, base.shape[0])] = base[...]
                offset += base.shape[0]
            for k in range(group):
                if gathered:
                    gathered.copy_table(k, outs[1], k)
                else:
                    outs[1][k] = tab_refs[0][k]

        def add(index, pair):
            if not second:
                add_pair(outs[0], 2 * index * n, pair)
                return
            for ref, held in zip(outs, out.split):
                local = index - held[0] * slots
                at = lax.div(local, slots) * out.stride + lax.rem(local, slots) * (2 * n)

                @pl.when(jnp.logical_and(local >= 0, local < len(held) * slots))
                def _():
                    add_pair(ref, at, pair)

        @pl.loop(0, count)
        def _(k):
            at = k * slots
            targets, terms = [], []
            for s in range(slots):
                c = at + s
                groups.fetch(c if side == "children" else parent_of(tab, c, slots), stage_ref, 2 * s)
            for s in range(slots):
                c = at + s
                if side == "children":
                    b = c + group * slots
                    target = parent_of(tab, b, slots)
                    weight = entry(tab, WEIGHT, b, slots) * (entry(tab, LIVE, target, slots) * couple_step)
                    mode = entry(tab, MODE, b, slots).astype(jnp.int32) + (start + k * step) * modes
                    terms.append(child_pair(stage_ref, 2 * s, mode, weight, right_ref, left_ref))
                else:
                    target = c
                    scale = entry(tab, LIVE, c, slots) * couple_step
                    wa, wc = entry(tab, WEIGHT_A, c, slots) * scale, entry(tab, WEIGHT_C, c, slots) * scale
                    mode = operator_of(tab, c, slots, modes)
                    terms.append(parent_pair(stage_ref, 2 * s, mode, wa, wc, right_ref, left_ref))
                targets.append(target)
            for target, pair in zip(targets, terms):
                add(target, pair)


def call(kernel, out_shapes, limit, args, smem=0, us=1.0, scratch=()):
    specs = [pl.BlockSpec(memory_space=SMEM)] * smem
    specs += [pl.BlockSpec(memory_space=VMEM)] * (len(args) - smem)
    return pl.pallas_call(
        kernel,
        out_shape=out_shapes,
        in_specs=specs,
        out_specs=jax.tree.map(lambda _: pl.BlockSpec(memory_space=VMEM), out_shapes),
        scratch_shapes=scratch,
        compiler_params=pltpu.CompilerParams(vmem_limit_bytes=limit),
        cost_estimate=pl.CostEstimate(flops=int(us * 1.1e9), bytes_accessed=1 << 19, transcendentals=0),
    )(*args)


def turn_order(group):
    return sorted(range(1, group), key=lambda k: (bin(k).count("1"), -k))


def shards(sizes, blocks, live_slots, parent_index, bath_mode, hamiltonian, coupling, correlation, damping, link_weight):
    depths, group = sizes
    slots, _, n, _ = blocks.shape
    modes = coupling.shape[0]
    total = group * slots
    limit = 8 * total * 2 * n * n * 4
    order = turn_order(group)
    split_hop = 2 if slots % 2 == 0 else 1
    ranks = range(group)

    def place(d, m):
        return d * group + m

    def permute(value, pairs):
        return lax.ppermute(value, AXES, pairs)

    def gather(value, parity):
        held = {0: value}
        for k in order:
            step = k & -k
            pairs = [(place(d, m), place(d, m ^ step)) for d in range(parity, depths, 2) for m in ranks]
            held[k] = permute(held[k ^ step], pairs)
        return [held[k] for k in ranks]

    def shift(value, step, parity=None):
        pairs = [
            (place(d, m), place(d + step, m))
            for d in range(depths)
            for m in ranks
            if 0 <= d + step < depths and (parity is None or d % 2 == parity)
        ]
        return permute(value, pairs)

    def neighbour(value, parity):
        pairs = [(place(d, m), place(d, m ^ 1)) for d in range(parity, depths, 2) for m in ranks]
        return permute(value, pairs)

    def mats(count, tables=0):
        return jax.ShapeDtypeStruct((count * n + tables * ROWS, n), f32)

    def sds(*shape, dtype=f32):
        return jax.ShapeDtypeStruct(shape, dtype)

    plain = 2 * slots
    stage = VMEM((plain * n, n), f32)

    def tables(count):
        return [SMEM((count, ROWS, LANES), f32), pltpu.SemaphoreType.DMA((count,))]

    operator_shapes = (sds(group * modes, 3 * n, n, dtype=bf16), sds(group * modes, n, 3 * n, dtype=bf16))
    couplings = coupling.reshape(modes * n, n)

    packed, own_table = call(
        pack_kernel,
        (mats(plain + modes, 1), sds(ROWS, n)),
        PACK_LIMIT,
        (live_slots, parent_index, bath_mode, damping, link_weight, correlation, blocks.reshape(plain * n, n), couplings),
        smem=6,
    )
    first = gather(packed, 1)
    near_table = shift(own_table, -1)
    powers = call(
        powers_kernel, (sds(3 * n, ORDER * n, dtype=bf16), sds(n, 3 * ORDER * n, dtype=bf16)), limit, (hamiltonian,)
    )
    *operators_odd, raw = call(
        functools.partial(operators_kernel, slots, group, modes, None),
        (*operator_shapes, mats((group - 1) * modes)),
        limit,
        (couplings, *first),
    )

    def free(states, parity, times, part=0, parts=1, prior=None):
        count = slots // parts
        return call(
            functools.partial(free_kernel, parity, times, slots, part * count),
            mats(2 * count * (1 if prior is None else part + 1)),
            limit,
            (states, *powers) if prior is None else (states, *powers, prior),
            us=4.5 * times / parts,
        )

    def free_parts(states, parity, times):
        return [free(states, parity, times, part, split_hop) for part in range(split_hop)]

    def free_chain(states, parity, times):
        done = None
        for part in range(split_hop):
            done = free(states, parity, times, part, split_hop, done)
        return done

    splits = {group: single(group), len(joined(group)): joined(group)}

    def pick(groups, sender, parts):
        return call(
            functools.partial(pick_kernel, sender, slots, splits[len(groups)], parts),
            [mats(plain // parts)] * parts,
            limit,
            (near_table, *groups),
            scratch=tables(1),
        )

    def send(groups, sender, parts, operators):
        outs = call(
            functools.partial(send_kernel, sender, slots, group, splits[len(groups)], modes, parts),
            [mats(plain // parts)] * parts + [sds(group, ROWS, n)],
            limit,
            (*operators, *groups),
            us=2,
            scratch=[stage, stage, SMEM((total,), jnp.int32), *tables(group)],
        )
        return outs[:parts], outs[-1]

    def join(frees, sums, picks, receiver, operators):
        return call(
            functools.partial(join_kernel, receiver, slots, modes, len(sums), len(picks)),
            mats(plain) if len(frees) > 1 else mats(plain, 1),
            limit,
            (own_table, *operators, *frees, *sums, *picks),
            scratch=tables(1),
        )

    def side(kind, bases, groups, tabs, receiver, operators, second=False, span=None):
        split = splits[len(groups)] if span is None else single(len(groups))
        span = (0, 1, group) if span is None else span
        return call(
            functools.partial(
                side_kernel, kind, receiver, slots, group, modes, span, split, len(bases), len(groups), len(tabs)
            ),
            [mats(plain * len(held), len(held)) for held in joined(group)]
            if second
            else [mats(2 * total), sds(group, ROWS, n)],
            limit,
            (*operators, *bases, *groups, *tabs),
            us=3,
            scratch=[stage, *tables(group + (span[2] if kind == "children" else 0))],
        )

    free_even = free(packed, 0, 1)
    free_odd = [part for k in ranks for part in free_parts(first[k], 1, 2)]
    picks = [shift(value, 1, 1) for value in pick(first, 1, split_hop)]
    sums, tabs_odd = send(first, 1, 1, operators_odd)
    sums = [shift(value, -1, 1) for value in sums]
    passed = shift(raw, -1, 1)
    operators_even = call(
        functools.partial(operators_kernel, slots, group, modes, 0), operator_shapes, limit, (couplings, passed)
    )
    own_state = join([free_even], sums, picks, 0, operators_odd)

    gathered = gather(own_state, 0)
    from_below = [shift(value, -1, 0) for value in gathered]
    from_above = [shift(value, 1, 0) for value in gathered]
    free_even = [free_chain(gathered[0], 0, 2)] + [free(gathered[k], 0, 2) for k in range(2, group, 2)]
    free_even = [value for own in free_even for value in (own, neighbour(own, 0))]
    evens, odds = (0, 2, group // 2), (1, 2, group // 2)
    states, _ = side("children", free_odd, from_below[::2], [tabs_odd], 1, operators_odd, span=evens)
    states, _ = side("parents", [states], from_above, [tabs_odd], 1, operators_odd)
    states = side("children", [states], from_below[1::2], [tabs_odd], 1, operators_odd, second=True, span=odds)

    from_above = [shift(value, 1, 1) for value in states[:2]]
    from_above.append(neighbour(from_above[0], 0))
    from_below = [shift(value, -1, 1) for value in states]
    last_odd = free(states[0], 1, 2)
    states, tabs_even = side("children", free_even, from_below, gathered, 0, operators_even)
    states = side("parents", [states], from_above, [tabs_even], 0, operators_even, second=True)

    sums, _ = send(states, 0, split_hop, operators_even)
    sums = [shift(value, -1, 0) for value in sums]
    picks = [shift(value, 1, 0) for value in pick(states, 0, 1)]
    last_even = free(states[0], 0, 1)
    return join([last_odd, last_even], sums, picks, 1, operators_odd).reshape(blocks.shape)


def solution(mesh):
    sizes = (mesh.shape["depth"], mesh.shape["mode"])

    def whole(*args):
        return shards(sizes, *args)

    return jax.shard_map(
        whole,
        mesh=mesh,
        in_specs=(
            P(("depth", "mode"), None, None, None),
            P(("depth", "mode")),
            P(("depth", "mode")),
            P(("depth", "mode")),
            P(),
            P("mode", None, None),
            P("mode", None),
            P(("depth", "mode")),
            P(("depth", "mode")),
        ),
        out_specs=P(("depth", "mode"), None, None, None),
        check_vma=False,
    )
```

```python
import functools
import math
import jax
import jax.numpy as jnp
from jax import lax
from jax.experimental import pallas as pl
from jax.experimental.pallas import tpu as pltpu
from jax.sharding import PartitionSpec as P

SUBSTEPS = 2
ORDER = 4
substep = 0.7
couple_step = 0.2

AXES = ("depth", "mode")
VMEM = pltpu.VMEM
SMEM = pltpu.SMEM
bf16 = jnp.bfloat16
f32 = jnp.float32

PARENT, MODE, LIVE, FACTOR, WEIGHT, WEIGHT_A, WEIGHT_C = range(7)
ROWS, LANES = 8, 128
PACK_LIMIT = 56 << 20


def split(value):
    high = value.astype(bf16)
    return high, (value - high.astype(f32)).astype(bf16)


def stack_rows(value):
    high, low = split(value)
    return jnp.concatenate([high, high, low], axis=0)


def stack_cols(value):
    high, low = split(value)
    return jnp.concatenate([high, low, high], axis=1)


def dot(first, second):
    return jnp.dot(first, second, preferred_element_type=f32)


def exact(first, second):
    return jnp.dot(first, second, preferred_element_type=f32, precision=lax.Precision.HIGHEST)


def odd_depth():
    return lax.rem(lax.axis_index("depth"), 2)


def rows(at, n, count=1):
    if not isinstance(at, int):
        at = pl.multiple_of(at, ROWS)
    return pl.ds(at, count * n)


def pack_kernel(live_ref, parent_ref, mode_ref, damping_ref, weight_ref, corr_ref, blocks_ref, coupling_ref, out_ref, table_ref):
    slots, n = live_ref.shape[0], blocks_ref.shape[1]
    size = blocks_ref.shape[0]
    out_ref[pl.ds(0, size)] = blocks_ref[...]
    out_ref[pl.ds(size + ROWS, coupling_ref.shape[0])] = coupling_ref[...]
    row = lax.broadcasted_iota(jnp.int32, (ROWS, n), 0)
    lane = lax.broadcasted_iota(jnp.int32, (ROWS, n), 1)
    table = jnp.zeros((ROWS, n), f32)
    first_mode = lax.axis_index("mode") * corr_ref.shape[0]
    for s in range(slots):
        mode = mode_ref[s] - first_mode
        live = live_ref[s].astype(f32)
        weight = weight_ref[s]
        values = {
            PARENT: parent_ref[s].astype(f32),
            MODE: mode.astype(f32),
            LIVE: live,
            FACTOR: damping_ref[s] * (-SUBSTEPS * substep),
            WEIGHT: weight * live,
            WEIGHT_A: weight * corr_ref[mode, 0],
            WEIGHT_C: weight * corr_ref[mode, 1],
        }
        for at, value in values.items():
            table = jnp.where(jnp.logical_and(row == at, lane == s), value, table)
    live_row = table[LIVE : LIVE + 1]
    table = jnp.where(row == FACTOR, live_row * jnp.exp(table), table)
    table_ref[...] = table
    out_ref[pl.ds(size, ROWS)] = table


def powers_kernel(ham_ref, right_ref, left_ref):
    n = ham_ref.shape[0]
    ham = (ham_ref[...] + ham_ref[...].T) * 0.5
    power = ham
    for k in range(1, ORDER + 1):
        if k > 1:
            power = exact(power, ham)
        scaled = power * (substep**k / math.factorial(k))
        right_ref[:, (k - 1) * n : k * n] = stack_rows(scaled)
        left_ref[:, (k - 1) * 3 * n : k * 3 * n] = stack_cols(scaled)


def single(group):
    return [[k] for k in range(group)]


def joined(group):
    return [[0], list(range(2, group)), [1]]


class Layout:
    def __init__(self, refs, slots, split):
        self.refs, self.slots, self.split = refs, slots, split
        self.group = sum(len(held) for held in split)
        self.n = refs[0].shape[1]
        self.size = 2 * slots * self.n
        self.stride = self.size + ROWS

    def base(self, k):
        for ref, held in zip(self.refs, self.split):
            if k in held:
                return ref, held.index(k) * self.stride

    def table(self, k):
        ref, base = self.base(k)
        return ref.at[pl.ds(base + self.size, ROWS), pl.ds(0, LANES)]

    def copy_table(self, k, target_ref, at):
        ref, base = self.base(k)
        target_ref[at] = ref[pl.ds(base + self.size, ROWS)]

    def fetch(self, index, stage_ref, at):
        for k in range(self.group):
            ref, base = self.base(k)
            local = index - k * self.slots

            @pl.when(jnp.logical_and(local >= 0, local < self.slots))
            def _():
                stage_ref[rows(at * self.n, self.n, 2)] = ref[rows(base + 2 * local * self.n, self.n, 2)]


def pull(sources, smem_ref, sem_ref):
    copies = [pltpu.make_async_copy(ref, smem_ref.at[i], sem_ref.at[i]) for i, ref in enumerate(sources)]
    for copy in copies:
        copy.start()
    for copy in copies:
        copy.wait()


def narrow(ref):
    return ref.at[pl.ds(0, ROWS), pl.ds(0, LANES)]


def operators_kernel(slots, group, modes, parity, own_ref, *refs):
    outs = refs[-2 - (parity is None) :]
    sources = refs[: -len(outs)]
    right_ref, left_ref = outs[0], outs[1]
    n = own_ref.shape[1]

    def put(at, value):
        sym = (value + value.T) * 0.5
        right_ref[at] = stack_rows(sym)
        left_ref[at] = stack_cols(sym)

    def own():
        for i in range(modes):
            put(i, own_ref[rows(i * n, n)])

    if parity is None:
        own()
        groups = Layout(sources, slots, single(group))
        for k in range(1, group):
            ref, base = groups.base(k)
            for i in range(modes):
                value = ref[rows(base + groups.stride + i * n, n)]
                put(k * modes + i, value)
                outs[2][rows(((k - 1) * modes + i) * n, n)] = value
    else:

        @pl.when(odd_depth() == parity)
        def _():
            own()
            for at in range(modes, group * modes):
                put(at, sources[0][rows((at - modes) * n, n)])


def taylor(real, imag, right, left):
    n = real.shape[0]
    out = dot(stack_cols(jnp.concatenate([real, imag], axis=0)), right)
    rp = [out[:n, k * n : (k + 1) * n] for k in range(ORDER)]
    ip = [out[n:, k * n : (k + 1) * n] for k in range(ORDER)]
    u_real, u_imag = real, imag
    stacked = [None] * ORDER
    for k in range(ORDER + 1):
        if k:
            turn = k % 4
            if turn == 1:
                u_real, u_imag = u_real - ip[k - 1], u_imag + rp[k - 1]
            elif turn == 2:
                u_real, u_imag = u_real - rp[k - 1], u_imag - ip[k - 1]
            elif turn == 3:
                u_real, u_imag = u_real + ip[k - 1], u_imag - rp[k - 1]
            else:
                u_real, u_imag = u_real + rp[k - 1], u_imag + ip[k - 1]
        j = ORDER - k
        if j:
            turn = j % 4
            if turn == 1:
                pair = (u_imag, -u_real)
            elif turn == 2:
                pair = (-u_real, -u_imag)
            elif turn == 3:
                pair = (-u_imag, u_real)
            else:
                pair = (u_real, u_imag)
            stacked[j - 1] = stack_rows(jnp.concatenate(pair, axis=1))
    done = dot(left, jnp.concatenate(stacked, axis=0))
    return u_real + done[:, :n], u_imag + done[:, n:]


def free_kernel(run_parity, times, slots, first, states_ref, right_ref, left_ref, *refs):
    out_ref = refs[-1]
    n = out_ref.shape[1]
    ahead = first if len(refs) > 1 else 0
    count = out_ref.shape[0] // (2 * n) - ahead
    pair = 2 if count % 2 == 0 else 1

    @pl.when(odd_depth() == run_parity)
    def _():
        right, left = right_ref[...], left_ref[...]
        if ahead:
            out_ref[pl.ds(0, 2 * ahead * n)] = refs[0][...]
        out_ref[pl.ds(2 * ahead * n, 2 * count * n)] = states_ref[pl.ds(2 * first * n, 2 * count * n)]

        @pl.loop(0, count // pair)
        def _(step):
            @pl.loop(0, times * SUBSTEPS)
            def _(turn):
                blocks = [ahead + step * pair + u for u in range(pair)]
                at = [(rows(2 * s * n, n), rows((2 * s + 1) * n, n)) for s in blocks]
                done = [taylor(out_ref[r], out_ref[i], right, left) for r, i in at]
                for (r, i), (real, imag) in zip(at, done):
                    out_ref[r] = real
                    out_ref[i] = imag

        factors = states_ref[pl.ds(2 * slots * n, ROWS)][FACTOR : FACTOR + 1]
        for s in range(count):
            scale = factors[:, first + s : first + s + 1] ** times
            at = rows(2 * (ahead + s) * n, n, 2)
            out_ref[at] = out_ref[at] * scale


def sided(real, imag, right, left):
    n = real.shape[0]
    after = dot(stack_cols(jnp.concatenate([real, imag], axis=0)), right)
    before = dot(left, stack_rows(jnp.concatenate([real, imag], axis=1)))
    return after[:n], after[n:], before[:, :n], before[:, n:]


def entry(tab, row, c, slots):
    if isinstance(c, int):
        return tab[c // slots, row, c % slots]
    return tab[lax.div(c, slots), row, lax.rem(c, slots)]


def operator_of(tab, c, slots, modes):
    back = c // slots if isinstance(c, int) else lax.div(c, slots)
    return back * modes + entry(tab, MODE, c, slots).astype(jnp.int32)


def parent_of(tab, c, slots):
    parent = entry(tab, PARENT, c, slots).astype(jnp.int32)
    back = lax.bitwise_xor(lax.axis_index("mode"), lax.div(parent, slots))
    return back * slots + lax.rem(parent, slots)


def child_pair(stage_ref, at, mode, weight, right_ref, left_ref):
    n = stage_ref.shape[1]
    ra, ia, rb, ib = sided(stage_ref[rows(at * n, n)], stage_ref[rows((at + 1) * n, n)], right_ref[mode], left_ref[mode])
    return weight * (ib - ia), weight * (ra - rb)


def parent_pair(stage_ref, at, mode, wa, wc, right_ref, left_ref):
    n = stage_ref.shape[1]
    ra, ia, rb, ib = sided(stage_ref[rows(at * n, n)], stage_ref[rows((at + 1) * n, n)], right_ref[mode], left_ref[mode])
    return wa * (ib - ia) + wc * (rb + ra), wa * (ra - rb) + wc * (ib + ia)


def add_pair(acc_ref, at, pair):
    n = acc_ref.shape[1]
    for i in range(2):
        where = rows(at + i * n, n)
        acc_ref[where] = acc_ref[where] + pair[i]


def part_of(parts, s):
    size = parts[0].shape[0] // (2 * parts[0].shape[1])
    return parts[s // size], 2 * (s % size)


def pick_kernel(sender, slots, split, parts, near_ref, *refs):
    tab, sem_ref = refs[-2:]
    picks = refs[-2 - parts : -2]
    groups = Layout(refs[: -2 - parts], slots, split)

    @pl.when(odd_depth() == sender)
    def _():
        pull([narrow(near_ref)], tab, sem_ref)
        for s in range(slots):
            pick, at = part_of(picks, s)
            groups.fetch(parent_of(tab, s, slots), pick, at)


def send_kernel(sender, slots, group, split, modes, parts, right_ref, left_ref, *refs):
    acc_ref, stage_ref, list_ref, tab, sem_ref = refs[-5:]
    tabs_ref = refs[-6]
    n = acc_ref.shape[1]
    sums = refs[-6 - parts : -6]
    groups = Layout(refs[: -6 - parts], slots, split)

    @pl.when(odd_depth() == sender)
    def _():
        pull([groups.table(k) for k in range(group)], tab, sem_ref)
        for k in range(group):
            groups.copy_table(k, tabs_ref, k)
        acc_ref[...] = jnp.zeros_like(acc_ref)

        def collect(c, count):
            mine = parent_of(tab, c, slots) < slots

            @pl.when(mine)
            def _():
                list_ref[count] = c

            return count + mine.astype(jnp.int32)

        count = lax.fori_loop(0, group * slots, collect, jnp.int32(0))

        @pl.loop(0, lax.div(count + slots - 1, slots))
        def _(batch):
            children = []
            for u in range(slots):
                place = batch * slots + u
                c = list_ref[jnp.minimum(place, count - 1)]
                groups.fetch(c, stage_ref, 2 * u)
                children.append((c, jnp.where(place < count, entry(tab, WEIGHT, c, slots), 0.0)))
            terms = [
                child_pair(stage_ref, 2 * u, operator_of(tab, c, slots, modes), weight, right_ref, left_ref)
                for u, (c, weight) in enumerate(children)
            ]
            for (c, _), pair in zip(children, terms):
                add_pair(acc_ref, 2 * parent_of(tab, c, slots) * n, pair)

        for s in range(slots):
            part, at = part_of(sums, s)
            part[rows(at * n, n, 2)] = acc_ref[rows(2 * s * n, n, 2)]


def join_kernel(receiver, slots, modes, sum_parts, pick_parts, own_ref, right_ref, left_ref, *refs):
    out_ref, tab, sem_ref = refs[-3:]
    picks = refs[-3 - pick_parts : -3]
    sums = refs[-3 - pick_parts - sum_parts : -3 - pick_parts]
    frees = refs[: -3 - pick_parts - sum_parts]
    n = frees[0].shape[1]

    @pl.when(odd_depth() == receiver)
    def _():
        pull([narrow(own_ref)], tab, sem_ref)
        terms = []
        for s in range(slots if picks else 0):
            pick, at = part_of(picks, s)
            wa, wc = tab[0, WEIGHT_A, s], tab[0, WEIGHT_C, s]
            terms.append(parent_pair(pick, at, operator_of(tab, s, slots, modes), wa, wc, right_ref, left_ref))
        for s in range(slots):
            scale = tab[0, LIVE, s] * couple_step
            for i in range(2):
                here = rows((2 * s + i) * n, n)
                added = terms[s][i] if picks else 0.0
                if sums:
                    part, at = part_of(sums, s)
                    added = part[rows((at + i) * n, n)] + added
                out_ref[here] = frees[0][here] + scale * added
        if out_ref.shape[0] > 2 * slots * n:
            out_ref[pl.ds(2 * slots * n, ROWS)] = own_ref[...]

    if len(frees) > 1:

        @pl.when(odd_depth() != receiver)
        def _():
            out_ref[...] = frees[1][...]


def side_kernel(side, receiver, slots, group, modes, span, split, base_count, group_count, tab_count, right_ref, left_ref, *refs):
    stage_ref, tab, sem_ref = refs[-3:]
    start, step, count = span
    bases = refs[:base_count]
    groups = Layout(refs[base_count : base_count + group_count], slots, split)
    tab_refs = refs[base_count + group_count : base_count + group_count + tab_count]
    outs = refs[base_count + group_count + tab_count : -3]
    second = len(outs[-1].shape) == 2
    n = stage_ref.shape[1]
    size = 2 * slots * n
    gathered = Layout(tab_refs, slots, single(group)) if tab_count > 1 else None
    own_tables = [gathered.table(k) if gathered else tab_refs[0].at[k, pl.ds(0, ROWS), pl.ds(0, LANES)] for k in range(group)]
    out = Layout(outs, slots, joined(group)) if second else None

    @pl.when(odd_depth() == receiver)
    def _():
        below = [groups.table(k) for k in range(count)] if side == "children" else []
        pull(own_tables + below, tab, sem_ref)
        if second:
            for k in range(group):
                ref, base = out.base(k)
                ref[pl.ds(base, size)] = bases[0][pl.ds(k * size, size)]
                ref[pl.ds(base + size, ROWS)] = tab_refs[0][k]
        else:
            offset = 0
            for base in bases:
                outs[0][pl.ds(offset, base.shape[0])] = base[...]
                offset += base.shape[0]
            for k in range(group):
                if gathered:
                    gathered.copy_table(k, outs[1], k)
                else:
                    outs[1][k] = tab_refs[0][k]

        def add(index, pair):
            if not second:
                add_pair(outs[0], 2 * index * n, pair)
                return
            for ref, held in zip(outs, out.split):
                local = index - held[0] * slots
                at = lax.div(local, slots) * out.stride + lax.rem(local, slots) * (2 * n)

                @pl.when(jnp.logical_and(local >= 0, local < len(held) * slots))
                def _():
                    add_pair(ref, at, pair)

        @pl.loop(0, count)
        def _(k):
            at = k * slots
            targets, terms = [], []
            for s in range(slots):
                c = at + s
                groups.fetch(c if side == "children" else parent_of(tab, c, slots), stage_ref, 2 * s)
            for s in range(slots):
                c = at + s
                if side == "children":
                    b = c + group * slots
                    target = parent_of(tab, b, slots)
                    weight = entry(tab, WEIGHT, b, slots) * (entry(tab, LIVE, target, slots) * couple_step)
                    mode = entry(tab, MODE, b, slots).astype(jnp.int32) + (start + k * step) * modes
                    terms.append(child_pair(stage_ref, 2 * s, mode, weight, right_ref, left_ref))
                else:
                    target = c
                    scale = entry(tab, LIVE, c, slots) * couple_step
                    wa, wc = entry(tab, WEIGHT_A, c, slots) * scale, entry(tab, WEIGHT_C, c, slots) * scale
                    mode = operator_of(tab, c, slots, modes)
                    terms.append(parent_pair(stage_ref, 2 * s, mode, wa, wc, right_ref, left_ref))
                targets.append(target)
            for target, pair in zip(targets, terms):
                add(target, pair)


def call(kernel, out_shapes, limit, args, smem=0, us=1.0, scratch=()):
    specs = [pl.BlockSpec(memory_space=SMEM)] * smem
    specs += [pl.BlockSpec(memory_space=VMEM)] * (len(args) - smem)
    return pl.pallas_call(
        kernel,
        out_shape=out_shapes,
        in_specs=specs,
        out_specs=jax.tree.map(lambda _: pl.BlockSpec(memory_space=VMEM), out_shapes),
        scratch_shapes=scratch,
        compiler_params=pltpu.CompilerParams(vmem_limit_bytes=limit),
        cost_estimate=pl.CostEstimate(flops=int(us * 1.1e9), bytes_accessed=1 << 19, transcendentals=0),
    )(*args)


def turn_order(group):
    return sorted(range(1, group), key=lambda k: (bin(k).count("1"), -k))


def shards(sizes, blocks, live_slots, parent_index, bath_mode, hamiltonian, coupling, correlation, damping, link_weight):
    depths, group = sizes
    slots, _, n, _ = blocks.shape
    modes = coupling.shape[0]
    total = group * slots
    limit = 8 * total * 2 * n * n * 4
    order = turn_order(group)
    split_hop = 2 if slots % 2 == 0 else 1
    ranks = range(group)

    def place(d, m):
        return d * group + m

    def permute(value, pairs):
        return lax.ppermute(value, AXES, pairs)

    def gather(value, parity):
        held = {0: value}
        for k in order:
            step = k & -k
            pairs = [(place(d, m), place(d, m ^ step)) for d in range(parity, depths, 2) for m in ranks]
            held[k] = permute(held[k ^ step], pairs)
        return [held[k] for k in ranks]

    def shift(value, step, parity=None):
        pairs = [
            (place(d, m), place(d + step, m))
            for d in range(depths)
            for m in ranks
            if 0 <= d + step < depths and (parity is None or d % 2 == parity)
        ]
        return permute(value, pairs)

    def neighbour(value, parity):
        pairs = [(place(d, m), place(d, m ^ 1)) for d in range(parity, depths, 2) for m in ranks]
        return permute(value, pairs)

    def mats(count, tables=0):
        return jax.ShapeDtypeStruct((count * n + tables * ROWS, n), f32)

    def sds(*shape, dtype=f32):
        return jax.ShapeDtypeStruct(shape, dtype)

    plain = 2 * slots
    stage = VMEM((plain * n, n), f32)

    def tables(count):
        return [SMEM((count, ROWS, LANES), f32), pltpu.SemaphoreType.DMA((count,))]

    operator_shapes = (sds(group * modes, 3 * n, n, dtype=bf16), sds(group * modes, n, 3 * n, dtype=bf16))
    couplings = coupling.reshape(modes * n, n)

    packed, own_table = call(
        pack_kernel,
        (mats(plain + modes, 1), sds(ROWS, n)),
        PACK_LIMIT,
        (live_slots, parent_index, bath_mode, damping, link_weight, correlation, blocks.reshape(plain * n, n), couplings),
        smem=6,
    )
    first = gather(packed, 1)
    near_table = shift(own_table, -1)
    powers = call(
        powers_kernel, (sds(3 * n, ORDER * n, dtype=bf16), sds(n, 3 * ORDER * n, dtype=bf16)), limit, (hamiltonian,)
    )
    *operators_odd, raw = call(
        functools.partial(operators_kernel, slots, group, modes, None),
        (*operator_shapes, mats((group - 1) * modes)),
        limit,
        (couplings, *first),
    )

    def free(states, parity, times, part=0, parts=1, prior=None):
        count = slots // parts
        return call(
            functools.partial(free_kernel, parity, times, slots, part * count),
            mats(2 * count * (1 if prior is None else part + 1)),
            limit,
            (states, *powers) if prior is None else (states, *powers, prior),
            us=4.5 * times / parts,
        )

    def free_parts(states, parity, times):
        return [free(states, parity, times, part, split_hop) for part in range(split_hop)]

    def free_chain(states, parity, times):
        done = None
        for part in range(split_hop):
            done = free(states, parity, times, part, split_hop, done)
        return done

    splits = {group: single(group), len(joined(group)): joined(group)}

    def pick(groups, sender, parts):
        return call(
            functools.partial(pick_kernel, sender, slots, splits[len(groups)], parts),
            [mats(plain // parts)] * parts,
            limit,
            (near_table, *groups),
            scratch=tables(1),
        )

    def send(groups, sender, parts, operators):
        outs = call(
            functools.partial(send_kernel, sender, slots, group, splits[len(groups)], modes, parts),
            [mats(plain // parts)] * parts + [sds(group, ROWS, n)],
            limit,
            (*operators, *groups),
            us=2,
            scratch=[stage, stage, SMEM((total,), jnp.int32), *tables(group)],
        )
        return outs[:parts], outs[-1]

    def join(frees, sums, picks, receiver, operators, noted=0):
        return call(
            functools.partial(join_kernel, receiver, slots, modes, len(sums), len(picks)),
            mats(plain, noted),
            limit,
            (own_table, *operators, *frees, *sums, *picks),
            scratch=tables(1),
        )

    def side(kind, bases, groups, tabs, receiver, operators, second=False, span=None):
        split = splits[len(groups)] if span is None else single(len(groups))
        span = (0, 1, group) if span is None else span
        return call(
            functools.partial(
                side_kernel, kind, receiver, slots, group, modes, span, split, len(bases), len(groups), len(tabs)
            ),
            [mats(plain * len(held), len(held)) for held in joined(group)]
            if second
            else [mats(2 * total), sds(group, ROWS, n)],
            limit,
            (*operators, *bases, *groups, *tabs),
            us=3,
            scratch=[stage, *tables(group + (span[2] if kind == "children" else 0))],
        )

    free_even = free(packed, 0, 1)
    free_odd = [part for k in ranks for part in free_parts(first[k], 1, 2)]
    picks = [shift(value, 1, 1) for value in pick(first, 1, split_hop)]
    sums, tabs_odd = send(first, 1, 1, operators_odd)
    sums = [shift(value, -1, 1) for value in sums]
    passed = shift(raw, -1, 1)
    operators_even = call(
        functools.partial(operators_kernel, slots, group, modes, 0), operator_shapes, limit, (couplings, passed)
    )
    own_state = join([free_even], sums, picks, 0, operators_odd, 1)

    gathered = gather(own_state, 0)
    from_below = [shift(value, -1, 0) for value in gathered]
    from_above = [shift(value, 1, 0) for value in gathered]
    free_even = gather(free_chain(gathered[0], 0, 2), 0)
    evens, odds = (0, 2, group // 2), (1, 2, group // 2)
    states, _ = side("children", free_odd, from_below[::2], [tabs_odd], 1, operators_odd, span=evens)
    states, _ = side("parents", [states], from_above, [tabs_odd], 1, operators_odd)
    states = side("children", [states], from_below[1::2], [tabs_odd], 1, operators_odd, second=True, span=odds)

    from_above = [shift(value, 1, 1) for value in states[:2]]
    from_above.append(neighbour(from_above[0], 0))
    from_below = [shift(value, -1, 1) for value in states]
    last_odd = free(states[0], 1, 2)
    states, tabs_even = side("children", free_even, from_below, gathered, 0, operators_even)
    states = side("parents", [states], from_above, [tabs_even], 0, operators_even, second=True)

    sums, _ = send(states, 0, split_hop, operators_even)
    sums = [shift(value, -1, 0) for value in sums]
    picks = [shift(value, 1, 0) for value in pick(states, 0, 1)]
    last_even = free(states[0], 0, 1)
    last_odd = join([last_odd], [], picks, 1, operators_odd)
    return join([last_odd, last_even], sums, [], 1, operators_odd).reshape(blocks.shape)


def solution(mesh):
    sizes = (mesh.shape["depth"], mesh.shape["mode"])

    def whole(*args):
        return shards(sizes, *args)

    return jax.shard_map(
        whole,
        mesh=mesh,
        in_specs=(
            P(("depth", "mode"), None, None, None),
            P(("depth", "mode")),
            P(("depth", "mode")),
            P(("depth", "mode")),
            P(),
            P("mode", None, None),
            P("mode", None),
            P(("depth", "mode")),
            P(("depth", "mode")),
        ),
        out_specs=P(("depth", "mode"), None, None, None),
        check_vma=False,
    )
```

```python
import functools
import math
import jax
import jax.numpy as jnp
from jax import lax
from jax.experimental import pallas as pl
from jax.experimental.pallas import tpu as pltpu
from jax.sharding import PartitionSpec as P

SUBSTEPS = 2
ORDER = 4
substep = 0.7
couple_step = 0.2

AXES = ("depth", "mode")
VMEM = pltpu.VMEM
SMEM = pltpu.SMEM
bf16 = jnp.bfloat16
f32 = jnp.float32

PARENT, MODE, LIVE, FACTOR, WEIGHT, WEIGHT_A, WEIGHT_C, DIAGONAL = range(8)
ROWS, LANES = 8, 128
PACK_LIMIT = 56 << 20


def split(value):
    high = value.astype(bf16)
    return high, (value - high.astype(f32)).astype(bf16)


def stack_rows(value):
    high, low = split(value)
    return jnp.concatenate([high, high, low], axis=0)


def stack_cols(value):
    high, low = split(value)
    return jnp.concatenate([high, low, high], axis=1)


def dot(first, second):
    return jnp.dot(first, second, preferred_element_type=f32)


def exact(first, second):
    return jnp.dot(first, second, preferred_element_type=f32, precision=lax.Precision.HIGHEST)


def odd_depth():
    return lax.rem(lax.axis_index("depth"), 2)


def rows(at, n, count=1):
    if not isinstance(at, int):
        at = pl.multiple_of(at, ROWS)
    return pl.ds(at, count * n)


def symmetric(value):
    return (value + value.T) * 0.5


def paired(operators):
    return [tuple(operators)] if len(operators) == 2 else operators


def pack_kernel(live_ref, parent_ref, mode_ref, damping_ref, weight_ref, corr_ref, blocks_ref, coupling_ref, out_ref, table_ref):
    slots, n = live_ref.shape[0], blocks_ref.shape[1]
    size = blocks_ref.shape[0]
    out_ref[pl.ds(0, size)] = blocks_ref[...]
    corner_row, corner_lane = (lax.broadcasted_iota(jnp.int32, (n, n), axis) for axis in range(2))
    operators = [symmetric(coupling_ref[pl.ds(i * n, n)]) for i in range(corr_ref.shape[0])]
    for i, value in enumerate(paired(operators)):
        if isinstance(value, tuple):
            value = jnp.where(corner_row <= corner_lane, *value)
        out_ref[pl.ds(size + ROWS + i * n, n)] = value
    row = lax.broadcasted_iota(jnp.int32, (ROWS, n), 0)
    lane = lax.broadcasted_iota(jnp.int32, (ROWS, n), 1)
    table = jnp.zeros((ROWS, n), f32)
    first_mode = lax.axis_index("mode") * corr_ref.shape[0]
    for s in range(slots):
        mode = mode_ref[s] - first_mode
        live = live_ref[s].astype(f32)
        weight = weight_ref[s]
        values = {
            PARENT: parent_ref[s].astype(f32),
            MODE: mode.astype(f32),
            LIVE: live,
            FACTOR: damping_ref[s] * (-SUBSTEPS * substep),
            WEIGHT: weight * live,
            WEIGHT_A: weight * corr_ref[mode, 0],
            WEIGHT_C: weight * corr_ref[mode, 1],
        }
        for at, value in values.items():
            table = jnp.where(jnp.logical_and(row == at, lane == s), value, table)
    for value in paired(operators):
        if isinstance(value, tuple):
            second = jnp.sum(jnp.where(corner_row == corner_lane, value[1], 0.0), axis=0, keepdims=True)
            table = jnp.where(row == DIAGONAL, second, table)
    live_row = table[LIVE : LIVE + 1]
    table = jnp.where(row == FACTOR, live_row * jnp.exp(table), table)
    table_ref[...] = table
    out_ref[pl.ds(size, ROWS)] = table


def powers_kernel(ham_ref, right_ref, left_ref):
    n = ham_ref.shape[0]
    ham = (ham_ref[...] + ham_ref[...].T) * 0.5
    power = ham
    for k in range(1, ORDER + 1):
        if k > 1:
            power = exact(power, ham)
        scaled = power * (substep**k / math.factorial(k))
        right_ref[:, (k - 1) * n : k * n] = stack_rows(scaled)
        left_ref[:, (k - 1) * 3 * n : k * 3 * n] = stack_cols(scaled)


def single(group):
    return [[k] for k in range(group)]


def joined(group):
    return [[0], list(range(2, group)), [1]]


class Layout:
    def __init__(self, refs, slots, split):
        self.refs, self.slots, self.split = refs, slots, split
        self.group = sum(len(held) for held in split)
        self.n = refs[0].shape[1]
        self.size = 2 * slots * self.n
        self.stride = self.size + ROWS

    def base(self, k):
        for ref, held in zip(self.refs, self.split):
            if k in held:
                return ref, held.index(k) * self.stride

    def table(self, k):
        ref, base = self.base(k)
        return ref.at[pl.ds(base + self.size, ROWS), pl.ds(0, LANES)]

    def copy_table(self, k, target_ref, at):
        ref, base = self.base(k)
        target_ref[at] = ref[pl.ds(base + self.size, ROWS)]

    def fetch(self, index, stage_ref, at):
        for k in range(self.group):
            ref, base = self.base(k)
            local = index - k * self.slots

            @pl.when(jnp.logical_and(local >= 0, local < self.slots))
            def _():
                stage_ref[rows(at * self.n, self.n, 2)] = ref[rows(base + 2 * local * self.n, self.n, 2)]


def pull(sources, smem_ref, sem_ref):
    copies = [pltpu.make_async_copy(ref, smem_ref.at[i], sem_ref.at[i]) for i, ref in enumerate(sources)]
    for copy in copies:
        copy.start()
    for copy in copies:
        copy.wait()


def narrow(ref):
    return ref.at[pl.ds(0, ROWS), pl.ds(0, LANES)]


def operators_kernel(slots, group, modes, parity, own_ref, *refs):
    outs = refs[-2 - (parity is None) :]
    sources = refs[: -len(outs)]
    right_ref, left_ref = outs[0], outs[1]
    n = own_ref.shape[1]
    size = 2 * slots * n
    squares = len(paired([None] * modes))
    block = ROWS + squares * n
    row, lane = (lax.broadcasted_iota(jnp.int32, (n, n), axis) for axis in range(2))

    def put(at, sym):
        right_ref[at] = stack_rows(sym)
        left_ref[at] = stack_cols(sym)

    def own():
        for i in range(modes):
            put(i, symmetric(own_ref[rows(i * n, n)]))

    def unpack(k, ref, base):
        if squares == modes:
            for i in range(modes):
                put(k * modes + i, ref[rows(base + ROWS + i * n, n)])
            return
        square = ref[rows(base + ROWS, n)]
        turned = square.T
        diagonal = ref[pl.ds(base, ROWS)][DIAGONAL : DIAGONAL + 1]
        put(k * modes, jnp.where(row <= lane, square, turned))
        put(k * modes + 1, jnp.where(row == lane, diagonal, jnp.where(row > lane, square, turned)))

    if parity is None:
        own()
        for k in range(1, group):
            unpack(k, sources[k], size)
            outs[2][pl.ds((k - 1) * block, block)] = sources[k][pl.ds(size, block)]
    else:

        @pl.when(odd_depth() == parity)
        def _():
            own()
            for k in range(1, group):
                unpack(k, sources[0], (k - 1) * block)


def taylor(real, imag, right, left):
    n = real.shape[0]
    out = dot(stack_cols(jnp.concatenate([real, imag], axis=0)), right)
    rp = [out[:n, k * n : (k + 1) * n] for k in range(ORDER)]
    ip = [out[n:, k * n : (k + 1) * n] for k in range(ORDER)]
    u_real, u_imag = real, imag
    stacked = [None] * ORDER
    for k in range(ORDER + 1):
        if k:
            turn = k % 4
            if turn == 1:
                u_real, u_imag = u_real - ip[k - 1], u_imag + rp[k - 1]
            elif turn == 2:
                u_real, u_imag = u_real - rp[k - 1], u_imag - ip[k - 1]
            elif turn == 3:
                u_real, u_imag = u_real + ip[k - 1], u_imag - rp[k - 1]
            else:
                u_real, u_imag = u_real + rp[k - 1], u_imag + ip[k - 1]
        j = ORDER - k
        if j:
            turn = j % 4
            if turn == 1:
                pair = (u_imag, -u_real)
            elif turn == 2:
                pair = (-u_real, -u_imag)
            elif turn == 3:
                pair = (-u_imag, u_real)
            else:
                pair = (u_real, u_imag)
            stacked[j - 1] = stack_rows(jnp.concatenate(pair, axis=1))
    done = dot(left, jnp.concatenate(stacked, axis=0))
    return u_real + done[:, :n], u_imag + done[:, n:]


def free_kernel(run_parity, times, slots, first, states_ref, right_ref, left_ref, *refs):
    out_ref = refs[-1]
    n = out_ref.shape[1]
    ahead = first if len(refs) > 1 else 0
    count = out_ref.shape[0] // (2 * n) - ahead
    pair = 2 if count % 2 == 0 else 1

    @pl.when(odd_depth() == run_parity)
    def _():
        right, left = right_ref[...], left_ref[...]
        if ahead:
            out_ref[pl.ds(0, 2 * ahead * n)] = refs[0][...]
        out_ref[pl.ds(2 * ahead * n, 2 * count * n)] = states_ref[pl.ds(2 * first * n, 2 * count * n)]

        @pl.loop(0, count // pair)
        def _(step):
            @pl.loop(0, times * SUBSTEPS)
            def _(turn):
                blocks = [ahead + step * pair + u for u in range(pair)]
                at = [(rows(2 * s * n, n), rows((2 * s + 1) * n, n)) for s in blocks]
                done = [taylor(out_ref[r], out_ref[i], right, left) for r, i in at]
                for (r, i), (real, imag) in zip(at, done):
                    out_ref[r] = real
                    out_ref[i] = imag

        factors = states_ref[pl.ds(2 * slots * n, ROWS)][FACTOR : FACTOR + 1]
        for s in range(count):
            scale = factors[:, first + s : first + s + 1] ** times
            at = rows(2 * (ahead + s) * n, n, 2)
            out_ref[at] = out_ref[at] * scale


def sided(real, imag, right, left):
    n = real.shape[0]
    after = dot(stack_cols(jnp.concatenate([real, imag], axis=0)), right)
    before = dot(left, stack_rows(jnp.concatenate([real, imag], axis=1)))
    return after[:n], after[n:], before[:, :n], before[:, n:]


def entry(tab, row, c, slots):
    if isinstance(c, int):
        return tab[c // slots, row, c % slots]
    return tab[lax.div(c, slots), row, lax.rem(c, slots)]


def operator_of(tab, c, slots, modes):
    back = c // slots if isinstance(c, int) else lax.div(c, slots)
    return back * modes + entry(tab, MODE, c, slots).astype(jnp.int32)


def parent_of(tab, c, slots):
    parent = entry(tab, PARENT, c, slots).astype(jnp.int32)
    back = lax.bitwise_xor(lax.axis_index("mode"), lax.div(parent, slots))
    return back * slots + lax.rem(parent, slots)


def child_pair(stage_ref, at, mode, weight, right_ref, left_ref):
    n = stage_ref.shape[1]
    ra, ia, rb, ib = sided(stage_ref[rows(at * n, n)], stage_ref[rows((at + 1) * n, n)], right_ref[mode], left_ref[mode])
    return weight * (ib - ia), weight * (ra - rb)


def parent_pair(stage_ref, at, mode, wa, wc, right_ref, left_ref):
    n = stage_ref.shape[1]
    ra, ia, rb, ib = sided(stage_ref[rows(at * n, n)], stage_ref[rows((at + 1) * n, n)], right_ref[mode], left_ref[mode])
    return wa * (ib - ia) + wc * (rb + ra), wa * (ra - rb) + wc * (ib + ia)


def add_pair(acc_ref, at, pair):
    n = acc_ref.shape[1]
    for i in range(2):
        where = rows(at + i * n, n)
        acc_ref[where] = acc_ref[where] + pair[i]


def part_of(parts, s):
    size = parts[0].shape[0] // (2 * parts[0].shape[1])
    return parts[s // size], 2 * (s % size)


def pick_kernel(sender, slots, split, parts, near_ref, *refs):
    tab, sem_ref = refs[-2:]
    picks = refs[-2 - parts : -2]
    groups = Layout(refs[: -2 - parts], slots, split)

    @pl.when(odd_depth() == sender)
    def _():
        pull([narrow(near_ref)], tab, sem_ref)
        for s in range(slots):
            pick, at = part_of(picks, s)
            groups.fetch(parent_of(tab, s, slots), pick, at)


def send_kernel(sender, slots, group, split, modes, parts, right_ref, left_ref, *refs):
    acc_ref, stage_ref, list_ref, tab, sem_ref = refs[-5:]
    tabs_ref = refs[-6]
    n = acc_ref.shape[1]
    sums = refs[-6 - parts : -6]
    groups = Layout(refs[: -6 - parts], slots, split)

    @pl.when(odd_depth() == sender)
    def _():
        pull([groups.table(k) for k in range(group)], tab, sem_ref)
        for k in range(group):
            groups.copy_table(k, tabs_ref, k)
        acc_ref[...] = jnp.zeros_like(acc_ref)

        def collect(c, count):
            mine = parent_of(tab, c, slots) < slots

            @pl.when(mine)
            def _():
                list_ref[count] = c

            return count + mine.astype(jnp.int32)

        count = lax.fori_loop(0, group * slots, collect, jnp.int32(0))

        @pl.loop(0, lax.div(count + slots - 1, slots))
        def _(batch):
            children = []
            for u in range(slots):
                place = batch * slots + u
                c = list_ref[jnp.minimum(place, count - 1)]
                groups.fetch(c, stage_ref, 2 * u)
                children.append((c, jnp.where(place < count, entry(tab, WEIGHT, c, slots), 0.0)))
            terms = [
                child_pair(stage_ref, 2 * u, operator_of(tab, c, slots, modes), weight, right_ref, left_ref)
                for u, (c, weight) in enumerate(children)
            ]
            for (c, _), pair in zip(children, terms):
                add_pair(acc_ref, 2 * parent_of(tab, c, slots) * n, pair)

        for s in range(slots):
            part, at = part_of(sums, s)
            part[rows(at * n, n, 2)] = acc_ref[rows(2 * s * n, n, 2)]


def join_kernel(receiver, slots, modes, sum_parts, pick_parts, own_ref, right_ref, left_ref, *refs):
    out_ref, tab, sem_ref = refs[-3:]
    picks = refs[-3 - pick_parts : -3]
    sums = refs[-3 - pick_parts - sum_parts : -3 - pick_parts]
    frees = refs[: -3 - pick_parts - sum_parts]
    n = frees[0].shape[1]

    @pl.when(odd_depth() == receiver)
    def _():
        pull([narrow(own_ref)], tab, sem_ref)
        terms = []
        for s in range(slots if picks else 0):
            pick, at = part_of(picks, s)
            wa, wc = tab[0, WEIGHT_A, s], tab[0, WEIGHT_C, s]
            terms.append(parent_pair(pick, at, operator_of(tab, s, slots, modes), wa, wc, right_ref, left_ref))
        for s in range(slots):
            scale = tab[0, LIVE, s] * couple_step
            for i in range(2):
                here = rows((2 * s + i) * n, n)
                added = terms[s][i] if picks else 0.0
                if sums:
                    part, at = part_of(sums, s)
                    added = part[rows((at + i) * n, n)] + added
                out_ref[here] = frees[0][here] + scale * added
        if out_ref.shape[0] > 2 * slots * n:
            out_ref[pl.ds(2 * slots * n, ROWS)] = own_ref[...]

    if len(frees) > 1:

        @pl.when(odd_depth() != receiver)
        def _():
            out_ref[...] = frees[1][...]


def side_kernel(side, receiver, slots, group, modes, span, split, base_count, group_count, tab_count, right_ref, left_ref, *refs):
    stage_ref, tab, sem_ref = refs[-3:]
    start, step, count = span
    bases = refs[:base_count]
    groups = Layout(refs[base_count : base_count + group_count], slots, split)
    tab_refs = refs[base_count + group_count : base_count + group_count + tab_count]
    outs = refs[base_count + group_count + tab_count : -3]
    second = len(outs[-1].shape) == 2
    n = stage_ref.shape[1]
    size = 2 * slots * n
    gathered = Layout(tab_refs, slots, single(group)) if tab_count > 1 else None
    own_tables = [gathered.table(k) if gathered else tab_refs[0].at[k, pl.ds(0, ROWS), pl.ds(0, LANES)] for k in range(group)]
    out = Layout(outs, slots, joined(group)) if second else None

    @pl.when(odd_depth() == receiver)
    def _():
        below = [groups.table(k) for k in range(count)] if side == "children" else []
        pull(own_tables + below, tab, sem_ref)
        if second:
            for k in range(group):
                ref, base = out.base(k)
                start_value = bases[0][pl.ds(k * size, size)]
                if base_count > 1:
                    start_value = start_value + bases[1 + k][...]
                ref[pl.ds(base, size)] = start_value
                ref[pl.ds(base + size, ROWS)] = tab_refs[0][k]
        else:
            offset = 0
            if not bases:
                outs[0][...] = jnp.zeros_like(outs[0])
            for base in bases:
                outs[0][pl.ds(offset, base.shape[0])] = base[...]
                offset += base.shape[0]
            for k in range(group):
                if gathered:
                    gathered.copy_table(k, outs[1], k)
                else:
                    outs[1][k] = tab_refs[0][k]

        def add(index, pair):
            if not second:
                add_pair(outs[0], 2 * index * n, pair)
                return
            for ref, held in zip(outs, out.split):
                local = index - held[0] * slots
                at = lax.div(local, slots) * out.stride + lax.rem(local, slots) * (2 * n)

                @pl.when(jnp.logical_and(local >= 0, local < len(held) * slots))
                def _():
                    add_pair(ref, at, pair)

        @pl.loop(0, count)
        def _(k):
            at = k * slots
            targets, terms = [], []
            for s in range(slots):
                c = at + s
                groups.fetch(c if side == "children" else parent_of(tab, c, slots), stage_ref, 2 * s)
            for s in range(slots):
                c = at + s
                if side == "children":
                    b = c + group * slots
                    target = parent_of(tab, b, slots)
                    weight = entry(tab, WEIGHT, b, slots) * (entry(tab, LIVE, target, slots) * couple_step)
                    mode = entry(tab, MODE, b, slots).astype(jnp.int32) + (start + k * step) * modes
                    terms.append(child_pair(stage_ref, 2 * s, mode, weight, right_ref, left_ref))
                else:
                    target = c
                    scale = entry(tab, LIVE, c, slots) * couple_step
                    wa, wc = entry(tab, WEIGHT_A, c, slots) * scale, entry(tab, WEIGHT_C, c, slots) * scale
                    mode = operator_of(tab, c, slots, modes)
                    terms.append(parent_pair(stage_ref, 2 * s, mode, wa, wc, right_ref, left_ref))
                targets.append(target)
            for target, pair in zip(targets, terms):
                add(target, pair)


def call(kernel, out_shapes, limit, args, smem=0, us=1.0, scratch=()):
    specs = [pl.BlockSpec(memory_space=SMEM)] * smem
    specs += [pl.BlockSpec(memory_space=VMEM)] * (len(args) - smem)
    return pl.pallas_call(
        kernel,
        out_shape=out_shapes,
        in_specs=specs,
        out_specs=jax.tree.map(lambda _: pl.BlockSpec(memory_space=VMEM), out_shapes),
        scratch_shapes=scratch,
        compiler_params=pltpu.CompilerParams(vmem_limit_bytes=limit),
        cost_estimate=pl.CostEstimate(flops=int(us * 1.1e9), bytes_accessed=1 << 19, transcendentals=0),
    )(*args)


def turn_order(group):
    return sorted(range(1, group), key=lambda k: (bin(k).count("1"), -k))


def shards(sizes, blocks, live_slots, parent_index, bath_mode, hamiltonian, coupling, correlation, damping, link_weight):
    depths, group = sizes
    slots, _, n, _ = blocks.shape
    modes = coupling.shape[0]
    total = group * slots
    limit = 8 * total * 2 * n * n * 4
    order = turn_order(group)
    split_hop = 2 if slots % 2 == 0 else 1
    ranks = range(group)

    def place(d, m):
        return d * group + m

    def permute(value, pairs):
        return lax.ppermute(value, AXES, pairs)

    def gather(value, parity):
        held = {0: value}
        for k in order:
            step = k & -k
            pairs = [(place(d, m), place(d, m ^ step)) for d in range(parity, depths, 2) for m in ranks]
            held[k] = permute(held[k ^ step], pairs)
        return [held[k] for k in ranks]

    def shift(value, step, parity=None):
        pairs = [
            (place(d, m), place(d + step, m))
            for d in range(depths)
            for m in ranks
            if 0 <= d + step < depths and (parity is None or d % 2 == parity)
        ]
        return permute(value, pairs)

    def neighbour(value, parity):
        pairs = [(place(d, m), place(d, m ^ 1)) for d in range(parity, depths, 2) for m in ranks]
        return permute(value, pairs)

    def mats(count, tables=0):
        return jax.ShapeDtypeStruct((count * n + tables * ROWS, n), f32)

    def sds(*shape, dtype=f32):
        return jax.ShapeDtypeStruct(shape, dtype)

    plain = 2 * slots
    stage = VMEM((plain * n, n), f32)

    def tables(count):
        return [SMEM((count, ROWS, LANES), f32), pltpu.SemaphoreType.DMA((count,))]

    operator_shapes = (sds(group * modes, 3 * n, n, dtype=bf16), sds(group * modes, n, 3 * n, dtype=bf16))
    couplings = coupling.reshape(modes * n, n)
    squares = len(paired([None] * modes))

    packed, own_table = call(
        pack_kernel,
        (mats(plain + squares, 1), sds(ROWS, n)),
        PACK_LIMIT,
        (live_slots, parent_index, bath_mode, damping, link_weight, correlation, blocks.reshape(plain * n, n), couplings),
        smem=6,
    )
    first = gather(packed, 1)
    near_table = shift(own_table, -1)
    powers = call(
        powers_kernel, (sds(3 * n, ORDER * n, dtype=bf16), sds(n, 3 * ORDER * n, dtype=bf16)), limit, (hamiltonian,)
    )
    *operators_odd, raw = call(
        functools.partial(operators_kernel, slots, group, modes, None),
        (*operator_shapes, mats((group - 1) * squares, group - 1)),
        limit,
        (couplings, *first),
    )

    def free(states, parity, times, part=0, parts=1, prior=None):
        count = slots // parts
        return call(
            functools.partial(free_kernel, parity, times, slots, part * count),
            mats(2 * count * (1 if prior is None else part + 1)),
            limit,
            (states, *powers) if prior is None else (states, *powers, prior),
            us=4.5 * times / parts,
        )

    def free_parts(states, parity, times):
        return [free(states, parity, times, part, split_hop) for part in range(split_hop)]

    def free_chain(states, parity, times):
        done = None
        for part in range(split_hop):
            done = free(states, parity, times, part, split_hop, done)
        return done

    splits = {group: single(group), len(joined(group)): joined(group)}

    def pick(groups, sender, parts):
        return call(
            functools.partial(pick_kernel, sender, slots, splits[len(groups)], parts),
            [mats(plain // parts)] * parts,
            limit,
            (near_table, *groups),
            scratch=tables(1),
        )

    def send(groups, sender, parts, operators):
        outs = call(
            functools.partial(send_kernel, sender, slots, group, splits[len(groups)], modes, parts),
            [mats(plain // parts)] * parts + [sds(group, ROWS, n)],
            limit,
            (*operators, *groups),
            us=2,
            scratch=[stage, stage, SMEM((total,), jnp.int32), *tables(group)],
        )
        return outs[:parts], outs[-1]

    def join(frees, sums, picks, receiver, operators, noted=0):
        return call(
            functools.partial(join_kernel, receiver, slots, modes, len(sums), len(picks)),
            mats(plain, noted),
            limit,
            (own_table, *operators, *frees, *sums, *picks),
            scratch=tables(1),
        )

    def side(kind, bases, groups, tabs, receiver, operators, second=False, span=None):
        split = splits[len(groups)] if span is None else single(len(groups))
        span = (0, 1, group) if span is None else span
        return call(
            functools.partial(
                side_kernel, kind, receiver, slots, group, modes, span, split, len(bases), len(groups), len(tabs)
            ),
            [mats(plain * len(held), len(held)) for held in joined(group)]
            if second
            else [mats(2 * total), sds(group, ROWS, n)],
            limit,
            (*operators, *bases, *groups, *tabs),
            us=3,
            scratch=[stage, *tables(group + (span[2] if kind == "children" else 0))],
        )

    free_even = free(packed, 0, 1)
    free_odd = [part for k in ranks for part in free_parts(first[k], 1, 2)]
    picks = [shift(value, 1, 1) for value in pick(first, 1, split_hop)]
    sums, tabs_odd = send(first, 1, 1, operators_odd)
    sums = [shift(value, -1, 1) for value in sums]
    passed = shift(raw, -1, 1)
    operators_even = call(
        functools.partial(operators_kernel, slots, group, modes, 0), operator_shapes, limit, (couplings, passed)
    )
    own_state = join([free_even], sums, picks, 0, operators_odd, 1)

    gathered = gather(own_state, 0)
    from_below = [shift(value, -1, 0) for value in gathered]
    from_above = [shift(value, 1, 0) for value in gathered]
    free_even = gather(free_chain(gathered[0], 0, 2), 0)
    evens, odds = (0, 2, group // 2), (1, 2, group // 2)
    states, _ = side("children", free_odd, from_below[::2], [tabs_odd], 1, operators_odd, span=evens)
    states, _ = side("parents", [states], from_above, [tabs_odd], 1, operators_odd)
    states = side("children", [states], from_below[1::2], [tabs_odd], 1, operators_odd, second=True, span=odds)

    from_above = [shift(value, 1, 1) for value in states[:2]]
    from_above.append(neighbour(from_above[0], 0))
    from_below = [shift(value, -1, 1) for value in states]
    last_odd = free(states[0], 1, 2)
    states, tabs_even = side("children", [], from_below, gathered, 0, operators_even)
    states = side("parents", [states, *free_even], from_above, [tabs_even], 0, operators_even, second=True)

    sums, _ = send(states, 0, split_hop, operators_even)
    sums = [shift(value, -1, 0) for value in sums]
    picks = [shift(value, 1, 0) for value in pick(states, 0, 1)]
    last_even = free(states[0], 0, 1)
    last_odd = join([last_odd], [], picks, 1, operators_odd)
    return join([last_odd, last_even], sums, [], 1, operators_odd).reshape(blocks.shape)


def solution(mesh):
    sizes = (mesh.shape["depth"], mesh.shape["mode"])

    def whole(*args):
        return shards(sizes, *args)

    return jax.shard_map(
        whole,
        mesh=mesh,
        in_specs=(
            P(("depth", "mode"), None, None, None),
            P(("depth", "mode")),
            P(("depth", "mode")),
            P(("depth", "mode")),
            P(),
            P("mode", None, None),
            P("mode", None),
            P(("depth", "mode")),
            P(("depth", "mode")),
        ),
        out_specs=P(("depth", "mode"), None, None, None),
        check_vma=False,
    )
```

```python
import functools
import math
import jax
import jax.numpy as jnp
from jax import lax
from jax.experimental import pallas as pl
from jax.experimental.pallas import tpu as pltpu
from jax.sharding import PartitionSpec as P

SUBSTEPS = 2
ORDER = 4
substep = 0.7
couple_step = 0.2

AXES = ("depth", "mode")
VMEM = pltpu.VMEM
SMEM = pltpu.SMEM
bf16 = jnp.bfloat16
f32 = jnp.float32

PARENT, MODE, LIVE, FACTOR, WEIGHT, WEIGHT_A, WEIGHT_C, DIAGONAL = range(8)
ROWS, LANES = 8, 128
PACK_LIMIT = 56 << 20


def split(value):
    high = value.astype(bf16)
    return high, (value - high.astype(f32)).astype(bf16)


def stack_rows(value):
    high, low = split(value)
    return jnp.concatenate([high, high, low], axis=0)


def stack_cols(value):
    high, low = split(value)
    return jnp.concatenate([high, low, high], axis=1)


def dot(first, second):
    return jnp.dot(first, second, preferred_element_type=f32)


def exact(first, second):
    return jnp.dot(first, second, preferred_element_type=f32, precision=lax.Precision.HIGHEST)


def odd_depth():
    return lax.rem(lax.axis_index("depth"), 2)


def rows(at, n, count=1):
    if not isinstance(at, int):
        at = pl.multiple_of(at, ROWS)
    return pl.ds(at, count * n)


def symmetric(value):
    return (value + value.T) * 0.5


def paired(operators):
    return [tuple(operators)] if len(operators) == 2 else operators


def pack_kernel(live_ref, parent_ref, mode_ref, damping_ref, weight_ref, corr_ref, blocks_ref, coupling_ref, out_ref, table_ref):
    slots, n = live_ref.shape[0], blocks_ref.shape[1]
    size = blocks_ref.shape[0]
    out_ref[pl.ds(0, size)] = blocks_ref[...]
    corner_row, corner_lane = (lax.broadcasted_iota(jnp.int32, (n, n), axis) for axis in range(2))
    operators = [symmetric(coupling_ref[pl.ds(i * n, n)]) for i in range(corr_ref.shape[0])]
    for i, value in enumerate(paired(operators)):
        if isinstance(value, tuple):
            value = jnp.where(corner_row <= corner_lane, *value)
        out_ref[pl.ds(size + ROWS + i * n, n)] = value
    row = lax.broadcasted_iota(jnp.int32, (ROWS, n), 0)
    lane = lax.broadcasted_iota(jnp.int32, (ROWS, n), 1)
    table = jnp.zeros((ROWS, n), f32)
    first_mode = lax.axis_index("mode") * corr_ref.shape[0]
    for s in range(slots):
        mode = mode_ref[s] - first_mode
        live = live_ref[s].astype(f32)
        weight = weight_ref[s]
        values = {
            PARENT: parent_ref[s].astype(f32),
            MODE: mode.astype(f32),
            LIVE: live,
            FACTOR: damping_ref[s] * (-SUBSTEPS * substep),
            WEIGHT: weight * live,
            WEIGHT_A: weight * corr_ref[mode, 0],
            WEIGHT_C: weight * corr_ref[mode, 1],
        }
        for at, value in values.items():
            table = jnp.where(jnp.logical_and(row == at, lane == s), value, table)
    for value in paired(operators):
        if isinstance(value, tuple):
            second = jnp.sum(jnp.where(corner_row == corner_lane, value[1], 0.0), axis=0, keepdims=True)
            table = jnp.where(row == DIAGONAL, second, table)
    live_row = table[LIVE : LIVE + 1]
    table = jnp.where(row == FACTOR, live_row * jnp.exp(table), table)
    table_ref[...] = table
    out_ref[pl.ds(size, ROWS)] = table


def powers_kernel(ham_ref, right_ref, left_ref):
    n = ham_ref.shape[0]
    ham = (ham_ref[...] + ham_ref[...].T) * 0.5
    power = ham
    for k in range(1, ORDER + 1):
        if k > 1:
            power = exact(power, ham)
        scaled = power * (substep**k / math.factorial(k))
        right_ref[:, (k - 1) * n : k * n] = stack_rows(scaled)
        left_ref[:, (k - 1) * 3 * n : k * 3 * n] = stack_cols(scaled)


def single(group):
    return [[k] for k in range(group)]


def joined(group):
    return [[0], list(range(2, group)), [1]]


class Layout:
    def __init__(self, refs, slots, split):
        self.refs, self.slots, self.split = refs, slots, split
        self.group = sum(len(held) for held in split)
        self.n = refs[0].shape[1]
        self.size = 2 * slots * self.n
        self.stride = self.size + ROWS

    def base(self, k):
        for ref, held in zip(self.refs, self.split):
            if k in held:
                return ref, held.index(k) * self.stride

    def table(self, k):
        ref, base = self.base(k)
        return ref.at[pl.ds(base + self.size, ROWS), pl.ds(0, LANES)]

    def copy_table(self, k, target_ref, at):
        ref, base = self.base(k)
        target_ref[at] = ref[pl.ds(base + self.size, ROWS)]

    def fetch(self, index, stage_ref, at):
        for k in range(self.group):
            ref, base = self.base(k)
            local = index - k * self.slots

            @pl.when(jnp.logical_and(local >= 0, local < self.slots))
            def _():
                stage_ref[rows(at * self.n, self.n, 2)] = ref[rows(base + 2 * local * self.n, self.n, 2)]


def pull(sources, smem_ref, sem_ref):
    copies = [pltpu.make_async_copy(ref, smem_ref.at[i], sem_ref.at[i]) for i, ref in enumerate(sources)]
    for copy in copies:
        copy.start()
    for copy in copies:
        copy.wait()


def narrow(ref):
    return ref.at[pl.ds(0, ROWS), pl.ds(0, LANES)]


def operators_kernel(slots, group, modes, parity, own_ref, *refs):
    outs = refs[-2 - (parity is None) :]
    sources = refs[: -len(outs)]
    right_ref, left_ref = outs[0], outs[1]
    n = own_ref.shape[1]
    size = 2 * slots * n
    squares = len(paired([None] * modes))
    block = ROWS + squares * n
    row, lane = (lax.broadcasted_iota(jnp.int32, (n, n), axis) for axis in range(2))

    def put(at, sym):
        right_ref[at] = stack_rows(sym)
        left_ref[at] = stack_cols(sym)

    def own():
        for i in range(modes):
            put(i, symmetric(own_ref[rows(i * n, n)]))

    def unpack(k, ref, base):
        if squares == modes:
            for i in range(modes):
                put(k * modes + i, ref[rows(base + ROWS + i * n, n)])
            return
        square = ref[rows(base + ROWS, n)]
        turned = square.T
        diagonal = ref[pl.ds(base, ROWS)][DIAGONAL : DIAGONAL + 1]
        put(k * modes, jnp.where(row <= lane, square, turned))
        put(k * modes + 1, jnp.where(row == lane, diagonal, jnp.where(row > lane, square, turned)))

    if parity is None:
        own()
        for k in range(1, group):
            unpack(k, sources[k], size)
            outs[2][pl.ds((k - 1) * block, block)] = sources[k][pl.ds(size, block)]
    else:

        @pl.when(odd_depth() == parity)
        def _():
            own()
            for k in range(1, group):
                unpack(k, sources[0], (k - 1) * block)


def taylor(real, imag, right, left):
    n = real.shape[0]
    out = dot(stack_cols(jnp.concatenate([real, imag], axis=0)), right)
    rp = [out[:n, k * n : (k + 1) * n] for k in range(ORDER)]
    ip = [out[n:, k * n : (k + 1) * n] for k in range(ORDER)]
    u_real, u_imag = real, imag
    stacked = [None] * ORDER
    for k in range(ORDER + 1):
        if k:
            turn = k % 4
            if turn == 1:
                u_real, u_imag = u_real - ip[k - 1], u_imag + rp[k - 1]
            elif turn == 2:
                u_real, u_imag = u_real - rp[k - 1], u_imag - ip[k - 1]
            elif turn == 3:
                u_real, u_imag = u_real + ip[k - 1], u_imag - rp[k - 1]
            else:
                u_real, u_imag = u_real + rp[k - 1], u_imag + ip[k - 1]
        j = ORDER - k
        if j:
            turn = j % 4
            if turn == 1:
                pair = (u_imag, -u_real)
            elif turn == 2:
                pair = (-u_real, -u_imag)
            elif turn == 3:
                pair = (-u_imag, u_real)
            else:
                pair = (u_real, u_imag)
            stacked[j - 1] = stack_rows(jnp.concatenate(pair, axis=1))
    done = dot(left, jnp.concatenate(stacked, axis=0))
    return u_real + done[:, :n], u_imag + done[:, n:]


def free_kernel(run_parity, times, slots, first, states_ref, right_ref, left_ref, *refs):
    out_ref = refs[-1]
    n = out_ref.shape[1]
    ahead = first if len(refs) > 1 else 0
    count = out_ref.shape[0] // (2 * n) - ahead
    pair = 2 if count % 2 == 0 else 1

    @pl.when(odd_depth() == run_parity)
    def _():
        right, left = right_ref[...], left_ref[...]
        if ahead:
            out_ref[pl.ds(0, 2 * ahead * n)] = refs[0][...]
        out_ref[pl.ds(2 * ahead * n, 2 * count * n)] = states_ref[pl.ds(2 * first * n, 2 * count * n)]

        @pl.loop(0, count // pair)
        def _(step):
            @pl.loop(0, times * SUBSTEPS)
            def _(turn):
                blocks = [ahead + step * pair + u for u in range(pair)]
                at = [(rows(2 * s * n, n), rows((2 * s + 1) * n, n)) for s in blocks]
                done = [taylor(out_ref[r], out_ref[i], right, left) for r, i in at]
                for (r, i), (real, imag) in zip(at, done):
                    out_ref[r] = real
                    out_ref[i] = imag

        factors = states_ref[pl.ds(2 * slots * n, ROWS)][FACTOR : FACTOR + 1]
        for s in range(count):
            scale = factors[:, first + s : first + s + 1] ** times
            at = rows(2 * (ahead + s) * n, n, 2)
            out_ref[at] = out_ref[at] * scale


def sided(real, imag, right, left):
    n = real.shape[0]
    after = dot(stack_cols(jnp.concatenate([real, imag], axis=0)), right)
    before = dot(left, stack_rows(jnp.concatenate([real, imag], axis=1)))
    return after[:n], after[n:], before[:, :n], before[:, n:]


def entry(tab, row, c, slots):
    if isinstance(c, int):
        return tab[c // slots, row, c % slots]
    return tab[lax.div(c, slots), row, lax.rem(c, slots)]


def operator_of(tab, c, slots, modes):
    back = c // slots if isinstance(c, int) else lax.div(c, slots)
    return back * modes + entry(tab, MODE, c, slots).astype(jnp.int32)


def parent_of(tab, c, slots):
    parent = entry(tab, PARENT, c, slots).astype(jnp.int32)
    back = lax.bitwise_xor(lax.axis_index("mode"), lax.div(parent, slots))
    return back * slots + lax.rem(parent, slots)


def child_pair(stage_ref, at, mode, weight, right_ref, left_ref):
    n = stage_ref.shape[1]
    ra, ia, rb, ib = sided(stage_ref[rows(at * n, n)], stage_ref[rows((at + 1) * n, n)], right_ref[mode], left_ref[mode])
    return weight * (ib - ia), weight * (ra - rb)


def parent_pair(stage_ref, at, mode, wa, wc, right_ref, left_ref):
    n = stage_ref.shape[1]
    ra, ia, rb, ib = sided(stage_ref[rows(at * n, n)], stage_ref[rows((at + 1) * n, n)], right_ref[mode], left_ref[mode])
    return wa * (ib - ia) + wc * (rb + ra), wa * (ra - rb) + wc * (ib + ia)


def add_pair(acc_ref, at, pair):
    n = acc_ref.shape[1]
    for i in range(2):
        where = rows(at + i * n, n)
        acc_ref[where] = acc_ref[where] + pair[i]


def part_of(parts, s):
    size = parts[0].shape[0] // (2 * parts[0].shape[1])
    return parts[s // size], 2 * (s % size)


def pick_kernel(sender, slots, split, parts, near_ref, *refs):
    tab, sem_ref = refs[-2:]
    picks = refs[-2 - parts : -2]
    groups = Layout(refs[: -2 - parts], slots, split)

    @pl.when(odd_depth() == sender)
    def _():
        pull([narrow(near_ref)], tab, sem_ref)
        for s in range(slots):
            pick, at = part_of(picks, s)
            groups.fetch(parent_of(tab, s, slots), pick, at)


def send_kernel(sender, slots, group, split, modes, parts, right_ref, left_ref, *refs):
    acc_ref, stage_ref, list_ref, tab, sem_ref = refs[-5:]
    tabs_ref = refs[-6]
    n = acc_ref.shape[1]
    sums = refs[-6 - parts : -6]
    groups = Layout(refs[: -6 - parts], slots, split)

    @pl.when(odd_depth() == sender)
    def _():
        pull([groups.table(k) for k in range(group)], tab, sem_ref)
        for k in range(group):
            groups.copy_table(k, tabs_ref, k)
        acc_ref[...] = jnp.zeros_like(acc_ref)

        def collect(c, count):
            mine = parent_of(tab, c, slots) < slots

            @pl.when(mine)
            def _():
                list_ref[count] = c

            return count + mine.astype(jnp.int32)

        count = lax.fori_loop(0, group * slots, collect, jnp.int32(0))

        @pl.loop(0, lax.div(count + slots - 1, slots))
        def _(batch):
            children = []
            for u in range(slots):
                place = batch * slots + u
                c = list_ref[jnp.minimum(place, count - 1)]
                groups.fetch(c, stage_ref, 2 * u)
                children.append((c, jnp.where(place < count, entry(tab, WEIGHT, c, slots), 0.0)))
            terms = [
                child_pair(stage_ref, 2 * u, operator_of(tab, c, slots, modes), weight, right_ref, left_ref)
                for u, (c, weight) in enumerate(children)
            ]
            for (c, _), pair in zip(children, terms):
                add_pair(acc_ref, 2 * parent_of(tab, c, slots) * n, pair)

        for s in range(slots):
            part, at = part_of(sums, s)
            part[rows(at * n, n, 2)] = acc_ref[rows(2 * s * n, n, 2)]


def join_kernel(receiver, slots, modes, sum_parts, pick_parts, own_ref, right_ref, left_ref, *refs):
    out_ref, tab, sem_ref = refs[-3:]
    picks = refs[-3 - pick_parts : -3]
    sums = refs[-3 - pick_parts - sum_parts : -3 - pick_parts]
    frees = refs[: -3 - pick_parts - sum_parts]
    n = frees[0].shape[1]

    @pl.when(odd_depth() == receiver)
    def _():
        pull([narrow(own_ref)], tab, sem_ref)
        terms = []
        for s in range(slots if picks else 0):
            pick, at = part_of(picks, s)
            wa, wc = tab[0, WEIGHT_A, s], tab[0, WEIGHT_C, s]
            terms.append(parent_pair(pick, at, operator_of(tab, s, slots, modes), wa, wc, right_ref, left_ref))
        for s in range(slots):
            scale = tab[0, LIVE, s] * couple_step
            for i in range(2):
                here = rows((2 * s + i) * n, n)
                added = terms[s][i] if picks else 0.0
                if sums:
                    part, at = part_of(sums, s)
                    added = part[rows((at + i) * n, n)] + added
                out_ref[here] = frees[0][here] + scale * added
        if out_ref.shape[0] > 2 * slots * n:
            out_ref[pl.ds(2 * slots * n, ROWS)] = own_ref[...]

    if len(frees) > 1:

        @pl.when(odd_depth() != receiver)
        def _():
            out_ref[...] = frees[1][...]


def side_kernel(side, receiver, slots, group, modes, span, split, base_count, group_count, tab_count, right_ref, left_ref, *refs):
    stage_ref, tab, sem_ref = refs[-3:]
    start, step, count = span
    bases = refs[:base_count]
    groups = Layout(refs[base_count : base_count + group_count], slots, split)
    tab_refs = refs[base_count + group_count : base_count + group_count + tab_count]
    outs = refs[base_count + group_count + tab_count : -3]
    second = len(outs[-1].shape) == 2
    n = stage_ref.shape[1]
    size = 2 * slots * n
    gathered = Layout(tab_refs, slots, single(group)) if tab_count > 1 else None
    own_tables = [gathered.table(k) if gathered else tab_refs[0].at[k, pl.ds(0, ROWS), pl.ds(0, LANES)] for k in range(group)]
    out = Layout(outs, slots, joined(group)) if second else None

    @pl.when(odd_depth() == receiver)
    def _():
        below = [groups.table(k) for k in range(count)] if side == "children" else []
        pull(own_tables + below, tab, sem_ref)
        if second:
            for k in range(group):
                ref, base = out.base(k)
                per = (base_count - 1) // group
                for p in range(per):
                    piece = size // per
                    ref[pl.ds(base + p * piece, piece)] = (
                        bases[0][pl.ds(k * size + p * piece, piece)] + bases[1 + k * per + p][...]
                    )
                ref[pl.ds(base + size, ROWS)] = tab_refs[0][k]
        else:
            offset = 0
            if not bases:
                outs[0][...] = jnp.zeros_like(outs[0])
            for base in bases:
                outs[0][pl.ds(offset, base.shape[0])] = base[...]
                offset += base.shape[0]
            for k in range(group):
                if gathered:
                    gathered.copy_table(k, outs[1], k)
                else:
                    outs[1][k] = tab_refs[0][k]

        def add(index, pair):
            if not second:
                add_pair(outs[0], 2 * index * n, pair)
                return
            for ref, held in zip(outs, out.split):
                local = index - held[0] * slots
                at = lax.div(local, slots) * out.stride + lax.rem(local, slots) * (2 * n)

                @pl.when(jnp.logical_and(local >= 0, local < len(held) * slots))
                def _():
                    add_pair(ref, at, pair)

        @pl.loop(0, count)
        def _(k):
            at = k * slots
            targets, terms = [], []
            for s in range(slots):
                c = at + s
                groups.fetch(c if side == "children" else parent_of(tab, c, slots), stage_ref, 2 * s)
            for s in range(slots):
                c = at + s
                if side == "children":
                    b = c + group * slots
                    target = parent_of(tab, b, slots)
                    weight = entry(tab, WEIGHT, b, slots) * (entry(tab, LIVE, target, slots) * couple_step)
                    mode = entry(tab, MODE, b, slots).astype(jnp.int32) + (start + k * step) * modes
                    terms.append(child_pair(stage_ref, 2 * s, mode, weight, right_ref, left_ref))
                else:
                    target = c
                    scale = entry(tab, LIVE, c, slots) * couple_step
                    wa, wc = entry(tab, WEIGHT_A, c, slots) * scale, entry(tab, WEIGHT_C, c, slots) * scale
                    mode = operator_of(tab, c, slots, modes)
                    terms.append(parent_pair(stage_ref, 2 * s, mode, wa, wc, right_ref, left_ref))
                targets.append(target)
            for target, pair in zip(targets, terms):
                add(target, pair)


def call(kernel, out_shapes, limit, args, smem=0, us=1.0, scratch=()):
    specs = [pl.BlockSpec(memory_space=SMEM)] * smem
    specs += [pl.BlockSpec(memory_space=VMEM)] * (len(args) - smem)
    return pl.pallas_call(
        kernel,
        out_shape=out_shapes,
        in_specs=specs,
        out_specs=jax.tree.map(lambda _: pl.BlockSpec(memory_space=VMEM), out_shapes),
        scratch_shapes=scratch,
        compiler_params=pltpu.CompilerParams(vmem_limit_bytes=limit),
        cost_estimate=pl.CostEstimate(flops=int(us * 1.1e9), bytes_accessed=1 << 19, transcendentals=0),
    )(*args)


def turn_order(group):
    return sorted(range(1, group), key=lambda k: (bin(k).count("1"), -k))


def shards(sizes, blocks, live_slots, parent_index, bath_mode, hamiltonian, coupling, correlation, damping, link_weight):
    depths, group = sizes
    slots, _, n, _ = blocks.shape
    modes = coupling.shape[0]
    total = group * slots
    limit = 8 * total * 2 * n * n * 4
    order = turn_order(group)
    split_hop = 2 if slots % 2 == 0 else 1
    ranks = range(group)

    def place(d, m):
        return d * group + m

    def permute(value, pairs):
        return lax.ppermute(value, AXES, pairs)

    def gather(value, parity):
        held = {0: value}
        for k in order:
            step = k & -k
            pairs = [(place(d, m), place(d, m ^ step)) for d in range(parity, depths, 2) for m in ranks]
            held[k] = permute(held[k ^ step], pairs)
        return [held[k] for k in ranks]

    def shift(value, step, parity=None):
        pairs = [
            (place(d, m), place(d + step, m))
            for d in range(depths)
            for m in ranks
            if 0 <= d + step < depths and (parity is None or d % 2 == parity)
        ]
        return permute(value, pairs)

    def neighbour(value, parity):
        pairs = [(place(d, m), place(d, m ^ 1)) for d in range(parity, depths, 2) for m in ranks]
        return permute(value, pairs)

    def mats(count, tables=0):
        return jax.ShapeDtypeStruct((count * n + tables * ROWS, n), f32)

    def sds(*shape, dtype=f32):
        return jax.ShapeDtypeStruct(shape, dtype)

    plain = 2 * slots
    stage = VMEM((plain * n, n), f32)

    def tables(count):
        return [SMEM((count, ROWS, LANES), f32), pltpu.SemaphoreType.DMA((count,))]

    operator_shapes = (sds(group * modes, 3 * n, n, dtype=bf16), sds(group * modes, n, 3 * n, dtype=bf16))
    couplings = coupling.reshape(modes * n, n)
    squares = len(paired([None] * modes))

    packed, own_table = call(
        pack_kernel,
        (mats(plain + squares, 1), sds(ROWS, n)),
        PACK_LIMIT,
        (live_slots, parent_index, bath_mode, damping, link_weight, correlation, blocks.reshape(plain * n, n), couplings),
        smem=6,
    )
    first = gather(packed, 1)
    near_table = shift(own_table, -1)
    powers = call(
        powers_kernel, (sds(3 * n, ORDER * n, dtype=bf16), sds(n, 3 * ORDER * n, dtype=bf16)), limit, (hamiltonian,)
    )
    *operators_odd, raw = call(
        functools.partial(operators_kernel, slots, group, modes, None),
        (*operator_shapes, mats((group - 1) * squares, group - 1)),
        limit,
        (couplings, *first),
    )

    def free(states, parity, times, part=0, parts=1, prior=None):
        count = slots // parts
        return call(
            functools.partial(free_kernel, parity, times, slots, part * count),
            mats(2 * count * (1 if prior is None else part + 1)),
            limit,
            (states, *powers) if prior is None else (states, *powers, prior),
            us=4.5 * times / parts,
        )

    def free_parts(states, parity, times):
        return [free(states, parity, times, part, split_hop) for part in range(split_hop)]

    def free_chain(states, parity, times):
        done = None
        for part in range(split_hop):
            done = free(states, parity, times, part, split_hop, done)
        return done

    splits = {group: single(group), len(joined(group)): joined(group)}

    def pick(groups, sender, parts):
        return call(
            functools.partial(pick_kernel, sender, slots, splits[len(groups)], parts),
            [mats(plain // parts)] * parts,
            limit,
            (near_table, *groups),
            scratch=tables(1),
        )

    def send(groups, sender, parts, operators):
        outs = call(
            functools.partial(send_kernel, sender, slots, group, splits[len(groups)], modes, parts),
            [mats(plain // parts)] * parts + [sds(group, ROWS, n)],
            limit,
            (*operators, *groups),
            us=2,
            scratch=[stage, stage, SMEM((total,), jnp.int32), *tables(group)],
        )
        return outs[:parts], outs[-1]

    def join(frees, sums, picks, receiver, operators, noted=0):
        return call(
            functools.partial(join_kernel, receiver, slots, modes, len(sums), len(picks)),
            mats(plain, noted),
            limit,
            (own_table, *operators, *frees, *sums, *picks),
            scratch=tables(1),
        )

    def side(kind, bases, groups, tabs, receiver, operators, second=False, span=None):
        split = splits[len(groups)] if span is None else single(len(groups))
        span = (0, 1, group) if span is None else span
        return call(
            functools.partial(
                side_kernel, kind, receiver, slots, group, modes, span, split, len(bases), len(groups), len(tabs)
            ),
            [mats(plain * len(held), len(held)) for held in joined(group)]
            if second
            else [mats(2 * total), sds(group, ROWS, n)],
            limit,
            (*operators, *bases, *groups, *tabs),
            us=3,
            scratch=[stage, *tables(group + (span[2] if kind == "children" else 0))],
        )

    free_even = free(packed, 0, 1)
    free_odd = [part for k in ranks for part in free_parts(first[k], 1, 2)]
    picks = [shift(value, 1, 1) for value in pick(first, 1, split_hop)]
    sums, tabs_odd = send(first, 1, 1, operators_odd)
    sums = [shift(value, -1, 1) for value in sums]
    own_state = join([free_even], sums, picks, 0, operators_odd, 1)

    gathered = gather(own_state, 0)
    from_below = [shift(value, -1, 0) for value in gathered]
    from_above = [shift(value, 1, 0) for value in gathered]
    free_even = gather(free_chain(gathered[0], 0, 2), 0)
    evens, odds = (0, 2, group // 2), (1, 2, group // 2)
    states, _ = side("children", [], from_below[::2], [tabs_odd], 1, operators_odd, span=evens)
    states, _ = side("parents", [states], from_above, [tabs_odd], 1, operators_odd)
    far_bases = [states, *free_odd]
    states = side("children", far_bases, from_below[1::2], [tabs_odd], 1, operators_odd, second=True, span=odds)

    from_above = [shift(value, 1, 1) for value in states[:2]]
    from_above.append(neighbour(from_above[0], 0))
    from_below = [shift(value, -1, 1) for value in states]
    passed = shift(raw, -1, 1)
    operators_even = call(
        functools.partial(operators_kernel, slots, group, modes, 0), operator_shapes, limit, (couplings, passed)
    )
    last_odd = free(states[0], 1, 2)
    states, tabs_even = side("children", [], from_below, gathered, 0, operators_even)
    states = side("parents", [states, *free_even], from_above, [tabs_even], 0, operators_even, second=True)

    sums, _ = send(states, 0, split_hop, operators_even)
    sums = [shift(value, -1, 0) for value in sums]
    picks = [shift(value, 1, 0) for value in pick(states, 0, 1)]
    last_even = free(states[0], 0, 1)
    last_odd = join([last_odd], [], picks, 1, operators_odd)
    return join([last_odd, last_even], sums, [], 1, operators_odd).reshape(blocks.shape)


def solution(mesh):
    sizes = (mesh.shape["depth"], mesh.shape["mode"])

    def whole(*args):
        return shards(sizes, *args)

    return jax.shard_map(
        whole,
        mesh=mesh,
        in_specs=(
            P(("depth", "mode"), None, None, None),
            P(("depth", "mode")),
            P(("depth", "mode")),
            P(("depth", "mode")),
            P(),
            P("mode", None, None),
            P("mode", None),
            P(("depth", "mode")),
            P(("depth", "mode")),
        ),
        out_specs=P(("depth", "mode"), None, None, None),
        check_vma=False,
    )
```

```python
import functools
import math
import jax
import jax.numpy as jnp
from jax import lax
from jax.experimental import pallas as pl
from jax.experimental.pallas import tpu as pltpu
from jax.sharding import PartitionSpec as P

SUBSTEPS = 2
ORDER = 4
substep = 0.7
couple_step = 0.2

AXES = ("depth", "mode")
VMEM = pltpu.VMEM
SMEM = pltpu.SMEM
bf16 = jnp.bfloat16
f32 = jnp.float32

PARENT, MODE, LIVE, FACTOR, WEIGHT, WEIGHT_A, WEIGHT_C, DIAGONAL = range(8)
ROWS, LANES = 8, 128
PACK_LIMIT = 56 << 20


def split(value):
    high = value.astype(bf16)
    return high, (value - high.astype(f32)).astype(bf16)


def stack_rows(value):
    high, low = split(value)
    return jnp.concatenate([high, high, low], axis=0)


def stack_cols(value):
    high, low = split(value)
    return jnp.concatenate([high, low, high], axis=1)


def dot(first, second):
    return jnp.dot(first, second, preferred_element_type=f32)


def exact(first, second):
    return jnp.dot(first, second, preferred_element_type=f32, precision=lax.Precision.HIGHEST)


def odd_depth():
    return lax.rem(lax.axis_index("depth"), 2)


def rows(at, n, count=1):
    if not isinstance(at, int):
        at = pl.multiple_of(at, ROWS)
    return pl.ds(at, count * n)


def symmetric(value):
    return (value + value.T) * 0.5


def paired(operators):
    return [tuple(operators)] if len(operators) == 2 else operators


def pack_kernel(live_ref, parent_ref, mode_ref, damping_ref, weight_ref, corr_ref, blocks_ref, coupling_ref, out_ref, table_ref):
    slots, n = live_ref.shape[0], blocks_ref.shape[1]
    size = blocks_ref.shape[0]
    out_ref[pl.ds(0, size)] = blocks_ref[...]
    corner_row, corner_lane = (lax.broadcasted_iota(jnp.int32, (n, n), axis) for axis in range(2))
    operators = [symmetric(coupling_ref[pl.ds(i * n, n)]) for i in range(corr_ref.shape[0])]
    for i, value in enumerate(paired(operators)):
        if isinstance(value, tuple):
            value = jnp.where(corner_row <= corner_lane, *value)
        out_ref[pl.ds(size + ROWS + i * n, n)] = value
    row = lax.broadcasted_iota(jnp.int32, (ROWS, n), 0)
    lane = lax.broadcasted_iota(jnp.int32, (ROWS, n), 1)
    table = jnp.zeros((ROWS, n), f32)
    first_mode = lax.axis_index("mode") * corr_ref.shape[0]
    for s in range(slots):
        mode = mode_ref[s] - first_mode
        live = live_ref[s].astype(f32)
        weight = weight_ref[s]
        values = {
            PARENT: parent_ref[s].astype(f32),
            MODE: mode.astype(f32),
            LIVE: live,
            FACTOR: damping_ref[s] * (-SUBSTEPS * substep),
            WEIGHT: weight * live,
            WEIGHT_A: weight * corr_ref[mode, 0],
            WEIGHT_C: weight * corr_ref[mode, 1],
        }
        for at, value in values.items():
            table = jnp.where(jnp.logical_and(row == at, lane == s), value, table)
    for value in paired(operators):
        if isinstance(value, tuple):
            second = jnp.sum(jnp.where(corner_row == corner_lane, value[1], 0.0), axis=0, keepdims=True)
            table = jnp.where(row == DIAGONAL, second, table)
    live_row = table[LIVE : LIVE + 1]
    table = jnp.where(row == FACTOR, live_row * jnp.exp(table), table)
    table_ref[...] = table
    out_ref[pl.ds(size, ROWS)] = table


def powers_kernel(ham_ref, right_ref, left_ref):
    n = ham_ref.shape[0]
    ham = (ham_ref[...] + ham_ref[...].T) * 0.5
    power = ham
    for k in range(1, ORDER + 1):
        if k > 1:
            power = exact(power, ham)
        scaled = power * (substep**k / math.factorial(k))
        right_ref[:, (k - 1) * n : k * n] = stack_rows(scaled)
        left_ref[:, (k - 1) * 3 * n : k * 3 * n] = stack_cols(scaled)


def single(group):
    return [[k] for k in range(group)]


def joined(group):
    return [[0], list(range(2, group)), [1]]


class Layout:
    def __init__(self, refs, slots, split):
        self.refs, self.slots, self.split = refs, slots, split
        self.group = sum(len(held) for held in split)
        self.n = refs[0].shape[1]
        self.size = 2 * slots * self.n
        self.stride = self.size + ROWS

    def base(self, k):
        for ref, held in zip(self.refs, self.split):
            if k in held:
                return ref, held.index(k) * self.stride

    def table(self, k):
        ref, base = self.base(k)
        return ref.at[pl.ds(base + self.size, ROWS), pl.ds(0, LANES)]

    def copy_table(self, k, target_ref, at):
        ref, base = self.base(k)
        target_ref[at] = ref[pl.ds(base + self.size, ROWS)]

    def fetch(self, index, stage_ref, at):
        for k in range(self.group):
            ref, base = self.base(k)
            local = index - k * self.slots

            @pl.when(jnp.logical_and(local >= 0, local < self.slots))
            def _():
                stage_ref[rows(at * self.n, self.n, 2)] = ref[rows(base + 2 * local * self.n, self.n, 2)]


def pull(sources, smem_ref, sem_ref):
    copies = [pltpu.make_async_copy(ref, smem_ref.at[i], sem_ref.at[i]) for i, ref in enumerate(sources)]
    for copy in copies:
        copy.start()
    for copy in copies:
        copy.wait()


def narrow(ref):
    return ref.at[pl.ds(0, ROWS), pl.ds(0, LANES)]


def operators_kernel(slots, group, modes, parity, own_ref, *refs):
    outs = refs[-2 - (parity is None) :]
    sources = refs[: -len(outs)]
    right_ref, left_ref = outs[0], outs[1]
    n = own_ref.shape[1]
    size = 2 * slots * n
    squares = len(paired([None] * modes))
    block = ROWS + squares * n
    row, lane = (lax.broadcasted_iota(jnp.int32, (n, n), axis) for axis in range(2))

    def put(at, sym):
        right_ref[at] = stack_rows(sym)
        left_ref[at] = stack_cols(sym)

    def own():
        for i in range(modes):
            put(i, symmetric(own_ref[rows(i * n, n)]))

    def unpack(k, ref, base):
        if squares == modes:
            for i in range(modes):
                put(k * modes + i, ref[rows(base + ROWS + i * n, n)])
            return
        square = ref[rows(base + ROWS, n)]
        turned = square.T
        diagonal = ref[pl.ds(base, ROWS)][DIAGONAL : DIAGONAL + 1]
        put(k * modes, jnp.where(row <= lane, square, turned))
        put(k * modes + 1, jnp.where(row == lane, diagonal, jnp.where(row > lane, square, turned)))

    if parity is None:
        own()
        for k in range(1, group):
            unpack(k, sources[k], size)
            outs[2][pl.ds((k - 1) * block, block)] = sources[k][pl.ds(size, block)]
    else:

        @pl.when(odd_depth() == parity)
        def _():
            own()
            for k in range(1, group):
                unpack(k, sources[0], (k - 1) * block)


def taylor(real, imag, right, left):
    n = real.shape[0]
    out = dot(stack_cols(jnp.concatenate([real, imag], axis=0)), right)
    rp = [out[:n, k * n : (k + 1) * n] for k in range(ORDER)]
    ip = [out[n:, k * n : (k + 1) * n] for k in range(ORDER)]
    u_real, u_imag = real, imag
    stacked = [None] * ORDER
    for k in range(ORDER + 1):
        if k:
            turn = k % 4
            if turn == 1:
                u_real, u_imag = u_real - ip[k - 1], u_imag + rp[k - 1]
            elif turn == 2:
                u_real, u_imag = u_real - rp[k - 1], u_imag - ip[k - 1]
            elif turn == 3:
                u_real, u_imag = u_real + ip[k - 1], u_imag - rp[k - 1]
            else:
                u_real, u_imag = u_real + rp[k - 1], u_imag + ip[k - 1]
        j = ORDER - k
        if j:
            turn = j % 4
            if turn == 1:
                pair = (u_imag, -u_real)
            elif turn == 2:
                pair = (-u_real, -u_imag)
            elif turn == 3:
                pair = (-u_imag, u_real)
            else:
                pair = (u_real, u_imag)
            stacked[j - 1] = stack_rows(jnp.concatenate(pair, axis=1))
    done = dot(left, jnp.concatenate(stacked, axis=0))
    return u_real + done[:, :n], u_imag + done[:, n:]


def free_kernel(run_parity, times, slots, first, states_ref, right_ref, left_ref, *refs):
    out_ref = refs[-1]
    n = out_ref.shape[1]
    ahead = first if len(refs) > 1 else 0
    count = out_ref.shape[0] // (2 * n) - ahead
    pair = 2 if count % 2 == 0 else 1

    @pl.when(odd_depth() == run_parity)
    def _():
        right, left = right_ref[...], left_ref[...]
        if ahead:
            out_ref[pl.ds(0, 2 * ahead * n)] = refs[0][...]
        out_ref[pl.ds(2 * ahead * n, 2 * count * n)] = states_ref[pl.ds(2 * first * n, 2 * count * n)]

        @pl.loop(0, count // pair)
        def _(step):
            @pl.loop(0, times * SUBSTEPS)
            def _(turn):
                blocks = [ahead + step * pair + u for u in range(pair)]
                at = [(rows(2 * s * n, n), rows((2 * s + 1) * n, n)) for s in blocks]
                done = [taylor(out_ref[r], out_ref[i], right, left) for r, i in at]
                for (r, i), (real, imag) in zip(at, done):
                    out_ref[r] = real
                    out_ref[i] = imag

        factors = states_ref[pl.ds(2 * slots * n, ROWS)][FACTOR : FACTOR + 1]
        for s in range(count):
            scale = factors[:, first + s : first + s + 1] ** times
            at = rows(2 * (ahead + s) * n, n, 2)
            out_ref[at] = out_ref[at] * scale


def sided(real, imag, right, left):
    n = real.shape[0]
    after = dot(stack_cols(jnp.concatenate([real, imag], axis=0)), right)
    before = dot(left, stack_rows(jnp.concatenate([real, imag], axis=1)))
    return after[:n], after[n:], before[:, :n], before[:, n:]


def entry(tab, row, c, slots):
    if isinstance(c, int):
        return tab[c // slots, row, c % slots]
    return tab[lax.div(c, slots), row, lax.rem(c, slots)]


def operator_of(tab, c, slots, modes):
    back = c // slots if isinstance(c, int) else lax.div(c, slots)
    return back * modes + entry(tab, MODE, c, slots).astype(jnp.int32)


def parent_of(tab, c, slots):
    parent = entry(tab, PARENT, c, slots).astype(jnp.int32)
    back = lax.bitwise_xor(lax.axis_index("mode"), lax.div(parent, slots))
    return back * slots + lax.rem(parent, slots)


def child_pair(stage_ref, at, mode, weight, right_ref, left_ref):
    n = stage_ref.shape[1]
    ra, ia, rb, ib = sided(stage_ref[rows(at * n, n)], stage_ref[rows((at + 1) * n, n)], right_ref[mode], left_ref[mode])
    return weight * (ib - ia), weight * (ra - rb)


def parent_pair(stage_ref, at, mode, wa, wc, right_ref, left_ref):
    n = stage_ref.shape[1]
    ra, ia, rb, ib = sided(stage_ref[rows(at * n, n)], stage_ref[rows((at + 1) * n, n)], right_ref[mode], left_ref[mode])
    return wa * (ib - ia) + wc * (rb + ra), wa * (ra - rb) + wc * (ib + ia)


def add_pair(acc_ref, at, pair):
    n = acc_ref.shape[1]
    for i in range(2):
        where = rows(at + i * n, n)
        acc_ref[where] = acc_ref[where] + pair[i]


def part_of(parts, s):
    size = parts[0].shape[0] // (2 * parts[0].shape[1])
    return parts[s // size], 2 * (s % size)


def pick_kernel(sender, slots, split, parts, near_ref, *refs):
    tab, sem_ref = refs[-2:]
    picks = refs[-2 - parts : -2]
    groups = Layout(refs[: -2 - parts], slots, split)

    @pl.when(odd_depth() == sender)
    def _():
        pull([narrow(near_ref)], tab, sem_ref)
        for s in range(slots):
            pick, at = part_of(picks, s)
            groups.fetch(parent_of(tab, s, slots), pick, at)


def send_kernel(sender, slots, group, split, modes, parts, right_ref, left_ref, *refs):
    acc_ref, stage_ref, list_ref, tab, sem_ref = refs[-5:]
    tabs_ref = refs[-6]
    n = acc_ref.shape[1]
    sums = refs[-6 - parts : -6]
    groups = Layout(refs[: -6 - parts], slots, split)

    @pl.when(odd_depth() == sender)
    def _():
        pull([groups.table(k) for k in range(group)], tab, sem_ref)
        for k in range(group):
            groups.copy_table(k, tabs_ref, k)
        acc_ref[...] = jnp.zeros_like(acc_ref)

        def collect(c, count):
            mine = parent_of(tab, c, slots) < slots

            @pl.when(mine)
            def _():
                list_ref[count] = c

            return count + mine.astype(jnp.int32)

        count = lax.fori_loop(0, group * slots, collect, jnp.int32(0))

        @pl.loop(0, lax.div(count + slots - 1, slots))
        def _(batch):
            children = []
            for u in range(slots):
                place = batch * slots + u
                c = list_ref[jnp.minimum(place, count - 1)]
                groups.fetch(c, stage_ref, 2 * u)
                children.append((c, jnp.where(place < count, entry(tab, WEIGHT, c, slots), 0.0)))
            terms = [
                child_pair(stage_ref, 2 * u, operator_of(tab, c, slots, modes), weight, right_ref, left_ref)
                for u, (c, weight) in enumerate(children)
            ]
            for (c, _), pair in zip(children, terms):
                add_pair(acc_ref, 2 * parent_of(tab, c, slots) * n, pair)

        for s in range(slots):
            part, at = part_of(sums, s)
            part[rows(at * n, n, 2)] = acc_ref[rows(2 * s * n, n, 2)]


def join_kernel(receiver, slots, modes, sum_parts, pick_parts, own_ref, right_ref, left_ref, *refs):
    out_ref, tab, sem_ref = refs[-3:]
    picks = refs[-3 - pick_parts : -3]
    sums = refs[-3 - pick_parts - sum_parts : -3 - pick_parts]
    frees = refs[: -3 - pick_parts - sum_parts]
    n = frees[0].shape[1]

    @pl.when(odd_depth() == receiver)
    def _():
        pull([narrow(own_ref)], tab, sem_ref)
        terms = []
        for s in range(slots if picks else 0):
            pick, at = part_of(picks, s)
            wa, wc = tab[0, WEIGHT_A, s], tab[0, WEIGHT_C, s]
            terms.append(parent_pair(pick, at, operator_of(tab, s, slots, modes), wa, wc, right_ref, left_ref))
        for s in range(slots):
            scale = tab[0, LIVE, s] * couple_step
            for i in range(2):
                here = rows((2 * s + i) * n, n)
                added = terms[s][i] if picks else 0.0
                if sums:
                    part, at = part_of(sums, s)
                    added = part[rows((at + i) * n, n)] + added
                out_ref[here] = frees[0][here] + scale * added
        if out_ref.shape[0] > 2 * slots * n:
            out_ref[pl.ds(2 * slots * n, ROWS)] = own_ref[...]

    if len(frees) > 1:

        @pl.when(odd_depth() != receiver)
        def _():
            out_ref[...] = frees[1][...]


def side_kernel(side, receiver, slots, group, modes, span, split, base_count, group_count, tab_count, right_ref, left_ref, *refs):
    stage_ref, tab, sem_ref = refs[-3:]
    start, step, count = span
    bases = refs[:base_count]
    groups = Layout(refs[base_count : base_count + group_count], slots, split)
    tab_refs = refs[base_count + group_count : base_count + group_count + tab_count]
    outs = refs[base_count + group_count + tab_count : -3]
    second = len(outs[-1].shape) == 2
    n = stage_ref.shape[1]
    size = 2 * slots * n
    gathered = Layout(tab_refs, slots, single(group)) if tab_count > 1 else None
    own_tables = [gathered.table(k) if gathered else tab_refs[0].at[k, pl.ds(0, ROWS), pl.ds(0, LANES)] for k in range(group)]
    out = Layout(outs, slots, joined(group)) if second else None

    @pl.when(odd_depth() == receiver)
    def _():
        below = [groups.table(k) for k in range(count)] if side == "children" else []
        pull(own_tables + below, tab, sem_ref)
        if second:
            for k in range(group):
                ref, base = out.base(k)
                per = (base_count - 1) // group
                for p in range(per):
                    piece = size // per
                    ref[pl.ds(base + p * piece, piece)] = (
                        bases[0][pl.ds(k * size + p * piece, piece)] + bases[1 + k * per + p][...]
                    )
                ref[pl.ds(base + size, ROWS)] = tab_refs[0][k]
        else:
            offset = 0
            if not bases:
                outs[0][...] = jnp.zeros_like(outs[0])
            for base in bases:
                outs[0][pl.ds(offset, base.shape[0])] = base[...]
                offset += base.shape[0]
            for k in range(group):
                if gathered:
                    gathered.copy_table(k, outs[1], k)
                else:
                    outs[1][k] = tab_refs[0][k]

        def add(index, pair):
            if not second:
                add_pair(outs[0], 2 * index * n, pair)
                return
            for ref, held in zip(outs, out.split):
                local = index - held[0] * slots
                at = lax.div(local, slots) * out.stride + lax.rem(local, slots) * (2 * n)

                @pl.when(jnp.logical_and(local >= 0, local < len(held) * slots))
                def _():
                    add_pair(ref, at, pair)

        @pl.loop(0, count)
        def _(k):
            at = k * slots
            targets, terms = [], []
            for s in range(slots):
                c = at + s
                groups.fetch(c if side == "children" else parent_of(tab, c, slots), stage_ref, 2 * s)
            for s in range(slots):
                c = at + s
                if side == "children":
                    b = c + group * slots
                    target = parent_of(tab, b, slots)
                    weight = entry(tab, WEIGHT, b, slots) * (entry(tab, LIVE, target, slots) * couple_step)
                    mode = entry(tab, MODE, b, slots).astype(jnp.int32) + (start + k * step) * modes
                    terms.append(child_pair(stage_ref, 2 * s, mode, weight, right_ref, left_ref))
                else:
                    target = c
                    scale = entry(tab, LIVE, c, slots) * couple_step
                    wa, wc = entry(tab, WEIGHT_A, c, slots) * scale, entry(tab, WEIGHT_C, c, slots) * scale
                    mode = operator_of(tab, c, slots, modes)
                    terms.append(parent_pair(stage_ref, 2 * s, mode, wa, wc, right_ref, left_ref))
                targets.append(target)
            for target, pair in zip(targets, terms):
                add(target, pair)


def call(kernel, out_shapes, limit, args, smem=0, us=1.0, scratch=()):
    specs = [pl.BlockSpec(memory_space=SMEM)] * smem
    specs += [pl.BlockSpec(memory_space=VMEM)] * (len(args) - smem)
    return pl.pallas_call(
        kernel,
        out_shape=out_shapes,
        in_specs=specs,
        out_specs=jax.tree.map(lambda _: pl.BlockSpec(memory_space=VMEM), out_shapes),
        scratch_shapes=scratch,
        compiler_params=pltpu.CompilerParams(vmem_limit_bytes=limit),
        cost_estimate=pl.CostEstimate(flops=int(us * 1.1e9), bytes_accessed=1 << 19, transcendentals=0),
    )(*args)


def turn_order(group):
    return sorted(range(1, group), key=lambda k: (bin(k).count("1"), -k))


def shards(sizes, blocks, live_slots, parent_index, bath_mode, hamiltonian, coupling, correlation, damping, link_weight):
    depths, group = sizes
    slots, _, n, _ = blocks.shape
    modes = coupling.shape[0]
    total = group * slots
    limit = 8 * total * 2 * n * n * 4
    order = turn_order(group)
    split_hop = 2 if slots % 2 == 0 else 1
    ranks = range(group)

    def place(d, m):
        return d * group + m

    def permute(value, pairs):
        return lax.ppermute(value, AXES, pairs)

    def gather(value, parity, distances=None):
        held = {0: value}
        for k in distances or order:
            step = k & -k
            pairs = [(place(d, m), place(d, m ^ step)) for d in range(parity, depths, 2) for m in ranks]
            held[k] = permute(held[k ^ step], pairs)
        return held if distances else [held[k] for k in ranks]

    def shift(value, step, parity=None):
        pairs = [
            (place(d, m), place(d + step, m))
            for d in range(depths)
            for m in ranks
            if 0 <= d + step < depths and (parity is None or d % 2 == parity)
        ]
        return permute(value, pairs)

    def neighbour(value, parity):
        pairs = [(place(d, m), place(d, m ^ 1)) for d in range(parity, depths, 2) for m in ranks]
        return permute(value, pairs)

    def mats(count, tables=0):
        return jax.ShapeDtypeStruct((count * n + tables * ROWS, n), f32)

    def sds(*shape, dtype=f32):
        return jax.ShapeDtypeStruct(shape, dtype)

    plain = 2 * slots
    stage = VMEM((plain * n, n), f32)

    def tables(count):
        return [SMEM((count, ROWS, LANES), f32), pltpu.SemaphoreType.DMA((count,))]

    operator_shapes = (sds(group * modes, 3 * n, n, dtype=bf16), sds(group * modes, n, 3 * n, dtype=bf16))
    couplings = coupling.reshape(modes * n, n)
    squares = len(paired([None] * modes))

    packed, own_table = call(
        pack_kernel,
        (mats(plain + squares, 1), sds(ROWS, n)),
        PACK_LIMIT,
        (live_slots, parent_index, bath_mode, damping, link_weight, correlation, blocks.reshape(plain * n, n), couplings),
        smem=6,
    )
    first = gather(packed, 1)
    near_table = shift(own_table, -1)
    powers = call(
        powers_kernel, (sds(3 * n, ORDER * n, dtype=bf16), sds(n, 3 * ORDER * n, dtype=bf16)), limit, (hamiltonian,)
    )
    *operators_odd, raw = call(
        functools.partial(operators_kernel, slots, group, modes, None),
        (*operator_shapes, mats((group - 1) * squares, group - 1)),
        limit,
        (couplings, *first),
    )

    def free(states, parity, times, part=0, parts=1, prior=None):
        count = slots // parts
        return call(
            functools.partial(free_kernel, parity, times, slots, part * count),
            mats(2 * count * (1 if prior is None else part + 1)),
            limit,
            (states, *powers) if prior is None else (states, *powers, prior),
            us=4.5 * times / parts,
        )

    def free_parts(states, parity, times):
        return [free(states, parity, times, part, split_hop) for part in range(split_hop)]

    def free_chain(states, parity, times):
        done = None
        for part in range(split_hop):
            done = free(states, parity, times, part, split_hop, done)
        return done

    splits = {group: single(group), len(joined(group)): joined(group)}

    def pick(groups, sender, parts):
        return call(
            functools.partial(pick_kernel, sender, slots, splits[len(groups)], parts),
            [mats(plain // parts)] * parts,
            limit,
            (near_table, *groups),
            scratch=tables(1),
        )

    def send(groups, sender, parts, operators):
        outs = call(
            functools.partial(send_kernel, sender, slots, group, splits[len(groups)], modes, parts),
            [mats(plain // parts)] * parts + [sds(group, ROWS, n)],
            limit,
            (*operators, *groups),
            us=2,
            scratch=[stage, stage, SMEM((total,), jnp.int32), *tables(group)],
        )
        return outs[:parts], outs[-1]

    def join(frees, sums, picks, receiver, operators, noted=0):
        return call(
            functools.partial(join_kernel, receiver, slots, modes, len(sums), len(picks)),
            mats(plain, noted),
            limit,
            (own_table, *operators, *frees, *sums, *picks),
            scratch=tables(1),
        )

    def side(kind, bases, groups, tabs, receiver, operators, second=False, span=None):
        split = splits[len(groups)] if span is None else single(len(groups))
        span = (0, 1, group) if span is None else span
        return call(
            functools.partial(
                side_kernel, kind, receiver, slots, group, modes, span, split, len(bases), len(groups), len(tabs)
            ),
            [mats(plain * len(held), len(held)) for held in joined(group)]
            if second
            else [mats(2 * total), sds(group, ROWS, n)],
            limit,
            (*operators, *bases, *groups, *tabs),
            us=3,
            scratch=[stage, *tables(group + (span[2] if kind == "children" else 0))],
        )

    free_even = free(packed, 0, 1)
    free_odd = [part for k in ranks for part in free_parts(first[k], 1, 2)]
    picks = [shift(value, 1, 1) for value in pick(first, 1, split_hop)]
    sums, tabs_odd = send(first, 1, 1, operators_odd)
    sums = [shift(value, -1, 1) for value in sums]
    own_state = join([free_even], sums, picks, 0, operators_odd, 1)

    gathered = gather(own_state, 0)
    from_below = [shift(value, -1, 0) for value in gathered]
    from_above = [shift(value, 1, 0) for value in gathered]
    evolved = gather(free_chain(gathered[0], 0, 2), 0, [k for k in order if k & (k - 1) == 0])
    free_even = [evolved[k] if k in evolved else free_chain(gathered[k], 0, 2) for k in ranks]
    evens, odds = (0, 2, group // 2), (1, 2, group // 2)
    states, _ = side("children", [], from_below[::2], [tabs_odd], 1, operators_odd, span=evens)
    states, _ = side("parents", [states], from_above, [tabs_odd], 1, operators_odd)
    far_bases = [states, *free_odd]
    states = side("children", far_bases, from_below[1::2], [tabs_odd], 1, operators_odd, second=True, span=odds)

    from_above = [shift(value, 1, 1) for value in states[:2]]
    from_above.append(neighbour(from_above[0], 0))
    from_below = [shift(value, -1, 1) for value in states]
    passed = shift(raw, -1, 1)
    operators_even = call(
        functools.partial(operators_kernel, slots, group, modes, 0), operator_shapes, limit, (couplings, passed)
    )
    last_odd = free(states[0], 1, 2)
    states, tabs_even = side("children", [], from_below, gathered, 0, operators_even)
    states = side("parents", [states, *free_even], from_above, [tabs_even], 0, operators_even, second=True)

    sums, _ = send(states, 0, split_hop, operators_even)
    sums = [shift(value, -1, 0) for value in sums]
    picks = [shift(value, 1, 0) for value in pick(states, 0, 1)]
    last_even = free(states[0], 0, 1)
    last_odd = join([last_odd], [], picks, 1, operators_odd)
    return join([last_odd, last_even], sums, [], 1, operators_odd).reshape(blocks.shape)


def solution(mesh):
    sizes = (mesh.shape["depth"], mesh.shape["mode"])

    def whole(*args):
        return shards(sizes, *args)

    return jax.shard_map(
        whole,
        mesh=mesh,
        in_specs=(
            P(("depth", "mode"), None, None, None),
            P(("depth", "mode")),
            P(("depth", "mode")),
            P(("depth", "mode")),
            P(),
            P("mode", None, None),
            P("mode", None),
            P(("depth", "mode")),
            P(("depth", "mode")),
        ),
        out_specs=P(("depth", "mode"), None, None, None),
        check_vma=False,
    )
```
